256 devices in a mesh: sub: 64 (over z, y, x_hi), crow: 4 (over x_lo, core).
Axes of the slice: x: 4 (x_hi: 2, x_lo: 2; x = x_hi * 2 + x_lo), y: 4, z: 8, core: 2. Of those that a mesh axis runs over, the one named last changes fastest.
Arguments:
- test_vectors: float32 [64, 48, 3, 512], P('sub', None, None, 'crow'), may hold values from -6 to 6
- ell_values: float32 [64, 9, 27, 512], P('sub', None, None, 'crow'), may hold values from -0.6 to 0.6
- ell_cols: int32 [64, 27, 512], P('sub', None, 'crow'), may hold values from 0 to 511
- ell_count: int32 [64, 512], P('sub', 'crow'), may hold values from 1 to 27
- pivot: float32 [64, 3, 512], P('sub', None, 'crow'), may hold values from 2.5 to 4
- send_rows: int32 [64, 6, 128], P('sub', None, 'crow'), may hold values from 0 to 127
- recv_rows: int32 [64, 6, 128], P('sub', None, 'crow'), may hold values from 0 to 127
- ov_count: int32 [64, 6, 4], P('sub', None, 'crow'), may hold values from 1 to 32, 64 in all within a row
Outputs:
- basis: float32 [64, 48, 3, 512], P('sub', None, None, 'crow')
- coarse: float32 [64, 7, 48, 48], P('sub', None, 'crow')
The draws below stay inside these ranges and needn't reach their ends.
Inputs may be any that keep to these rules, and one draw needn't show every extreme that they name: `ov_count`: in each pair the live margin rows of the 4 blocks add up to 64; some block of some pair holds exactly 32.
All inputs are finite; a program needn't handle non-finite values.
Results may differ from the reference program's by a relative error of at most 0.0003.
Values sent between devices are 32-bit elements; how exact they have to be, the bound alone decides.
No kernel may reach another device: no remote copies, remote signals or barrier semaphores. Data moves between devices by JAX's collectives and lax.ppermute only.
A program may use at most 64 MiB of HBM per device.

```python
import math
import jax
import jax.numpy as jnp
import numpy as np
from jax import lax

ROWS_DEV = 128
VECS = 48
BLOCKS = 27
RADIUS = 3
OVD = 32
ITERS = 2
ROWS = 512
SUBS = 64
N_CROW = 4


def with_ends(entries, own_key, low, largest):
    extent = entries.shape
    place = [jax.random.randint(jax.random.fold_in(own_key, axis), (), 0, extent[axis]) for axis in range(len(extent))]
    entries = entries.at[tuple(place)].set(low)
    longest = extent.index(max(extent))
    place[longest] = (place[longest] + 1) % extent[longest]
    return entries.at[tuple(place)].set(largest)


def block_levels(stream_key, dims, pieces, least, largest):
    factor_of = 1.0
    for axis_at, blocks in pieces:
        heights = jax.random.uniform(jax.random.fold_in(jax.random.fold_in(stream_key, 6), axis_at), (blocks,), jnp.float32, least / len(pieces), largest / len(pieces))
        factor_of = factor_of * jnp.repeat(jnp.exp(heights), dims[axis_at] // blocks).reshape((-1,) + (1,) * (len(dims) - 1 - axis_at))
    return factor_of


def split_up(count, total, most, slope):
    weights = [(1 << 20) // math.isqrt(grade ** slope) + 1 for grade in range(2, count + 1)]
    rest, given = total - most - (count - 1), [1] * (count - 1)
    while rest > 0:
        free = [i for i in range(count - 1) if given[i] < most]
        whole, left = sum([weights[i] for i in free]), rest
        for i in free:
            addition = min(most - given[i], max(1, left * weights[i] // whole), rest)
            given[i] = given[i] + addition
            rest = rest - addition
    return np.array([most] + given)


def uneven_parts(key, count, total, reach, lean):
    if count == 2:
        one = jax.random.randint(key, (), max(1, total - reach), min(reach, total - 1) + 1)
        return jnp.stack([one, total - one])
    lengths = jnp.asarray(split_up(count, total, reach, lean), jnp.int32)
    twos = (count - 1) // 2
    donor, receiver = lengths[1:1 + 2 * twos:2], lengths[2:2 + 2 * twos:2]
    slack = jnp.minimum(donor - 1, reach - receiver)
    shifted = jax.random.randint(jax.random.fold_in(key, 1), (twos,), 0, 1 << 20) % (slack + 1)
    lengths = lengths.at[1:1 + 2 * twos:2].set(donor - shifted).at[2:2 + 2 * twos:2].set(receiver + shifted)
    return lengths[jax.random.permutation(jax.random.fold_in(key, 2), count)]


def scatter_about(stream_key, shape, scale, reach, split=(), kind=jnp.bfloat16):
    array = jax.random.normal(stream_key, shape, jnp.float32) * scale
    if len(split) > 0:
        array = block_levels(stream_key, shape, split, -0.22, 0.18) * array
    return jnp.clip(array, min=-reach, max=reach).astype(kind)


def setup_inputs(seed: int = 0) -> dict:
    splits = jax.random.split(jax.random.key(seed), 9)
    return {
        "test_vectors": scatter_about(splits[0], (SUBS, VECS, 3, ROWS), 1.0, 6.0, ((0, 64), (3, 4)), jnp.float32),
        "ell_values": scatter_about(splits[1], (SUBS, 9, BLOCKS, ROWS), 0.1, 0.6, ((0, 64), (3, 4)), jnp.float32),
        "ell_cols": with_ends(jax.random.randint(splits[2], (SUBS, BLOCKS, ROWS), 0, ROWS), jax.random.fold_in(splits[2], 1), 0, ROWS - 1).astype(jnp.int32),
        "ell_count": with_ends(jax.random.randint(splits[3], (SUBS, ROWS), 1, BLOCKS + 1), jax.random.fold_in(splits[3], 1), 1, BLOCKS).astype(jnp.int32),
        "pivot": jnp.clip(2.5 + 1.5 * jax.random.uniform(splits[4], (SUBS, 3, ROWS), jnp.float32) ** block_levels(splits[4], (SUBS, 3, ROWS), ((0, 64), (2, 4)), -0.2, 0.2), 2.5, 4.0),
        "send_rows": with_ends(jax.random.randint(splits[5], (SUBS, 2 * RADIUS, OVD * N_CROW), 0, ROWS_DEV), jax.random.fold_in(splits[5], 1), 0, ROWS_DEV - 1).astype(jnp.int32),
        "recv_rows": with_ends(jax.random.randint(splits[6], (SUBS, 2 * RADIUS, OVD * N_CROW), 0, ROWS_DEV), jax.random.fold_in(splits[6], 1), 0, ROWS_DEV - 1).astype(jnp.int32),
        "ov_count": jax.vmap(lambda own: uneven_parts(own, N_CROW, 2 * OVD, OVD, 2))(jax.random.split(splits[7], SUBS * (2 * RADIUS))).reshape((SUBS, 2 * RADIUS, N_CROW)).astype(jnp.int32),
    }


HIGH = lax.Precision.HIGHEST

def apply_op(whole, own, values, columns, counts, diagonal):
    total = diagonal[None, :, :] * own
    stored = columns.shape[0]
    for first in range(0, stored, 9):
        last = min(first + 9, stored)
        width = last - first
        picks = columns[first:last].astype(jnp.int32).reshape(-1)
        picked = jnp.take(whole, picks, axis=2).reshape(whole.shape[0], 3, width, -1)
        index_range = jnp.arange(first, last, dtype=jnp.int32)
        live = (index_range[:, None] < counts[None, :]).astype(own.dtype)
        factor = (values[:, first:last, :] * live[None, :, :]).reshape(3, 3, width, -1)
        total = total + jnp.einsum('abkr,vbkr->var', factor, picked, precision=HIGH)
    return total

def orthonormal(block):
    gram = jnp.einsum('var,war->vw', block, block, precision=HIGH)
    lower = jnp.linalg.cholesky(gram)
    flat = block.reshape(block.shape[0], -1)
    solved = jax.scipy.linalg.solve_triangular(lower, flat, lower=True)
    return solved.reshape(block.shape)

def reference(test_vectors, ell_values, ell_cols, ell_count, pivot, send_rows, recv_rows, ov_count):

    def local(items):
        start, values, columns, counts, diagonal = items
        current = start
        for step in range(ITERS):
            current = orthonormal(apply_op(current, current, values, columns, counts, diagonal))
        return (current, apply_op(current, current, values, columns, counts, diagonal))
    basis, image = lax.map(local, (test_vectors, ell_values, ell_cols, ell_count, pivot))
    span = OVD * N_CROW
    block_of = (jnp.arange(span) // OVD).astype(jnp.int32)
    within = (jnp.arange(span) % OVD).astype(jnp.int32)
    lifted = (block_of * ROWS_DEV).astype(jnp.int32)
    scale = ROWS_DEV * N_CROW / OVD
    picker = jax.vmap(lambda field, rows: jnp.take(field, rows, axis=2))
    center = jnp.einsum('nvar,nwar->nvw', basis, image, precision=HIGH)
    blocks = []
    for slot in range(2 * RADIUS):
        offset = slot - RADIUS if slot < RADIUS else slot - RADIUS + 1
        source = (send_rows[:, slot, :] + lifted[None, :]).astype(jnp.int32)
        arrived = picker(jnp.roll(image, -offset, 0), jnp.roll(source, -offset, 0))
        target = (recv_rows[:, slot, :] + lifted[None, :]).astype(jnp.int32)
        limit = jnp.take(ov_count[:, slot, :], block_of, axis=1)
        live = (within[None, :] < limit).astype(basis.dtype)
        mine = picker(basis, target) * live[:, None, None, :]
        blocks.append(jnp.einsum('nvat,nwat->nvw', mine, arrived, precision=HIGH) * scale)
        if slot == RADIUS - 1:
            blocks.append(center)
    return (basis, jnp.stack(blocks, axis=1))
```

```python
import jax
import jax.numpy as jnp
from jax import lax
from jax.experimental import pallas as pl
from jax.experimental.pallas import tpu as pltpu
from jax.sharding import PartitionSpec as P

RADIUS = 3
SLOTS = 2 * RADIUS
V = 48
LANES = 128
NB = 27
NC = 4
OVD = 32
SCALE = float(LANES * NC // OVD)
TILES = V // 8

X0 = 0
VAL0 = 3 * V
COL0 = VAL0 + 9 * NB
PIV0 = COL0 + NB
SEND0 = PIV0 + 3
RECV0 = SEND0 + SLOTS
LIVE0 = RECV0 + SLOTS
PACKED = LIVE0 + SLOTS

OFFSETS = [o - RADIUS if o < RADIUS else o - RADIUS + 1 for o in range(SLOTS)]
HIGH = lax.Precision.HIGHEST
F32 = jnp.float32


def vmem():
    return pl.BlockSpec(memory_space=pltpu.VMEM)


def smem():
    return pl.BlockSpec(memory_space=pltpu.SMEM)


def pack_kernel(c_ref, ov_ref, x_ref, val_ref, col_ref, cnt_ref, piv_ref, send_ref, recv_ref, out_ref):
    out_ref[X0 : X0 + 3 * V, :] = x_ref[...]
    count = cnt_ref[...]
    for k in range(NB):
        live = k < count
        for ab in range(9):
            out_ref[VAL0 + ab * NB + k : VAL0 + ab * NB + k + 1, :] = jnp.where(live, val_ref[ab * NB + k], 0.0)
        out_ref[COL0 + k : COL0 + k + 1, :] = col_ref[k].astype(F32)
    for a in range(3):
        out_ref[PIV0 + a : PIV0 + a + 1, :] = piv_ref[a]
    lane = lax.broadcasted_iota(jnp.int32, (1, LANES), 1)
    c = c_ref[0]
    here = (lane // OVD) == c
    for o in range(SLOTS):
        for ref, base in ((send_ref, SEND0), (recv_ref, RECV0)):
            piece = ref[o].astype(F32)
            row = jnp.concatenate([piece] * NC, axis=1)
            out_ref[base + o : base + o + 1, :] = jnp.where(here, row, 0.0)
        alive = here & ((lane % OVD) < ov_ref[o])
        out_ref[LIVE0 + o : LIVE0 + o + 1, :] = jnp.where(alive, 1.0, 0.0).astype(F32)


def wide(row):
    return jnp.broadcast_to(row, (8, LANES))


def lanes_of(block, index):
    return jnp.take_along_axis(block, index, axis=1)


def start_op(pay_ref, src_ref, dst_ref):
    for q in range(NC):
        for a in range(3):
            piv = wide(pay_ref[q, PIV0 + a : PIV0 + a + 1, :])
            for t in range(TILES):
                rows = slice(a * V + 8 * t, a * V + 8 * t + 8)
                dst_ref[q, rows, :] = piv * src_ref[q, rows, :]


def op_piece(pay_ref, src_ref, dst_ref, rc, first, width):
    total = [[dst_ref[rc, a * V + 8 * t : a * V + 8 * t + 8, :] for t in range(TILES)] for a in range(3)]
    for u in range(width):
        k = first + u
        col = wide(pay_ref[rc, pl.ds(COL0 + k, 1), :]).astype(jnp.int32)
        index = col & (LANES - 1)
        which = col >> 7
        is_q = [which == q for q in range(NC - 1)]
        val = [[wide(pay_ref[rc, pl.ds(VAL0 + (3 * a + b) * NB + k, 1), :]) for b in range(3)] for a in range(3)]
        for b in range(3):
            for t in range(TILES):
                got = [lanes_of(src_ref[q, b * V + 8 * t : b * V + 8 * t + 8, :], index) for q in range(NC)]
                pick = got[NC - 1]
                for q in range(NC - 1):
                    pick = jnp.where(is_q[q], got[q], pick)
                for a in range(3):
                    total[a][t] = total[a][t] + val[a][b] * pick
    for a in range(3):
        for t in range(TILES):
            dst_ref[rc, a * V + 8 * t : a * V + 8 * t + 8, :] = total[a][t]


def flat(ref):
    return jnp.concatenate([ref[q, a * V : a * V + V, :] for a in range(3) for q in range(NC)], axis=1)


def gram_to(m_ref, block):
    gram = lax.dot_general(block, block, (((1,), (1,)), ((), ())), precision=HIGH, preferred_element_type=F32)
    row = lax.broadcasted_iota(jnp.int32, (V, 64), 0)
    lane = lax.broadcasted_iota(jnp.int32, (V, 64), 1)
    eye = jnp.where(row == lane, 1.0, 0.0).astype(F32)
    m_ref[...] = jnp.concatenate([eye, gram, jnp.zeros((V, LANES - 64 - V), F32)], axis=1)


CHOL = 4


def factor_piece(m_ref, col_ref, j):
    sub = lax.broadcasted_iota(jnp.int32, (8, LANES), 0)
    m = [m_ref[8 * t : 8 * t + 8, :] for t in range(TILES)]
    cols = []
    for s in range(CHOL):
        index = jnp.full((8, LANES), 64 + s, jnp.int32) + j
        cols.append([lanes_of(m[t], index) for t in range(TILES)])
        for t in range(TILES):
            col_ref[s, 8 * t : 8 * t + 8, :] = cols[s][t]
    for s in range(CHOL):
        row = wide(m_ref[pl.ds(j + s, 1), :])
        head = {n: wide(col_ref[n, pl.ds(j + s, 1), :]) for n in range(s, CHOL)}
        inverse = 1.0 / head[s]
        for t in range(TILES):
            factor = jnp.where(sub + 8 * t > j + s, cols[s][t] * inverse, 0.0)
            m[t] = m[t] - factor * row
            m_ref[8 * t : 8 * t + 8, :] = m[t]
            for n in range(s + 1, CHOL):
                cols[n][t] = cols[n][t] - factor * head[n]
                col_ref[n, 8 * t : 8 * t + 8, :] = cols[n][t]


def inverse_of(m_ref):
    m = m_ref[...]
    row = lax.broadcasted_iota(jnp.int32, (V, LANES), 0)
    lane = lax.broadcasted_iota(jnp.int32, (V, LANES), 1)
    diag = jnp.sum(jnp.where(lane == row + 64, m, 0.0), axis=1, keepdims=True)
    return m[:, :V] / jnp.sqrt(diag)


def solve_to(dst_ref, linv, src_ref):
    out = jnp.dot(linv, flat(src_ref), precision=HIGH, preferred_element_type=F32)
    for a in range(3):
        for q in range(NC):
            at = (a * NC + q) * LANES
            dst_ref[q, a * V : a * V + V, :] = out[:, at : at + LANES]


def rows_of(src_ref, index, tiles):
    lane = lax.broadcasted_iota(jnp.int32, (8, LANES), 1) // OVD
    out = []
    for at in tiles:
        pick = lanes_of(src_ref[NC - 1, at, :], index)
        for q in range(NC - 1):
            pick = jnp.where(lane == q, lanes_of(src_ref[q, at, :], index), pick)
        out.append(pick)
    return out


def index_row(pay_ref, row):
    total = pay_ref[0, pl.ds(row, 1), :]
    for q in range(1, NC):
        total = total + pay_ref[q, pl.ds(row, 1), :]
    return wide(total)


PARTS = 12
WIDTH = NC * NB // PARTS


def main_kernel(c_ref, pay_ref, y2_ref, w_ref, linv_ref, s1_ref, s2_ref, y_ref, z_ref, m_ref, col_ref, g_ref):
    c = c_ref[0]

    def loop(src_ref, dst_ref, chol):
        start_op(pay_ref, src_ref, dst_ref)

        def step(it, carry):
            op_piece(pay_ref, src_ref, dst_ref, it // 3, (it % 3) * WIDTH, WIDTH)
            if chol:
                factor_piece(m_ref, col_ref, it * CHOL)
            return carry

        lax.fori_loop(0, PARTS, step, 0)

    loop(pay_ref, y_ref, False)
    gram_to(m_ref, flat(y_ref))
    loop(y_ref, z_ref, True)
    solve_to(y2_ref, inverse_of(m_ref), z_ref)
    gram_to(m_ref, flat(y2_ref))
    loop(y2_ref, w_ref, True)
    linv = inverse_of(m_ref)
    linv_ref[...] = linv
    first = index_row(pay_ref, SEND0 + c).astype(jnp.int32)
    second = index_row(pay_ref, SEND0 + NC + c // 2).astype(jnp.int32)
    half = (c % 2) * (V // 2)
    tiles = [slice(8 * t, 8 * t + 8) for t in range(3 * TILES)]
    for n, index in enumerate((first, second)):
        for at, piece in zip(tiles, rows_of(w_ref, index, tiles)):
            g_ref[n, at, :] = piece
    both = jnp.concatenate([g_ref[n, a * V : a * V + V, :] for n in range(2) for a in range(3)], axis=1)
    image = jnp.dot(linv, both, precision=HIGH, preferred_element_type=F32)
    for a in range(3):
        s1_ref[a * V : a * V + V, :] = image[:, a * LANES : a * LANES + LANES]
        g_ref[1, a * V : a * V + V, :] = image[:, (3 + a) * LANES : (4 + a) * LANES]
        s2_ref[a * (V // 2) : (a + 1) * (V // 2), :] = g_ref[1, pl.ds(pl.multiple_of(a * V + half, 8), V // 2), :]


def middle_kernel(c_ref, pay_ref, y2_ref, w_ref, linv_ref, basis_ref, mine1_ref, mine2_ref, center_ref, q_ref):
    c = c_ref[0]
    linv = linv_ref[...]
    solve_to(q_ref, linv, y2_ref)
    basis_ref[...] = q_ref[c]
    tiles = [slice(8 * t, 8 * t + 8) for t in range(3 * TILES)]
    for out_ref, slot in ((mine1_ref, c), (mine2_ref, NC + c // 2)):
        index = index_row(pay_ref, RECV0 + slot).astype(jnp.int32)
        live = index_row(pay_ref, LIVE0 + slot)
        for at, piece in zip(tiles, rows_of(q_ref, index, tiles)):
            out_ref[at, :] = piece * live
    image = jnp.dot(linv, flat(w_ref), precision=HIGH, preferred_element_type=F32)
    center_ref[...] = lax.dot_general(
        flat(q_ref), image, (((1,), (1,)), ((), ())), precision=HIGH, preferred_element_type=F32
    )


def coarse_kernel(c_ref, mine1_ref, mine2_ref, got1_ref, got2_ref, own_ref, a_ref, b_ref, d_ref, r_ref):
    c = c_ref[0]

    def side(ref, count):
        return jnp.concatenate([ref[a * count : a * count + count, :] for a in range(3)], axis=1)

    nt = (((1,), (1,)), ((), ()))
    one = lax.dot_general(side(mine1_ref, V), side(got1_ref, V), nt, precision=HIGH, preferred_element_type=F32) * SCALE
    two = lax.dot_general(side(mine2_ref, V), side(got2_ref, V // 2), nt, precision=HIGH, preferred_element_type=F32) * SCALE
    part = V // NC
    for d in range(NC):
        r_ref[d, 0:part, 0:V] = one[d * part : d * part + part, :]
        r_ref[d, 16 : 16 + part, 0 : V // 2] = two[d * part : d * part + part, :]
    own_ref[...] = r_ref[c]
    a_ref[...] = r_ref[c ^ 1]
    b_ref[...] = r_ref[c ^ 2]
    d_ref[...] = r_ref[c ^ 3]


def join_kernel(c_ref, center_ref, own_ref, a_ref, b_ref, d_ref, out_ref, r_ref):
    c = c_ref[0]
    part = V // NC
    for m, ref in enumerate((own_ref, a_ref, b_ref, d_ref)):
        r_ref[m] = ref[...]
    for slot in range(NC):
        out_ref[slot if slot < RADIUS else slot + 1] = r_ref[c ^ slot, 0:part, 0:V]
    for slot in range(NC, SLOTS):
        even = 2 * (slot - NC)
        low = r_ref[c ^ even, 16 : 16 + part, 0 : V // 2]
        high = r_ref[c ^ (even + 1), 16 : 16 + part, 0 : V // 2]
        out_ref[slot + 1] = jnp.concatenate([low, high], axis=1)
    for d in range(NC):
        @pl.when(c == d)
        def _():
            out_ref[RADIUS] = center_ref[d * part : d * part + part, :]


def shards(test_vectors, ell_values, ell_cols, ell_count, pivot, send_rows, recv_rows, ov_count):
    shape = jax.ShapeDtypeStruct
    c = lax.axis_index("crow").astype(jnp.int32).reshape(1)
    x = jnp.transpose(test_vectors[0], (1, 0, 2)).reshape(3 * V, LANES)
    packed = pl.pallas_call(
        pack_kernel,
        out_shape=shape((PACKED, LANES), F32),
        in_specs=[smem(), smem()] + [vmem()] * 7,
        out_specs=vmem(),
    )(
        c,
        ov_count.reshape(SLOTS),
        x,
        ell_values.reshape(9 * NB, 1, LANES),
        ell_cols.reshape(NB, 1, LANES),
        ell_count.reshape(1, LANES),
        pivot.reshape(3, 1, LANES),
        send_rows.reshape(SLOTS, 1, OVD),
        recv_rows.reshape(SLOTS, 1, OVD),
    )
    pay = lax.all_gather(packed, "crow", axis=0)
    block = (NC, 3 * V, LANES)
    y2, w, linv, s1, s2 = pl.pallas_call(
        main_kernel,
        out_shape=(
            shape(block, F32),
            shape(block, F32),
            shape((V, V), F32),
            shape((3 * V, LANES), F32),
            shape((3 * V // 2, LANES), F32),
        ),
        in_specs=[smem(), vmem()],
        out_specs=(vmem(),) * 5,
        scratch_shapes=[
            pltpu.VMEM(block, F32),
            pltpu.VMEM(block, F32),
            pltpu.VMEM((V, LANES), F32),
            pltpu.VMEM((CHOL, V, LANES), F32),
            pltpu.VMEM((2, 3 * V, LANES), F32),
        ],
    )(c, pay)

    size = lax.axis_size("sub")

    def across(piece, slot_of):
        pairs = []
        for j in range(size):
            for n in range(NC):
                i = (j - OFFSETS[slot_of(n)]) % size
                pairs.append((j * NC + n, i * NC + n))
        return lax.ppermute(piece, ("sub", "crow"), pairs)

    got1 = across(s1, lambda n: n)
    got2 = across(s2, lambda n: NC + n // 2)
    basis, mine1, mine2, center = pl.pallas_call(
        middle_kernel,
        out_shape=(
            shape((3 * V, LANES), F32),
            shape((3 * V, LANES), F32),
            shape((3 * V, LANES), F32),
            shape((V, V), F32),
        ),
        in_specs=[smem()] + [vmem()] * 4,
        out_specs=(vmem(),) * 4,
        scratch_shapes=[pltpu.VMEM(block, F32)],
    )(c, pay, y2, w, linv)
    slab = shape((32, LANES), F32)
    own, to1, to2, to3 = pl.pallas_call(
        coarse_kernel,
        out_shape=(slab,) * 4,
        in_specs=[smem()] + [vmem()] * 4,
        out_specs=(vmem(),) * 4,
        scratch_shapes=[pltpu.VMEM((NC, 32, LANES), F32)],
    )(c, mine1, mine2, got1, got2)
    got = [lax.ppermute(t, "crow", [(n, n ^ m) for n in range(NC)]) for m, t in ((1, to1), (2, to2), (3, to3))]
    coarse = pl.pallas_call(
        join_kernel,
        out_shape=shape((2 * RADIUS + 1, V // NC, V), F32),
        in_specs=[smem()] + [vmem()] * 5,
        out_specs=vmem(),
        scratch_shapes=[pltpu.VMEM((NC, 32, LANES), F32)],
    )(c, center, own, *got)
    basis = jnp.transpose(basis.reshape(3, V, LANES), (1, 0, 2))
    return basis[None], coarse[None]


def solution(mesh):
    placed = (
        P("sub", None, None, "crow"),
        P("sub", None, None, "crow"),
        P("sub", None, "crow"),
        P("sub", "crow"),
        P("sub", None, "crow"),
        P("sub", None, "crow"),
        P("sub", None, "crow"),
        P("sub", None, "crow"),
    )
    return jax.shard_map(
        shards,
        mesh=mesh,
        in_specs=placed,
        out_specs=(P("sub", None, None, "crow"), P("sub", None, "crow", None)),
        check_vma=False,
    )
```

```python
import jax
import jax.numpy as jnp
from jax import lax
from jax.experimental import pallas as pl
from jax.experimental.pallas import tpu as pltpu
from jax.sharding import PartitionSpec as P

RADIUS = 3
SLOTS = 2 * RADIUS
V = 48
LANES = 128
NB = 27
NC = 4
OVD = 32
SCALE = float(LANES * NC // OVD)
TILES = V // 8

X0 = 0
VAL0 = 3 * V
COL0 = VAL0 + 9 * NB
PIV0 = COL0 + NB
SEND0 = PIV0 + 3
RECV0 = SEND0 + SLOTS
LIVE0 = RECV0 + SLOTS
PACKED = LIVE0 + SLOTS

OFFSETS = [o - RADIUS if o < RADIUS else o - RADIUS + 1 for o in range(SLOTS)]
HIGH = lax.Precision.HIGHEST
F32 = jnp.float32


def vmem():
    return pl.BlockSpec(memory_space=pltpu.VMEM)


def smem():
    return pl.BlockSpec(memory_space=pltpu.SMEM)


def pack_kernel(c_ref, ov_ref, x_ref, val_ref, col_ref, cnt_ref, piv_ref, send_ref, recv_ref, out_ref):
    out_ref[X0 : X0 + 3 * V, :] = x_ref[...]
    count = cnt_ref[...]
    for k in range(NB):
        live = k < count
        for ab in range(9):
            out_ref[VAL0 + ab * NB + k : VAL0 + ab * NB + k + 1, :] = jnp.where(live, val_ref[ab * NB + k], 0.0)
        out_ref[COL0 + k : COL0 + k + 1, :] = col_ref[k].astype(F32)
    for a in range(3):
        out_ref[PIV0 + a : PIV0 + a + 1, :] = piv_ref[a]
    lane = lax.broadcasted_iota(jnp.int32, (1, LANES), 1)
    c = c_ref[0]
    here = (lane // OVD) == c
    for o in range(SLOTS):
        for ref, base in ((send_ref, SEND0), (recv_ref, RECV0)):
            piece = ref[o].astype(F32)
            row = jnp.concatenate([piece] * NC, axis=1)
            out_ref[base + o : base + o + 1, :] = jnp.where(here, row, 0.0)
        alive = here & ((lane % OVD) < ov_ref[o])
        out_ref[LIVE0 + o : LIVE0 + o + 1, :] = jnp.where(alive, 1.0, 0.0).astype(F32)


def wide(row):
    return jnp.broadcast_to(row, (8, LANES))


def lanes_of(block, index):
    return jnp.take_along_axis(block, index, axis=1)


def start_op(pay_ref, src_ref, dst_ref):
    for q in range(NC):
        for a in range(3):
            piv = wide(pay_ref[q, PIV0 + a : PIV0 + a + 1, :])
            for t in range(TILES):
                rows = slice(a * V + 8 * t, a * V + 8 * t + 8)
                dst_ref[q, rows, :] = piv * src_ref[q, rows, :]


ONE = 18
BF16 = jnp.bfloat16


def value_row(pay_ref, rc, ab, k):
    return wide(pay_ref[rc, pl.ds(VAL0 + ab * NB + k, 1), :])


def add_block(pay_ref, dst_ref, rc, k, pick_of):
    val = [[value_row(pay_ref, rc, 3 * a + b, k) for b in range(3)] for a in range(3)]
    for t in range(TILES):
        pick = [pick_of(b, t) for b in range(3)]
        for a in range(3):
            at = slice(a * V + 8 * t, a * V + 8 * t + 8)
            dst_ref[rc, at, :] = dst_ref[rc, at, :] + (
                val[a][0] * pick[0] + val[a][1] * pick[1] + val[a][2] * pick[2]
            )


def lane_block(pay_ref, src_ref, dst_ref, rc, k):
    col = wide(pay_ref[rc, pl.ds(COL0 + k, 1), :]).astype(jnp.int32)
    index = col & (LANES - 1)
    odd = (col & LANES) != 0
    top = col >= 2 * LANES

    def pick_of(b, t):
        got = [lanes_of(src_ref[q, b * V + 8 * t : b * V + 8 * t + 8, :], index) for q in range(NC)]
        return jnp.where(top, jnp.where(odd, got[3], got[2]), jnp.where(odd, got[1], got[0]))

    add_block(pay_ref, dst_ref, rc, k, pick_of)


def one_hot(pay_ref, oh_ref, k):
    half = 2 * LANES
    place = lax.broadcasted_iota(jnp.int32, (half, half), 0).astype(F32).astype(BF16)
    for m in range(2):
        col = jnp.concatenate([pay_ref[2 * m + n, pl.ds(COL0 + k, 1), :] for n in range(2)], axis=1)
        for h in range(2):
            local = col - float(h * half)
            local = jnp.where((local >= 0.0) & (local < float(half)), local, -1.0)
            target = jnp.concatenate([jnp.broadcast_to(local, (16, half)).astype(BF16)] * (half // 16), axis=0)
            oh_ref[m, k, h * half : h * half + half, :] = jnp.where(
                place == target, jnp.ones((), BF16), jnp.zeros((), BF16)
            )


def split_to(x_ref, src_ref):
    for q in range(NC):
        at = slice(q * LANES, q * LANES + LANES)
        value = src_ref[q, 0 : 3 * V, :]
        high = value.astype(BF16)
        x_ref[0 : 3 * V, at] = high
        x_ref[3 * V :, at] = (value - high.astype(F32)).astype(BF16)


def issue(x_ref, oh_ref, t_ref, k, parity):
    for m in range(2):
        got = jnp.dot(x_ref[...], oh_ref[m, k], preferred_element_type=F32)
        t_ref[parity, m] = got[: 3 * V, :] + got[3 * V :, :]


def take(pay_ref, dst_ref, t_ref, k, parity):
    for m in range(2):
        for n in range(2):
            at = slice(n * LANES, n * LANES + LANES)
            add_block(
                pay_ref, dst_ref, 2 * m + n, k, lambda b, t: t_ref[parity, m, b * V + 8 * t : b * V + 8 * t + 8, at]
            )


def flat(ref):
    return jnp.concatenate([ref[q, a * V : a * V + V, :] for a in range(3) for q in range(NC)], axis=1)


def gram_to(m_ref, block):
    gram = lax.dot_general(block, block, (((1,), (1,)), ((), ())), precision=HIGH, preferred_element_type=F32)
    row = lax.broadcasted_iota(jnp.int32, (V, 64), 0)
    lane = lax.broadcasted_iota(jnp.int32, (V, 64), 1)
    eye = jnp.where(row == lane, 1.0, 0.0).astype(F32)
    m_ref[:V, :] = jnp.concatenate([eye, gram, jnp.zeros((V, LANES - 64 - V), F32)], axis=1)


CHOL = 3
UN = 6


def factor_piece(m_ref, col_ref, j):
    sub = lax.broadcasted_iota(jnp.int32, (8, LANES), 0)
    m = [m_ref[8 * t : 8 * t + 8, :] for t in range(TILES)]
    cols = []
    for s in range(CHOL):
        index = jnp.full((8, LANES), 64 + s, jnp.int32) + j
        cols.append([lanes_of(m[t], index) for t in range(TILES)])
        for t in range(TILES):
            col_ref[s, 8 * t : 8 * t + 8, :] = cols[s][t]
    for s in range(CHOL):
        row = wide(m_ref[pl.ds(j + s, 1), :])
        head = {n: wide(col_ref[n, pl.ds(j + s, 1), :]) for n in range(s, CHOL)}
        inverse = 1.0 / head[s]
        for t in range(TILES):
            factor = jnp.where(sub + 8 * t > j + s, cols[s][t] * inverse, 0.0)
            m[t] = m[t] - factor * row
            m_ref[8 * t : 8 * t + 8, :] = m[t]
            for n in range(s + 1, CHOL):
                cols[n][t] = cols[n][t] - factor * head[n]
                col_ref[n, 8 * t : 8 * t + 8, :] = cols[n][t]


def inverse_of(m_ref):
    m = m_ref[:V, :]
    row = lax.broadcasted_iota(jnp.int32, (V, LANES), 0)
    lane = lax.broadcasted_iota(jnp.int32, (V, LANES), 1)
    diag = jnp.sum(jnp.where(lane == row + 64, m, 0.0), axis=1, keepdims=True)
    return m[:, :V] / jnp.sqrt(diag)


def solve_to(dst_ref, linv, src_ref):
    out = jnp.dot(linv, flat(src_ref), precision=HIGH, preferred_element_type=F32)
    for a in range(3):
        for q in range(NC):
            at = (a * NC + q) * LANES
            dst_ref[q, a * V : a * V + V, :] = out[:, at : at + LANES]


def rows_of(src_ref, index, tiles):
    lane = lax.broadcasted_iota(jnp.int32, (8, LANES), 1) // OVD
    out = []
    for at in tiles:
        pick = lanes_of(src_ref[NC - 1, at, :], index)
        for q in range(NC - 1):
            pick = jnp.where(lane == q, lanes_of(src_ref[q, at, :], index), pick)
        out.append(pick)
    return out


def index_row(pay_ref, row):
    total = pay_ref[0, pl.ds(row, 1), :]
    for q in range(1, NC):
        total = total + pay_ref[q, pl.ds(row, 1), :]
    return wide(total)


def main_kernel(
    c_ref, pay_ref, y2_ref, w_ref, linv_ref, s1_ref, s2_ref, y_ref, z_ref, m_ref, col_ref, g_ref, x_ref, oh_ref, t_ref
):
    c = c_ref[0]
    m_ref[V:, :] = jnp.zeros((8, LANES), F32)

    def loop(src_ref, dst_ref, first):
        start_op(pay_ref, src_ref, dst_ref)
        split_to(x_ref, src_ref)
        if first:
            one_hot(pay_ref, oh_ref, 0)
            one_hot(pay_ref, oh_ref, 1)
        issue(x_ref, oh_ref, t_ref, 0, 0)

        def step(it, carry):
            for u in range(UN):
                k = UN * it + u
                issue(x_ref, oh_ref, t_ref, jnp.minimum(k + 1, ONE - 1), (u + 1) % 2)
                for rc in (2 * (u % 2), 2 * (u % 2) + 1):
                    lane_block(pay_ref, src_ref, dst_ref, rc, ONE + (UN // 2) * it + u // 2)
                if first:
                    one_hot(pay_ref, oh_ref, jnp.minimum(k + 2, ONE - 1))
                else:
                    factor_piece(m_ref, col_ref, k * CHOL)
                take(pay_ref, dst_ref, t_ref, k, u % 2)
            return carry

        lax.fori_loop(0, ONE // UN, step, 0)

    loop(pay_ref, y_ref, True)
    gram_to(m_ref, flat(y_ref))
    loop(y_ref, z_ref, False)
    solve_to(y2_ref, inverse_of(m_ref), z_ref)
    gram_to(m_ref, flat(y2_ref))
    loop(y2_ref, w_ref, False)
    linv = inverse_of(m_ref)
    linv_ref[...] = linv
    first = index_row(pay_ref, SEND0 + c).astype(jnp.int32)
    second = index_row(pay_ref, SEND0 + NC + c // 2).astype(jnp.int32)
    half = (c % 2) * (V // 2)
    tiles = [slice(8 * t, 8 * t + 8) for t in range(3 * TILES)]
    for n, index in enumerate((first, second)):
        for at, piece in zip(tiles, rows_of(w_ref, index, tiles)):
            g_ref[n, at, :] = piece
    both = jnp.concatenate([g_ref[n, a * V : a * V + V, :] for n in range(2) for a in range(3)], axis=1)
    image = jnp.dot(linv, both, precision=HIGH, preferred_element_type=F32)
    for a in range(3):
        s1_ref[a * V : a * V + V, :] = image[:, a * LANES : a * LANES + LANES]
        g_ref[1, a * V : a * V + V, :] = image[:, (3 + a) * LANES : (4 + a) * LANES]
        s2_ref[a * (V // 2) : (a + 1) * (V // 2), :] = g_ref[1, pl.ds(pl.multiple_of(a * V + half, 8), V // 2), :]


def middle_kernel(c_ref, pay_ref, y2_ref, w_ref, linv_ref, basis_ref, mine1_ref, mine2_ref, center_ref, q_ref):
    c = c_ref[0]
    linv = linv_ref[...]
    solve_to(q_ref, linv, y2_ref)
    basis_ref[...] = q_ref[c]
    tiles = [slice(8 * t, 8 * t + 8) for t in range(3 * TILES)]
    for out_ref, slot in ((mine1_ref, c), (mine2_ref, NC + c // 2)):
        index = index_row(pay_ref, RECV0 + slot).astype(jnp.int32)
        live = index_row(pay_ref, LIVE0 + slot)
        for at, piece in zip(tiles, rows_of(q_ref, index, tiles)):
            out_ref[at, :] = piece * live
    image = jnp.dot(linv, flat(w_ref), precision=HIGH, preferred_element_type=F32)
    center_ref[...] = lax.dot_general(
        flat(q_ref), image, (((1,), (1,)), ((), ())), precision=HIGH, preferred_element_type=F32
    )


def coarse_kernel(c_ref, mine1_ref, mine2_ref, got1_ref, got2_ref, own_ref, a_ref, b_ref, d_ref, r_ref):
    c = c_ref[0]

    def side(ref, count):
        return jnp.concatenate([ref[a * count : a * count + count, :] for a in range(3)], axis=1)

    nt = (((1,), (1,)), ((), ()))
    one = lax.dot_general(side(mine1_ref, V), side(got1_ref, V), nt, precision=HIGH, preferred_element_type=F32) * SCALE
    two = lax.dot_general(side(mine2_ref, V), side(got2_ref, V // 2), nt, precision=HIGH, preferred_element_type=F32) * SCALE
    part = V // NC
    for d in range(NC):
        r_ref[d, 0:part, 0:V] = one[d * part : d * part + part, :]
        r_ref[d, 16 : 16 + part, 0 : V // 2] = two[d * part : d * part + part, :]
    own_ref[...] = r_ref[c]
    a_ref[...] = r_ref[c ^ 1]
    b_ref[...] = r_ref[c ^ 2]
    d_ref[...] = r_ref[c ^ 3]


def join_kernel(c_ref, center_ref, own_ref, a_ref, b_ref, d_ref, out_ref, r_ref):
    c = c_ref[0]
    part = V // NC
    for m, ref in enumerate((own_ref, a_ref, b_ref, d_ref)):
        r_ref[m] = ref[...]
    for slot in range(NC):
        out_ref[slot if slot < RADIUS else slot + 1] = r_ref[c ^ slot, 0:part, 0:V]
    for slot in range(NC, SLOTS):
        even = 2 * (slot - NC)
        low = r_ref[c ^ even, 16 : 16 + part, 0 : V // 2]
        high = r_ref[c ^ (even + 1), 16 : 16 + part, 0 : V // 2]
        out_ref[slot + 1] = jnp.concatenate([low, high], axis=1)
    for d in range(NC):
        @pl.when(c == d)
        def _():
            out_ref[RADIUS] = center_ref[d * part : d * part + part, :]


def shards(test_vectors, ell_values, ell_cols, ell_count, pivot, send_rows, recv_rows, ov_count):
    shape = jax.ShapeDtypeStruct
    c = lax.axis_index("crow").astype(jnp.int32).reshape(1)
    x = jnp.transpose(test_vectors[0], (1, 0, 2)).reshape(3 * V, LANES)
    packed = pl.pallas_call(
        pack_kernel,
        out_shape=shape((PACKED, LANES), F32),
        in_specs=[smem(), smem()] + [vmem()] * 7,
        out_specs=vmem(),
    )(
        c,
        ov_count.reshape(SLOTS),
        x,
        ell_values.reshape(9 * NB, 1, LANES),
        ell_cols.reshape(NB, 1, LANES),
        ell_count.reshape(1, LANES),
        pivot.reshape(3, 1, LANES),
        send_rows.reshape(SLOTS, 1, OVD),
        recv_rows.reshape(SLOTS, 1, OVD),
    )
    pay = lax.all_gather(packed, "crow", axis=0)
    block = (NC, 3 * V, LANES)
    y2, w, linv, s1, s2 = pl.pallas_call(
        main_kernel,
        out_shape=(
            shape(block, F32),
            shape(block, F32),
            shape((V, V), F32),
            shape((3 * V, LANES), F32),
            shape((3 * V // 2, LANES), F32),
        ),
        in_specs=[smem(), vmem()],
        out_specs=(vmem(),) * 5,
        scratch_shapes=[
            pltpu.VMEM(block, F32),
            pltpu.VMEM(block, F32),
            pltpu.VMEM((V + 8, LANES), F32),
            pltpu.VMEM((CHOL, V + 8, LANES), F32),
            pltpu.VMEM((2, 3 * V, LANES), F32),
            pltpu.VMEM((6 * V, NC * LANES), BF16),
            pltpu.VMEM((2, ONE, NC * LANES, 2 * LANES), BF16),
            pltpu.VMEM((2, 2, 3 * V, 2 * LANES), F32),
        ],
    )(c, pay)

    size = lax.axis_size("sub")

    def across(piece, slot_of):
        pairs = []
        for j in range(size):
            for n in range(NC):
                i = (j - OFFSETS[slot_of(n)]) % size
                pairs.append((j * NC + n, i * NC + n))
        return lax.ppermute(piece, ("sub", "crow"), pairs)

    got1 = across(s1, lambda n: n)
    got2 = across(s2, lambda n: NC + n // 2)
    basis, mine1, mine2, center = pl.pallas_call(
        middle_kernel,
        out_shape=(
            shape((3 * V, LANES), F32),
            shape((3 * V, LANES), F32),
            shape((3 * V, LANES), F32),
            shape((V, V), F32),
        ),
        in_specs=[smem()] + [vmem()] * 4,
        out_specs=(vmem(),) * 4,
        scratch_shapes=[pltpu.VMEM(block, F32)],
    )(c, pay, y2, w, linv)
    slab = shape((32, LANES), F32)
    own, to1, to2, to3 = pl.pallas_call(
        coarse_kernel,
        out_shape=(slab,) * 4,
        in_specs=[smem()] + [vmem()] * 4,
        out_specs=(vmem(),) * 4,
        scratch_shapes=[pltpu.VMEM((NC, 32, LANES), F32)],
    )(c, mine1, mine2, got1, got2)
    got = [lax.ppermute(t, "crow", [(n, n ^ m) for n in range(NC)]) for m, t in ((1, to1), (2, to2), (3, to3))]
    coarse = pl.pallas_call(
        join_kernel,
        out_shape=shape((2 * RADIUS + 1, V // NC, V), F32),
        in_specs=[smem()] + [vmem()] * 5,
        out_specs=vmem(),
        scratch_shapes=[pltpu.VMEM((NC, 32, LANES), F32)],
    )(c, center, own, *got)
    basis = jnp.transpose(basis.reshape(3, V, LANES), (1, 0, 2))
    return basis[None], coarse[None]


def solution(mesh):
    placed = (
        P("sub", None, None, "crow"),
        P("sub", None, None, "crow"),
        P("sub", None, "crow"),
        P("sub", "crow"),
        P("sub", None, "crow"),
        P("sub", None, "crow"),
        P("sub", None, "crow"),
        P("sub", None, "crow"),
    )
    return jax.shard_map(
        shards,
        mesh=mesh,
        in_specs=placed,
        out_specs=(P("sub", None, None, "crow"), P("sub", None, "crow", None)),
        check_vma=False,
    )
```

```python
import jax
import jax.numpy as jnp
from jax import lax
from jax.experimental import pallas as pl
from jax.experimental.pallas import tpu as pltpu
from jax.sharding import PartitionSpec as P

RADIUS = 3
SLOTS = 2 * RADIUS
V = 48
LANES = 128
NB = 27
NC = 4
OVD = 32
SCALE = float(LANES * NC // OVD)
TILES = V // 8

COL0 = 0
PIV0 = COL0 + NB
SEND0 = PIV0 + 3
RECV0 = SEND0 + SLOTS
LIVE0 = RECV0 + SLOTS
PACKED = LIVE0 + SLOTS

OFFSETS = [o - RADIUS if o < RADIUS else o - RADIUS + 1 for o in range(SLOTS)]
SENT = [0, 2, 5, 3]
GOT = [SENT[c ^ 2] for c in range(NC)]
SPLIT = [1, 4, 1, 4]
HIGH = lax.Precision.HIGHEST
F32 = jnp.float32


def vmem():
    return pl.BlockSpec(memory_space=pltpu.VMEM)


def smem():
    return pl.BlockSpec(memory_space=pltpu.SMEM)


def whole():
    return pl.BlockSpec(memory_space=pl.ANY)


def pack_kernel(c_ref, ov_ref, col_ref, cnt_ref, piv_ref, send_ref, recv_ref, out_ref):
    count = cnt_ref[...]
    for k in range(NB):
        out_ref[COL0 + k : COL0 + k + 1, :] = jnp.where(k < count, col_ref[k].astype(F32), -1.0)
    for a in range(3):
        out_ref[PIV0 + a : PIV0 + a + 1, :] = piv_ref[a]
    lane = lax.broadcasted_iota(jnp.int32, (1, LANES), 1)
    c = c_ref[0]
    here = (lane // OVD) == c
    for o in range(SLOTS):
        for ref, base in ((send_ref, SEND0), (recv_ref, RECV0)):
            piece = ref[o].astype(F32)
            row = jnp.concatenate([piece] * NC, axis=1)
            out_ref[base + o : base + o + 1, :] = jnp.where(here, row, 0.0)
        alive = here & ((lane % OVD) < ov_ref[o])
        out_ref[LIVE0 + o : LIVE0 + o + 1, :] = jnp.where(alive, 1.0, 0.0).astype(F32)


def fetch(pairs, sem):
    copies = [pltpu.make_async_copy(src, dst, sem.at[n]) for n, (src, dst) in enumerate(pairs)]
    for copy in copies:
        copy.start()
    for copy in copies:
        copy.wait()


def entry(table, c):
    value = jnp.int32(table[0])
    for n in range(1, NC):
        value = jnp.where(c == n, table[n], value)
    return value


def wide(row):
    return jnp.broadcast_to(row, (8, LANES))


def lanes_of(block, index):
    return jnp.take_along_axis(block, index, axis=1)


def start_op(small_ref, src_ref, dst_ref):
    for q in range(NC):
        for a in range(3):
            piv = wide(small_ref[q, PIV0 + a : PIV0 + a + 1, :])
            for t in range(TILES):
                rows = slice(a * V + 8 * t, a * V + 8 * t + 8)
                dst_ref[q, rows, :] = piv * src_ref[q, rows, :]


ONE = 18
BF16 = jnp.bfloat16


def value_row(val_ref, rc, ab, k):
    return wide(val_ref[rc, ab * NB + k])


def add_block(val, dst_ref, rc, pick_of):
    for t in range(TILES):
        pick = [pick_of(b, t) for b in range(3)]
        for a in range(3):
            at = slice(a * V + 8 * t, a * V + 8 * t + 8)
            dst_ref[rc, at, :] = dst_ref[rc, at, :] + (
                val[3 * a] * pick[0] + val[3 * a + 1] * pick[1] + val[3 * a + 2] * pick[2]
            )


def lane_block(val_ref, small_ref, src_ref, dst_ref, rc, k):
    col = wide(small_ref[rc, pl.ds(COL0 + k, 1), :]).astype(jnp.int32)
    val = [jnp.where(col >= 0, value_row(val_ref, rc, ab, k), 0.0) for ab in range(9)]
    index = col & (LANES - 1)
    odd = (col & LANES) != 0
    top = col >= 2 * LANES

    def pick_of(b, t):
        got = [lanes_of(src_ref[q, b * V + 8 * t : b * V + 8 * t + 8, :], index) for q in range(NC)]
        return jnp.where(top, jnp.where(odd, got[3], got[2]), jnp.where(odd, got[1], got[0]))

    add_block(val, dst_ref, rc, pick_of)


def one_hot(small_ref, oh_ref, k):
    half = 2 * LANES
    place = lax.broadcasted_iota(jnp.int32, (half, half), 0).astype(F32).astype(BF16)
    for m in range(2):
        col = jnp.concatenate([small_ref[2 * m + n, pl.ds(COL0 + k, 1), :] for n in range(2)], axis=1)
        for h in range(2):
            local = col - float(h * half)
            local = jnp.where((local >= 0.0) & (local < float(half)), local, -1.0)
            target = jnp.concatenate([jnp.broadcast_to(local, (16, half)).astype(BF16)] * (half // 16), axis=0)
            oh_ref[m, k, h * half : h * half + half, :] = jnp.where(
                place == target, jnp.ones((), BF16), jnp.zeros((), BF16)
            )


def split_to(x_ref, src_ref):
    for q in range(NC):
        at = slice(q * LANES, q * LANES + LANES)
        value = src_ref[q, 0 : 3 * V, :]
        high = value.astype(BF16)
        x_ref[0 : 3 * V, at] = high
        x_ref[3 * V :, at] = (value - high.astype(F32)).astype(BF16)


def issue(x_ref, oh_ref, t_ref, k, parity):
    for m in range(2):
        got = jnp.dot(x_ref[...], oh_ref[m, k], preferred_element_type=F32)
        t_ref[parity, m] = got[: 3 * V, :] + got[3 * V :, :]


def take(val_ref, dst_ref, t_ref, k, parity):
    for m in range(2):
        for n in range(2):
            at = slice(n * LANES, n * LANES + LANES)
            rc = 2 * m + n
            val = [value_row(val_ref, rc, ab, k) for ab in range(9)]
            add_block(val, dst_ref, rc, lambda b, t: t_ref[parity, m, b * V + 8 * t : b * V + 8 * t + 8, at])


def flat(ref):
    return jnp.concatenate([ref[q, a * V : a * V + V, :] for a in range(3) for q in range(NC)], axis=1)


def gram_to(m_ref, block):
    gram = lax.dot_general(block, block, (((1,), (1,)), ((), ())), precision=HIGH, preferred_element_type=F32)
    row = lax.broadcasted_iota(jnp.int32, (V, 64), 0)
    lane = lax.broadcasted_iota(jnp.int32, (V, 64), 1)
    eye = jnp.where(row == lane, 1.0, 0.0).astype(F32)
    m_ref[:V, :] = jnp.concatenate([eye, gram, jnp.zeros((V, LANES - 64 - V), F32)], axis=1)


CHOL = 3
UN = 6


def factor_piece(m_ref, col_ref, j):
    sub = lax.broadcasted_iota(jnp.int32, (8, LANES), 0)
    m = [m_ref[8 * t : 8 * t + 8, :] for t in range(TILES)]
    cols = []
    for s in range(CHOL):
        index = jnp.full((8, LANES), 64 + s, jnp.int32) + j
        cols.append([lanes_of(m[t], index) for t in range(TILES)])
        for t in range(TILES):
            col_ref[s, 8 * t : 8 * t + 8, :] = cols[s][t]
    for s in range(CHOL):
        row = wide(m_ref[pl.ds(j + s, 1), :])
        head = {n: wide(col_ref[n, pl.ds(j + s, 1), :]) for n in range(s, CHOL)}
        inverse = 1.0 / head[s]
        for t in range(TILES):
            factor = jnp.where(sub + 8 * t > j + s, cols[s][t] * inverse, 0.0)
            m[t] = m[t] - factor * row
            m_ref[8 * t : 8 * t + 8, :] = m[t]
            for n in range(s + 1, CHOL):
                cols[n][t] = cols[n][t] - factor * head[n]
                col_ref[n, 8 * t : 8 * t + 8, :] = cols[n][t]


def inverse_of(m_ref):
    m = m_ref[:V, :]
    row = lax.broadcasted_iota(jnp.int32, (V, LANES), 0)
    lane = lax.broadcasted_iota(jnp.int32, (V, LANES), 1)
    diag = jnp.sum(jnp.where(lane == row + 64, m, 0.0), axis=1, keepdims=True)
    return m[:, :V] / jnp.sqrt(diag)


def solve_to(dst_ref, linv, src_ref):
    out = jnp.dot(linv, flat(src_ref), precision=HIGH, preferred_element_type=F32)
    for a in range(3):
        for q in range(NC):
            at = (a * NC + q) * LANES
            dst_ref[q, a * V : a * V + V, :] = out[:, at : at + LANES]


def rows_of(src_ref, index, tiles, c):
    block = (lax.broadcasted_iota(jnp.int32, (8, LANES), 1) // OVD) ^ c
    out = []
    for at in tiles:
        pick = lanes_of(src_ref[NC - 1, at, :], index)
        for q in range(NC - 1):
            pick = jnp.where(block == q, lanes_of(src_ref[q, at, :], index), pick)
        out.append(pick)
    return out


def index_row(small_ref, row):
    total = small_ref[0, pl.ds(row, 1), :]
    for q in range(1, NC):
        total = total + small_ref[q, pl.ds(row, 1), :]
    return total


def main_kernel(
    c_ref, x0, x1, x2, x3, v0, v1, v2, v3, p0, p1, p2, p3,
    y2_ref, w_ref, linv_ref, s1_ref, s2_ref, row_ref,
    in_ref, val_ref, small_ref, sem, y_ref, z_ref, m_ref, col_ref, g_ref, x_ref, oh_ref, t_ref,
):
    c = c_ref[0]
    fetch(
        [(ref, dst.at[m]) for refs, dst in (((x0, x1, x2, x3), in_ref), ((v0, v1, v2, v3), val_ref), ((p0, p1, p2, p3), small_ref)) for m, ref in enumerate(refs)],
        sem,
    )
    for m in range(NC):
        col = small_ref[m, COL0 : COL0 + NB, :]
        local = (col.astype(jnp.int32) ^ (c * LANES)).astype(F32)
        small_ref[m, COL0 : COL0 + NB, :] = jnp.where(col < 0.0, -1.0, local)
    m_ref[V:, :] = jnp.zeros((8, LANES), F32)

    def loop(src_ref, dst_ref, first):
        start_op(small_ref, src_ref, dst_ref)
        split_to(x_ref, src_ref)
        if first:
            one_hot(small_ref, oh_ref, 0)
            one_hot(small_ref, oh_ref, 1)
        issue(x_ref, oh_ref, t_ref, 0, 0)

        def step(it, carry):
            for u in range(UN):
                k = UN * it + u
                issue(x_ref, oh_ref, t_ref, jnp.minimum(k + 1, ONE - 1), (u + 1) % 2)
                for rc in (2 * (u % 2), 2 * (u % 2) + 1):
                    lane_block(val_ref, small_ref, src_ref, dst_ref, rc, ONE + (UN // 2) * it + u // 2)
                if first:
                    one_hot(small_ref, oh_ref, jnp.minimum(k + 2, ONE - 1))
                else:
                    factor_piece(m_ref, col_ref, k * CHOL)
                take(val_ref, dst_ref, t_ref, k, u % 2)
            return carry

        lax.fori_loop(0, ONE // UN, step, 0)

    loop(in_ref, y_ref, True)
    gram_to(m_ref, flat(y_ref))
    loop(y_ref, z_ref, False)
    solve_to(y2_ref, inverse_of(m_ref), z_ref)
    gram_to(m_ref, flat(y2_ref))
    loop(y2_ref, w_ref, False)
    linv = inverse_of(m_ref)
    linv_ref[...] = linv
    first = wide(index_row(small_ref, SEND0 + entry(SENT, c))).astype(jnp.int32)
    second = wide(index_row(small_ref, SEND0 + entry(SPLIT, c))).astype(jnp.int32)
    half = (c // 2) * (V // 2)
    for n, slot in enumerate((entry(GOT, c), entry(SPLIT, c))):
        row_ref[2 * n : 2 * n + 1, :] = index_row(small_ref, RECV0 + slot)
        row_ref[2 * n + 1 : 2 * n + 2, :] = index_row(small_ref, LIVE0 + slot)
    tiles = [slice(8 * t, 8 * t + 8) for t in range(3 * TILES)]
    for n, index in enumerate((first, second)):
        for at, piece in zip(tiles, rows_of(w_ref, index, tiles, c)):
            g_ref[n, at, :] = piece
    both = jnp.concatenate([g_ref[n, a * V : a * V + V, :] for n in range(2) for a in range(3)], axis=1)
    image = jnp.dot(linv, both, precision=HIGH, preferred_element_type=F32)
    for a in range(3):
        s1_ref[a * V : a * V + V, :] = image[:, a * LANES : a * LANES + LANES]
        g_ref[1, a * V : a * V + V, :] = image[:, (3 + a) * LANES : (4 + a) * LANES]
        s2_ref[a * (V // 2) : (a + 1) * (V // 2), :] = g_ref[1, pl.ds(pl.multiple_of(a * V + half, 8), V // 2), :]


def middle_kernel(c_ref, row_ref, y2_ref, w_ref, linv_ref, basis_ref, mine1_ref, mine2_ref, center_ref, q_ref):
    c = c_ref[0]
    linv = linv_ref[...]
    solve_to(q_ref, linv, y2_ref)
    basis_ref[...] = q_ref[0]
    tiles = [slice(8 * t, 8 * t + 8) for t in range(3 * TILES)]
    for n, out_ref in enumerate((mine1_ref, mine2_ref)):
        index = wide(row_ref[2 * n : 2 * n + 1, :]).astype(jnp.int32)
        live = wide(row_ref[2 * n + 1 : 2 * n + 2, :])
        for at, piece in zip(tiles, rows_of(q_ref, index, tiles, c)):
            out_ref[at, :] = piece * live
    image = jnp.dot(linv, flat(w_ref), precision=HIGH, preferred_element_type=F32)
    center_ref[...] = lax.dot_general(
        flat(q_ref), image, (((1,), (1,)), ((), ())), precision=HIGH, preferred_element_type=F32
    )


def coarse_kernel(c_ref, mine1_ref, mine2_ref, in1_ref, in2_ref, own_ref, a_ref, b_ref, d_ref, r_ref, got1_ref, got2_ref, sem):
    c = c_ref[0]
    fetch([(in1_ref, got1_ref), (in2_ref, got2_ref)], sem)

    def side(ref, count):
        return jnp.concatenate([ref[a * count : a * count + count, :] for a in range(3)], axis=1)

    nt = (((1,), (1,)), ((), ()))
    one = lax.dot_general(side(mine1_ref, V), side(got1_ref, V), nt, precision=HIGH, preferred_element_type=F32) * SCALE
    two = lax.dot_general(side(mine2_ref, V), side(got2_ref, V // 2), nt, precision=HIGH, preferred_element_type=F32) * SCALE
    part = V // NC
    for d in range(NC):
        r_ref[d, 0:part, 0:V] = one[d * part : d * part + part, :]
        r_ref[d, 16 : 16 + part, 0 : V // 2] = two[d * part : d * part + part, :]
    own_ref[...] = r_ref[c]
    a_ref[...] = r_ref[c ^ 1]
    b_ref[...] = r_ref[c ^ 2]
    d_ref[...] = r_ref[c ^ 3]


def join_kernel(c_ref, center_ref, own_ref, a_ref, b_ref, d_ref, out_ref, r_ref, sem):
    c = c_ref[0]
    part = V // NC
    fetch([(ref, r_ref.at[m]) for m, ref in enumerate((own_ref, a_ref, b_ref, d_ref))], sem)

    def put(place, value):
        for v in range(part):
            out_ref[place * part + v] = value[v : v + 1, :]

    for d in range(NC):
        slot = GOT[d]
        put(slot if slot < RADIUS else slot + 1, r_ref[c ^ d, 0:part, 0:V])
    for d in range(2):
        slot = SPLIT[d]
        sides = [r_ref[c ^ (d + 2 * h), 16 : 16 + part, 0 : V // 2] for h in range(2)]
        put(slot if slot < RADIUS else slot + 1, jnp.concatenate(sides, axis=1))
    for d in range(NC):

        @pl.when(c == d)
        def _():
            put(RADIUS, center_ref[d * part : d * part + part, :])


def shards(test_vectors, ell_values, ell_cols, ell_count, pivot, send_rows, recv_rows, ov_count):
    shape = jax.ShapeDtypeStruct
    c = lax.axis_index("crow").astype(jnp.int32).reshape(1)
    x = jnp.transpose(test_vectors[0], (1, 0, 2)).reshape(3 * V, LANES)
    values = ell_values.reshape(9 * NB, 1, LANES)

    def pass_on(piece, m):
        return lax.ppermute(piece, "crow", [(n, n ^ m) for n in range(NC)])

    far_x = pass_on(x, 2)
    far_v = pass_on(values, 2)
    small = pl.pallas_call(
        pack_kernel,
        out_shape=shape((PACKED, LANES), F32),
        in_specs=[smem(), smem()] + [vmem()] * 5,
        out_specs=vmem(),
    )(
        c,
        ov_count.reshape(SLOTS),
        ell_cols.reshape(NB, 1, LANES),
        ell_count.reshape(1, LANES),
        pivot.reshape(3, 1, LANES),
        send_rows.reshape(SLOTS, 1, OVD),
        recv_rows.reshape(SLOTS, 1, OVD),
    )
    far_s = pass_on(small, 2)
    blocks = []
    for own, far in ((x, far_x), (values, far_v), (small, far_s)):
        blocks += [own, pass_on(own, 1), far, pass_on(far, 1)]
    block = (NC, 3 * V, LANES)
    y2, w, linv, s1, s2, row = pl.pallas_call(
        main_kernel,
        out_shape=(
            shape(block, F32),
            shape(block, F32),
            shape((V, V), F32),
            shape((3 * V, LANES), F32),
            shape((3 * V // 2, LANES), F32),
            shape((8, LANES), F32),
        ),
        in_specs=[smem()] + [whole()] * 12,
        out_specs=(vmem(),) * 6,
        scratch_shapes=[
            pltpu.VMEM(block, F32),
            pltpu.VMEM((NC, 9 * NB, 1, LANES), F32),
            pltpu.VMEM((NC, PACKED, LANES), F32),
            pltpu.SemaphoreType.DMA((12,)),
            pltpu.VMEM(block, F32),
            pltpu.VMEM(block, F32),
            pltpu.VMEM((V + 8, LANES), F32),
            pltpu.VMEM((CHOL, V + 8, LANES), F32),
            pltpu.VMEM((2, 3 * V, LANES), F32),
            pltpu.VMEM((6 * V, NC * LANES), BF16),
            pltpu.VMEM((2, ONE, NC * LANES, 2 * LANES), BF16),
            pltpu.VMEM((2, 2, 3 * V, 2 * LANES), F32),
        ],
    )(c, *blocks)

    size = lax.axis_size("sub")

    def across(piece, slots, turn):
        pairs = []
        for j in range(size):
            for n in range(NC):
                i = (j - OFFSETS[slots[n]]) % size
                pairs.append((j * NC + n, i * NC + (n ^ turn)))
        return lax.ppermute(piece, ("sub", "crow"), pairs)

    got1 = across(s1, SENT, 2)
    got2 = across(s2, SPLIT, 0)
    basis, mine1, mine2, center = pl.pallas_call(
        middle_kernel,
        out_shape=(
            shape((3 * V, LANES), F32),
            shape((3 * V, LANES), F32),
            shape((3 * V, LANES), F32),
            shape((V, V), F32),
        ),
        in_specs=[smem()] + [vmem()] * 4,
        out_specs=(vmem(),) * 4,
        scratch_shapes=[pltpu.VMEM(block, F32)],
    )(c, row, y2, w, linv)
    slab = shape((32, LANES), F32)
    own, to1, to2, to3 = pl.pallas_call(
        coarse_kernel,
        out_shape=(slab,) * 4,
        in_specs=[smem()] + [vmem()] * 2 + [whole()] * 2,
        out_specs=(vmem(),) * 4,
        scratch_shapes=[
            pltpu.VMEM((NC, 32, LANES), F32),
            pltpu.VMEM((3 * V, LANES), F32),
            pltpu.VMEM((3 * V // 2, LANES), F32),
            pltpu.SemaphoreType.DMA((2,)),
        ],
    )(c, mine1, mine2, got1, got2)
    got = [pass_on(t, m) for m, t in ((1, to1), (2, to2), (3, to3))]
    coarse = pl.pallas_call(
        join_kernel,
        out_shape=shape(((2 * RADIUS + 1) * (V // NC), 1, V), F32),
        in_specs=[smem(), vmem()] + [whole()] * 4,
        out_specs=vmem(),
        scratch_shapes=[pltpu.VMEM((NC, 32, LANES), F32), pltpu.SemaphoreType.DMA((4,))],
    )(c, center, own, *got)
    coarse = coarse.reshape(2 * RADIUS + 1, V // NC, V)
    basis = jnp.transpose(basis.reshape(3, V, LANES), (1, 0, 2))
    return basis[None], coarse[None]


def solution(mesh):
    placed = (
        P("sub", None, None, "crow"),
        P("sub", None, None, "crow"),
        P("sub", None, "crow"),
        P("sub", "crow"),
        P("sub", None, "crow"),
        P("sub", None, "crow"),
        P("sub", None, "crow"),
        P("sub", None, "crow"),
    )
    return jax.shard_map(
        shards,
        mesh=mesh,
        in_specs=placed,
        out_specs=(P("sub", None, None, "crow"), P("sub", None, "crow", None)),
        check_vma=False,
    )
```

```python
import jax
import jax.numpy as jnp
from jax import lax
from jax.experimental import pallas as pl
from jax.experimental.pallas import tpu as pltpu
from jax.sharding import PartitionSpec as P

RADIUS = 3
SLOTS = 2 * RADIUS
V = 48
LANES = 128
NB = 27
NC = 4
OVD = 32
SCALE = float(LANES * NC // OVD)
TILES = V // 8

COL0 = 3 * V
PIV0 = COL0 + NB
SEND0 = PIV0 + 3
RECV0 = SEND0 + SLOTS
LIVE0 = RECV0 + SLOTS
PACKED = LIVE0 + SLOTS

OFFSETS = [o - RADIUS if o < RADIUS else o - RADIUS + 1 for o in range(SLOTS)]
SENT = [0, 2, 5, 3]
GOT = [SENT[c ^ 2] for c in range(NC)]
SPLIT = [1, 4, 1, 4]
HIGH = lax.Precision.HIGHEST
F32 = jnp.float32


def vmem():
    return pl.BlockSpec(memory_space=pltpu.VMEM)


def smem():
    return pl.BlockSpec(memory_space=pltpu.SMEM)


LIMIT = pltpu.CompilerParams(vmem_limit_bytes=40 * 2**20)


def near(array):
    return pltpu.with_memory_space_constraint(array, pltpu.VMEM)


class Blocks:
    def __init__(self, refs):
        self.refs = refs

    def __getitem__(self, at):
        return self.refs[at[0]][at[1:]]


def pack_kernel(c_ref, ov_ref, x_ref, col_ref, cnt_ref, piv_ref, send_ref, recv_ref, out_ref):
    out_ref[0 : 3 * V, :] = x_ref[...]
    count = cnt_ref[...]
    for k in range(NB):
        out_ref[COL0 + k : COL0 + k + 1, :] = jnp.where(k < count, col_ref[k].astype(F32), -1.0)
    for a in range(3):
        out_ref[PIV0 + a : PIV0 + a + 1, :] = piv_ref[a]
    lane = lax.broadcasted_iota(jnp.int32, (1, LANES), 1)
    c = c_ref[0]
    here = (lane // OVD) == c
    for o in range(SLOTS):
        for ref, base in ((send_ref, SEND0), (recv_ref, RECV0)):
            piece = ref[o].astype(F32)
            row = jnp.concatenate([piece] * NC, axis=1)
            out_ref[base + o : base + o + 1, :] = jnp.where(here, row, 0.0)
        alive = here & ((lane % OVD) < ov_ref[o])
        out_ref[LIVE0 + o : LIVE0 + o + 1, :] = jnp.where(alive, 1.0, 0.0).astype(F32)


def entry(table, c):
    value = jnp.int32(table[0])
    for n in range(1, NC):
        value = jnp.where(c == n, table[n], value)
    return value


def wide(row):
    return jnp.broadcast_to(row, (8, LANES))


def lanes_of(block, index):
    return jnp.take_along_axis(block, index, axis=1)


def start_op(small_ref, src_ref, dst_ref):
    for q in range(NC):
        for a in range(3):
            piv = wide(small_ref[q, PIV0 + a : PIV0 + a + 1, :])
            for t in range(TILES):
                rows = slice(a * V + 8 * t, a * V + 8 * t + 8)
                dst_ref[q, rows, :] = piv * src_ref[q, rows, :]


ONE = 18
BF16 = jnp.bfloat16


def value_row(val_ref, rc, ab, k):
    return wide(val_ref[rc, ab * NB + k, :, :])


def add_block(val, dst_ref, rc, pick_of):
    for t in range(TILES):
        pick = [pick_of(b, t) for b in range(3)]
        for a in range(3):
            at = slice(a * V + 8 * t, a * V + 8 * t + 8)
            dst_ref[rc, at, :] = dst_ref[rc, at, :] + (
                val[3 * a] * pick[0] + val[3 * a + 1] * pick[1] + val[3 * a + 2] * pick[2]
            )


def lane_block(val_ref, cols_ref, src_ref, dst_ref, rc, k):
    col = wide(cols_ref[rc, pl.ds(k, 1), :]).astype(jnp.int32)
    val = [jnp.where(col >= 0, value_row(val_ref, rc, ab, k), 0.0) for ab in range(9)]
    index = col & (LANES - 1)
    odd = (col & LANES) != 0
    top = col >= 2 * LANES

    def pick_of(b, t):
        got = [lanes_of(src_ref[q, b * V + 8 * t : b * V + 8 * t + 8, :], index) for q in range(NC)]
        return jnp.where(top, jnp.where(odd, got[3], got[2]), jnp.where(odd, got[1], got[0]))

    add_block(val, dst_ref, rc, pick_of)


def one_hot(cols_ref, oh_ref, k):
    half = 2 * LANES
    place = lax.broadcasted_iota(jnp.int32, (half, half), 0).astype(F32).astype(BF16)
    for m in range(2):
        col = jnp.concatenate([cols_ref[2 * m + n, pl.ds(k, 1), :] for n in range(2)], axis=1)
        for h in range(2):
            local = col - float(h * half)
            local = jnp.where((local >= 0.0) & (local < float(half)), local, -1.0)
            target = jnp.concatenate([jnp.broadcast_to(local, (16, half)).astype(BF16)] * (half // 16), axis=0)
            oh_ref[m, k, h * half : h * half + half, :] = jnp.where(
                place == target, jnp.ones((), BF16), jnp.zeros((), BF16)
            )


def split_to(x_ref, src_ref):
    for q in range(NC):
        at = slice(q * LANES, q * LANES + LANES)
        value = src_ref[q, 0 : 3 * V, :]
        x_ref[0 : 3 * V, at], x_ref[3 * V :, at] = halves(value)


def issue(x_ref, oh_ref, t_ref, k, parity):
    for m in range(2):
        got = jnp.dot(x_ref[...], oh_ref[m, k], preferred_element_type=F32)
        t_ref[parity, m] = got[: 3 * V, :] + got[3 * V :, :]


def take(val_ref, dst_ref, t_ref, k, parity):
    for m in range(2):
        for n in range(2):
            at = slice(n * LANES, n * LANES + LANES)
            rc = 2 * m + n
            val = [value_row(val_ref, rc, ab, k) for ab in range(9)]
            add_block(val, dst_ref, rc, lambda b, t: t_ref[parity, m, b * V + 8 * t : b * V + 8 * t + 8, at])


def flat(ref):
    return jnp.concatenate([ref[q, a * V : a * V + V, :] for a in range(3) for q in range(NC)], axis=1)


NT = (((1,), (1,)), ((), ()))


def gram_to(m_ref, x_ref):
    total = jnp.zeros((2 * V, V), F32)
    for b in range(3):
        high = x_ref[b * V : b * V + V, :]
        both = jnp.concatenate([high, x_ref[(3 + b) * V : (4 + b) * V, :]], axis=0)
        total = total + lax.dot_general(both, high, NT, preferred_element_type=F32)
    low = total[V:, :]
    gram = total[:V, :] + low + low.T
    row = lax.broadcasted_iota(jnp.int32, (V, 64), 0)
    lane = lax.broadcasted_iota(jnp.int32, (V, 64), 1)
    eye = jnp.where(row == lane, 1.0, 0.0).astype(F32)
    m_ref[:V, :] = jnp.concatenate([eye, gram, jnp.zeros((V, LANES - 64 - V), F32)], axis=1)


def halves(value):
    high = value.astype(BF16)
    return high, (value - high.astype(F32)).astype(BF16)


def mix(linv, value):
    left, left_low = halves(linv)
    right, right_low = halves(value)
    return jnp.dot(
        jnp.concatenate([left, left, left_low], axis=1),
        jnp.concatenate([right, right_low, right], axis=0),
        preferred_element_type=F32,
    )


CHOL = 3
UN = 6


def factor_piece(m_ref, col_ref, j):
    sub = lax.broadcasted_iota(jnp.int32, (8, LANES), 0)
    m = [m_ref[8 * t : 8 * t + 8, :] for t in range(TILES)]
    cols = []
    for s in range(CHOL):
        index = jnp.full((8, LANES), 64 + s, jnp.int32) + j
        cols.append([lanes_of(m[t], index) for t in range(TILES)])
        for t in range(TILES):
            col_ref[s, 8 * t : 8 * t + 8, :] = cols[s][t]
    for s in range(CHOL):
        row = wide(m_ref[pl.ds(j + s, 1), :])
        head = {n: wide(col_ref[n, pl.ds(j + s, 1), :]) for n in range(s, CHOL)}
        inverse = 1.0 / head[s]
        for t in range(TILES):
            factor = jnp.where(sub + 8 * t > j + s, cols[s][t] * inverse, 0.0)
            m[t] = m[t] - factor * row
            m_ref[8 * t : 8 * t + 8, :] = m[t]
            for n in range(s + 1, CHOL):
                cols[n][t] = cols[n][t] - factor * head[n]
                col_ref[n, 8 * t : 8 * t + 8, :] = cols[n][t]


def inverse_of(m_ref):
    m = m_ref[:V, :]
    row = lax.broadcasted_iota(jnp.int32, (V, LANES), 0)
    lane = lax.broadcasted_iota(jnp.int32, (V, LANES), 1)
    diag = jnp.sum(jnp.where(lane == row + 64, m, 0.0), axis=1, keepdims=True)
    return m[:, :V] / jnp.sqrt(diag)


def solve_to(dst_ref, linv, src_ref):
    out = mix(linv, flat(src_ref))
    for a in range(3):
        for q in range(NC):
            at = (a * NC + q) * LANES
            dst_ref[q, a * V : a * V + V, :] = out[:, at : at + LANES]


def rows_of(src_ref, index, tiles, c):
    block = (lax.broadcasted_iota(jnp.int32, (8, LANES), 1) // OVD) ^ c
    out = []
    for at in tiles:
        pick = lanes_of(src_ref[NC - 1, at, :], index)
        for q in range(NC - 1):
            pick = jnp.where(block == q, lanes_of(src_ref[q, at, :], index), pick)
        out.append(pick)
    return out


def index_row(small_ref, row):
    total = small_ref[0, pl.ds(row, 1), :]
    for q in range(1, NC):
        total = total + small_ref[q, pl.ds(row, 1), :]
    return total


def main_kernel(
    c_ref, p0, p1, p2, p3, v0, v1, v2, v3,
    y2_ref, w_ref, linv_ref, s1_ref, s2_ref, row_ref,
    y_ref, z_ref, m_ref, col_ref, g_ref, x_ref, oh_ref, t_ref, cols_ref,
):
    c = c_ref[0]
    small_ref = Blocks((p0, p1, p2, p3))
    val_ref = Blocks((v0, v1, v2, v3))
    for m in range(NC):
        col = small_ref[m, COL0 : COL0 + NB, :]
        local = (col.astype(jnp.int32) ^ (c * LANES)).astype(F32)
        cols_ref[m, 0:NB, :] = jnp.where(col < 0.0, -1.0, local)
    m_ref[V:, :] = jnp.zeros((8, LANES), F32)

    def loop(src_ref, dst_ref, first):
        split_to(x_ref, src_ref)
        if first:
            one_hot(cols_ref, oh_ref, 0)
            one_hot(cols_ref, oh_ref, 1)
        else:
            gram_to(m_ref, x_ref)
        start_op(small_ref, src_ref, dst_ref)
        issue(x_ref, oh_ref, t_ref, 0, 0)

        def step(it, carry):
            for u in range(UN):
                k = UN * it + u
                issue(x_ref, oh_ref, t_ref, jnp.minimum(k + 1, ONE - 1), (u + 1) % 2)
                for rc in (2 * (u % 2), 2 * (u % 2) + 1):
                    lane_block(val_ref, cols_ref, src_ref, dst_ref, rc, ONE + (UN // 2) * it + u // 2)
                if first:
                    one_hot(cols_ref, oh_ref, jnp.minimum(k + 2, ONE - 1))
                else:
                    factor_piece(m_ref, col_ref, k * CHOL)
                take(val_ref, dst_ref, t_ref, k, u % 2)
            return carry

        lax.fori_loop(0, ONE // UN, step, 0)

    loop(small_ref, y_ref, True)
    loop(y_ref, z_ref, False)
    solve_to(y2_ref, inverse_of(m_ref), z_ref)
    loop(y2_ref, w_ref, False)
    linv = inverse_of(m_ref)
    linv_ref[...] = linv
    first = wide(index_row(small_ref, SEND0 + entry(SENT, c))).astype(jnp.int32)
    second = wide(index_row(small_ref, SEND0 + entry(SPLIT, c))).astype(jnp.int32)
    half = (c // 2) * (V // 2)
    for n, slot in enumerate((entry(GOT, c), entry(SPLIT, c))):
        row_ref[2 * n : 2 * n + 1, :] = index_row(small_ref, RECV0 + slot)
        row_ref[2 * n + 1 : 2 * n + 2, :] = index_row(small_ref, LIVE0 + slot)
    tiles = [slice(8 * t, 8 * t + 8) for t in range(3 * TILES)]
    for n, index in enumerate((first, second)):
        for at, piece in zip(tiles, rows_of(w_ref, index, tiles, c)):
            g_ref[n, at, :] = piece
    both = jnp.concatenate([g_ref[n, a * V : a * V + V, :] for n in range(2) for a in range(3)], axis=1)
    image = mix(linv, both)
    for a in range(3):
        s1_ref[a * V : a * V + V, :] = image[:, a * LANES : a * LANES + LANES]
        g_ref[1, a * V : a * V + V, :] = image[:, (3 + a) * LANES : (4 + a) * LANES]
        s2_ref[a * (V // 2) : (a + 1) * (V // 2), :] = g_ref[1, pl.ds(pl.multiple_of(a * V + half, 8), V // 2), :]


def middle_kernel(c_ref, row_ref, y2_ref, w_ref, linv_ref, basis_ref, mine1_ref, mine2_ref, center_ref, q_ref):
    c = c_ref[0]
    linv = linv_ref[...]
    solve_to(q_ref, linv, y2_ref)
    basis_ref[...] = q_ref[0]
    tiles = [slice(8 * t, 8 * t + 8) for t in range(3 * TILES)]
    for n, out_ref in enumerate((mine1_ref, mine2_ref)):
        index = wide(row_ref[2 * n : 2 * n + 1, :]).astype(jnp.int32)
        live = wide(row_ref[2 * n + 1 : 2 * n + 2, :])
        for at, piece in zip(tiles, rows_of(q_ref, index, tiles, c)):
            out_ref[at, :] = piece * live
    image = mix(linv, flat(w_ref))
    center_ref[...] = lax.dot_general(
        flat(q_ref), image, NT, precision=HIGH, preferred_element_type=F32
    )


def coarse_kernel(c_ref, mine1_ref, mine2_ref, got1_ref, got2_ref, own_ref, a_ref, b_ref, d_ref, r_ref):
    c = c_ref[0]

    def side(ref, count):
        return jnp.concatenate([ref[a * count : a * count + count, :] for a in range(3)], axis=1)

    one = lax.dot_general(side(mine1_ref, V), side(got1_ref, V), NT, precision=HIGH, preferred_element_type=F32) * SCALE
    two = lax.dot_general(side(mine2_ref, V), side(got2_ref, V // 2), NT, precision=HIGH, preferred_element_type=F32) * SCALE
    part = V // NC
    for d in range(NC):
        r_ref[d, 0:part, 0:V] = one[d * part : d * part + part, :]
        r_ref[d, 16 : 16 + part, 0 : V // 2] = two[d * part : d * part + part, :]
    own_ref[...] = r_ref[c]
    a_ref[...] = r_ref[c ^ 1]
    b_ref[...] = r_ref[c ^ 2]
    d_ref[...] = r_ref[c ^ 3]


def join_kernel(c_ref, center_ref, own_ref, a_ref, b_ref, d_ref, out_ref, r_ref):
    c = c_ref[0]
    part = V // NC
    for m, ref in enumerate((own_ref, a_ref, b_ref, d_ref)):
        r_ref[m] = ref[...]

    def put(place, value):
        for v in range(part):
            out_ref[place * part + v] = value[v : v + 1, :]

    for d in range(NC):
        slot = GOT[d]
        put(slot if slot < RADIUS else slot + 1, r_ref[c ^ d, 0:part, 0:V])
    for d in range(2):
        slot = SPLIT[d]
        sides = [r_ref[c ^ (d + 2 * h), 16 : 16 + part, 0 : V // 2] for h in range(2)]
        put(slot if slot < RADIUS else slot + 1, jnp.concatenate(sides, axis=1))
    for d in range(NC):

        @pl.when(c == d)
        def _():
            put(RADIUS, center_ref[d * part : d * part + part, :])


def shards(test_vectors, ell_values, ell_cols, ell_count, pivot, send_rows, recv_rows, ov_count):
    shape = pltpu.VMEM
    c = lax.axis_index("crow").astype(jnp.int32).reshape(1)
    x = jnp.transpose(test_vectors[0], (1, 0, 2)).reshape(3 * V, LANES)
    values = ell_values.reshape(9 * NB, 1, LANES)

    def pass_on(piece, m):
        return lax.ppermute(piece, "crow", [(n, n ^ m) for n in range(NC)])

    far_v = pass_on(values, 2)
    packed = pl.pallas_call(
        pack_kernel,
        out_shape=shape((PACKED, LANES), F32),
        in_specs=[smem(), smem()] + [vmem()] * 6,
        out_specs=vmem(),
        compiler_params=LIMIT,
    )(
        c,
        ov_count.reshape(SLOTS),
        x,
        ell_cols.reshape(NB, 1, LANES),
        ell_count.reshape(1, LANES),
        pivot.reshape(3, 1, LANES),
        send_rows.reshape(SLOTS, 1, OVD),
        recv_rows.reshape(SLOTS, 1, OVD),
    )
    far_p = pass_on(packed, 2)
    blocks = []
    for own, far in ((packed, far_p), (values, far_v)):
        blocks += [own, pass_on(own, 1), far, pass_on(far, 1)]
    block = (NC, 3 * V, LANES)
    y2, w, linv, s1, s2, row = pl.pallas_call(
        main_kernel,
        out_shape=(
            shape(block, F32),
            shape(block, F32),
            shape((V, V), F32),
            shape((3 * V, LANES), F32),
            shape((3 * V // 2, LANES), F32),
            shape((8, LANES), F32),
        ),
        in_specs=[smem()] + [vmem()] * 8,
        out_specs=(vmem(),) * 6,
        scratch_shapes=[
            pltpu.VMEM(block, F32),
            pltpu.VMEM(block, F32),
            pltpu.VMEM((V + 8, LANES), F32),
            pltpu.VMEM((CHOL, V + 8, LANES), F32),
            pltpu.VMEM((2, 3 * V, LANES), F32),
            pltpu.VMEM((6 * V, NC * LANES), BF16),
            pltpu.VMEM((2, ONE, NC * LANES, 2 * LANES), BF16),
            pltpu.VMEM((2, 2, 3 * V, 2 * LANES), F32),
            pltpu.VMEM((NC, 32, LANES), F32),
        ],
        compiler_params=LIMIT,
    )(c, *map(near, blocks))

    size = lax.axis_size("sub")

    def across(piece, slots, turn):
        pairs = []
        for j in range(size):
            for n in range(NC):
                i = (j - OFFSETS[slots[n]]) % size
                pairs.append((j * NC + n, i * NC + (n ^ turn)))
        return lax.ppermute(piece, ("sub", "crow"), pairs)

    got1 = across(s1, SENT, 2)
    got2 = across(s2, SPLIT, 0)
    basis, mine1, mine2, center = pl.pallas_call(
        middle_kernel,
        out_shape=(
            jax.ShapeDtypeStruct((3 * V, LANES), F32),
            shape((3 * V, LANES), F32),
            shape((3 * V, LANES), F32),
            shape((V, V), F32),
        ),
        in_specs=[smem()] + [vmem()] * 4,
        out_specs=(vmem(),) * 4,
        scratch_shapes=[pltpu.VMEM(block, F32)],
        compiler_params=LIMIT,
    )(c, *map(near, (row, y2, w, linv)))
    slab = shape((32, LANES), F32)
    own, to1, to2, to3 = pl.pallas_call(
        coarse_kernel,
        out_shape=(slab,) * 4,
        in_specs=[smem()] + [vmem()] * 4,
        out_specs=(vmem(),) * 4,
        scratch_shapes=[pltpu.VMEM((NC, 32, LANES), F32)],
        compiler_params=LIMIT,
    )(c, *map(near, (mine1, mine2, got1, got2)))
    got = [pass_on(t, m) for m, t in ((1, to1), (2, to2), (3, to3))]
    coarse = pl.pallas_call(
        join_kernel,
        out_shape=jax.ShapeDtypeStruct(((2 * RADIUS + 1) * (V // NC), 1, V), F32),
        in_specs=[smem()] + [vmem()] * 5,
        out_specs=vmem(),
        scratch_shapes=[pltpu.VMEM((NC, 32, LANES), F32)],
        compiler_params=LIMIT,
    )(c, *map(near, (center, own, *got)))
    coarse = coarse.reshape(2 * RADIUS + 1, V // NC, V)
    basis = jnp.transpose(basis.reshape(3, V, LANES), (1, 0, 2))
    return basis[None], coarse[None]


def solution(mesh):
    placed = (
        P("sub", None, None, "crow"),
        P("sub", None, None, "crow"),
        P("sub", None, "crow"),
        P("sub", "crow"),
        P("sub", None, "crow"),
        P("sub", None, "crow"),
        P("sub", None, "crow"),
        P("sub", None, "crow"),
    )
    return jax.shard_map(
        shards,
        mesh=mesh,
        in_specs=placed,
        out_specs=(P("sub", None, None, "crow"), P("sub", None, "crow", None)),
        check_vma=False,
    )
```

```python
import jax
import jax.numpy as jnp
from jax import lax
from jax.experimental import pallas as pl
from jax.experimental.pallas import tpu as pltpu
from jax.sharding import PartitionSpec as P

RADIUS = 3
SLOTS = 2 * RADIUS
V = 48
LANES = 128
NB = 27
NC = 4
OVD = 32
SCALE = float(LANES * NC // OVD)
TILES = V // 8

COL0 = 3 * V
PIV0 = COL0 + NB
SEND0 = PIV0 + 3
RECV0 = SEND0 + SLOTS
LIVE0 = RECV0 + SLOTS
PACKED = LIVE0 + SLOTS

OFFSETS = [o - RADIUS if o < RADIUS else o - RADIUS + 1 for o in range(SLOTS)]
SENT = [0, 2, 5, 3]
GOT = [SENT[c ^ 2] for c in range(NC)]
SPLIT = [1, 1, 4, 4]
HIGH = lax.Precision.HIGHEST
F32 = jnp.float32


def vmem():
    return pl.BlockSpec(memory_space=pltpu.VMEM)


def smem():
    return pl.BlockSpec(memory_space=pltpu.SMEM)


LIMIT = pltpu.CompilerParams(vmem_limit_bytes=40 * 2**20)


def near(array):
    return pltpu.with_memory_space_constraint(array, pltpu.VMEM)


class Blocks:
    def __init__(self, refs):
        self.refs = refs

    def __getitem__(self, at):
        return self.refs[at[0]][at[1:]]


def pack_kernel(c_ref, ov_ref, x_ref, col_ref, cnt_ref, piv_ref, send_ref, recv_ref, out_ref):
    out_ref[0 : 3 * V, :] = x_ref[...]
    count = cnt_ref[...]
    for k in range(NB):
        out_ref[COL0 + k : COL0 + k + 1, :] = jnp.where(k < count, col_ref[k].astype(F32), -1.0)
    for a in range(3):
        out_ref[PIV0 + a : PIV0 + a + 1, :] = piv_ref[a]
    lane = lax.broadcasted_iota(jnp.int32, (1, LANES), 1)
    c = c_ref[0]
    here = (lane // OVD) == c
    for o in range(SLOTS):
        for ref, base in ((send_ref, SEND0), (recv_ref, RECV0)):
            piece = ref[o].astype(F32)
            row = jnp.concatenate([piece] * NC, axis=1)
            out_ref[base + o : base + o + 1, :] = jnp.where(here, row, 0.0)
        alive = here & ((lane % OVD) < ov_ref[o])
        out_ref[LIVE0 + o : LIVE0 + o + 1, :] = jnp.where(alive, 1.0, 0.0).astype(F32)


def entry(table, c):
    value = jnp.int32(table[0])
    for n in range(1, NC):
        value = jnp.where(c == n, table[n], value)
    return value


def wide(row):
    return jnp.broadcast_to(row, (8, LANES))


def lanes_of(block, index):
    return jnp.take_along_axis(block, index, axis=1)


def start_op(small_ref, src_ref, dst_ref):
    for q in range(NC):
        for a in range(3):
            piv = wide(small_ref[q, PIV0 + a : PIV0 + a + 1, :])
            for t in range(TILES):
                rows = slice(a * V + 8 * t, a * V + 8 * t + 8)
                dst_ref[q, rows, :] = piv * src_ref[q, rows, :]


ONE = 18
BF16 = jnp.bfloat16


def value_row(val_ref, rc, ab, k):
    return wide(val_ref[rc, ab * NB + k, :, :])


def add_block(val, dst_ref, rc, pick_of):
    for t in range(TILES):
        pick = [pick_of(b, t) for b in range(3)]
        for a in range(3):
            at = slice(a * V + 8 * t, a * V + 8 * t + 8)
            dst_ref[rc, at, :] = dst_ref[rc, at, :] + (
                val[3 * a] * pick[0] + val[3 * a + 1] * pick[1] + val[3 * a + 2] * pick[2]
            )


def lane_block(val_ref, cols_ref, src_ref, dst_ref, rc, k):
    col = wide(cols_ref[rc, pl.ds(k, 1), :]).astype(jnp.int32)
    val = [jnp.where(col >= 0, value_row(val_ref, rc, ab, k), 0.0) for ab in range(9)]
    index = col & (LANES - 1)
    odd = (col & LANES) != 0
    top = col >= 2 * LANES

    def pick_of(b, t):
        got = [lanes_of(src_ref[q, b * V + 8 * t : b * V + 8 * t + 8, :], index) for q in range(NC)]
        return jnp.where(top, jnp.where(odd, got[3], got[2]), jnp.where(odd, got[1], got[0]))

    add_block(val, dst_ref, rc, pick_of)


def one_hot(cols_ref, oh_ref, k):
    half = 2 * LANES
    place = lax.broadcasted_iota(jnp.int32, (half, half), 0).astype(F32).astype(BF16)
    for m in range(2):
        col = jnp.concatenate([cols_ref[2 * m + n, pl.ds(k, 1), :] for n in range(2)], axis=1)
        for h in range(2):
            local = col - float(h * half)
            local = jnp.where((local >= 0.0) & (local < float(half)), local, -1.0)
            target = jnp.concatenate([jnp.broadcast_to(local, (16, half)).astype(BF16)] * (half // 16), axis=0)
            oh_ref[m, k, h * half : h * half + half, :] = jnp.where(
                place == target, jnp.ones((), BF16), jnp.zeros((), BF16)
            )


def split_to(x_ref, src_ref):
    for q in range(NC):
        at = slice(q * LANES, q * LANES + LANES)
        value = src_ref[q, 0 : 3 * V, :]
        x_ref[0 : 3 * V, at], x_ref[3 * V :, at] = halves(value)


def issue(x_ref, oh_ref, t_ref, k, parity):
    for m in range(2):
        got = jnp.dot(x_ref[...], oh_ref[m, k], preferred_element_type=F32)
        t_ref[parity, m] = got[: 3 * V, :] + got[3 * V :, :]


def take(val_ref, dst_ref, t_ref, k, parity):
    for m in range(2):
        for n in range(2):
            at = slice(n * LANES, n * LANES + LANES)
            rc = 2 * m + n
            val = [value_row(val_ref, rc, ab, k) for ab in range(9)]
            add_block(val, dst_ref, rc, lambda b, t: t_ref[parity, m, b * V + 8 * t : b * V + 8 * t + 8, at])


def flat(ref):
    return jnp.concatenate([ref[q, a * V : a * V + V, :] for a in range(3) for q in range(NC)], axis=1)


NT = (((1,), (1,)), ((), ()))


def gram_to(m_ref, x_ref):
    total = jnp.zeros((2 * V, V), F32)
    for b in range(3):
        high = x_ref[b * V : b * V + V, :]
        both = jnp.concatenate([high, x_ref[(3 + b) * V : (4 + b) * V, :]], axis=0)
        total = total + lax.dot_general(both, high, NT, preferred_element_type=F32)
    low = total[V:, :]
    gram = total[:V, :] + low + low.T
    row = lax.broadcasted_iota(jnp.int32, (V, 64), 0)
    lane = lax.broadcasted_iota(jnp.int32, (V, 64), 1)
    eye = jnp.where(row == lane, 1.0, 0.0).astype(F32)
    m_ref[:V, :] = jnp.concatenate([eye, gram, jnp.zeros((V, LANES - 64 - V), F32)], axis=1)


def halves(value):
    high = value.astype(BF16)
    return high, (value - high.astype(F32)).astype(BF16)


def mix(linv, value):
    left, left_low = halves(linv)
    right, right_low = halves(value)
    return jnp.dot(
        jnp.concatenate([left, left, left_low], axis=1),
        jnp.concatenate([right, right_low, right], axis=0),
        preferred_element_type=F32,
    )


CHOL = 3
UN = 6


def factor_piece(m_ref, col_ref, j):
    sub = lax.broadcasted_iota(jnp.int32, (8, LANES), 0)
    m = [m_ref[8 * t : 8 * t + 8, :] for t in range(TILES)]
    cols = []
    for s in range(CHOL):
        index = jnp.full((8, LANES), 64 + s, jnp.int32) + j
        cols.append([lanes_of(m[t], index) for t in range(TILES)])
        for t in range(TILES):
            col_ref[s, 8 * t : 8 * t + 8, :] = cols[s][t]
    for s in range(CHOL):
        row = wide(m_ref[pl.ds(j + s, 1), :])
        head = {n: wide(col_ref[n, pl.ds(j + s, 1), :]) for n in range(s, CHOL)}
        inverse = 1.0 / head[s]
        for t in range(TILES):
            factor = jnp.where(sub + 8 * t > j + s, cols[s][t] * inverse, 0.0)
            m[t] = m[t] - factor * row
            m_ref[8 * t : 8 * t + 8, :] = m[t]
            for n in range(s + 1, CHOL):
                cols[n][t] = cols[n][t] - factor * head[n]
                col_ref[n, 8 * t : 8 * t + 8, :] = cols[n][t]


def inverse_of(m_ref):
    m = m_ref[:V, :]
    row = lax.broadcasted_iota(jnp.int32, (V, LANES), 0)
    lane = lax.broadcasted_iota(jnp.int32, (V, LANES), 1)
    diag = jnp.sum(jnp.where(lane == row + 64, m, 0.0), axis=1, keepdims=True)
    return m[:, :V] / jnp.sqrt(diag)


def solve_to(dst_ref, linv, src_ref):
    out = mix(linv, flat(src_ref))
    for a in range(3):
        for q in range(NC):
            at = (a * NC + q) * LANES
            dst_ref[q, a * V : a * V + V, :] = out[:, at : at + LANES]


def rows_of(src_ref, index, tiles, c):
    block = (lax.broadcasted_iota(jnp.int32, (8, LANES), 1) // OVD) ^ c
    out = []
    for at in tiles:
        pick = lanes_of(src_ref[NC - 1, at, :], index)
        for q in range(NC - 1):
            pick = jnp.where(block == q, lanes_of(src_ref[q, at, :], index), pick)
        out.append(pick)
    return out


def index_row(small_ref, row):
    total = small_ref[0, pl.ds(row, 1), :]
    for q in range(1, NC):
        total = total + small_ref[q, pl.ds(row, 1), :]
    return total


def main_kernel(
    c_ref, p0, p1, p2, p3, v0, v1, v2, v3,
    y2_ref, w_ref, linv_ref, s1_ref, s2_ref, row_ref,
    y_ref, z_ref, m_ref, col_ref, g_ref, x_ref, oh_ref, t_ref, cols_ref,
):
    c = c_ref[0]
    small_ref = Blocks((p0, p1, p2, p3))
    val_ref = Blocks((v0, v1, v2, v3))
    for m in range(NC):
        col = small_ref[m, COL0 : COL0 + NB, :]
        local = (col.astype(jnp.int32) ^ (c * LANES)).astype(F32)
        cols_ref[m, 0:NB, :] = jnp.where(col < 0.0, -1.0, local)
    m_ref[V:, :] = jnp.zeros((8, LANES), F32)

    def loop(src_ref, dst_ref, first):
        split_to(x_ref, src_ref)
        if first:
            one_hot(cols_ref, oh_ref, 0)
            one_hot(cols_ref, oh_ref, 1)
        else:
            gram_to(m_ref, x_ref)
        start_op(small_ref, src_ref, dst_ref)
        issue(x_ref, oh_ref, t_ref, 0, 0)

        def step(it, carry):
            for u in range(UN):
                k = UN * it + u
                issue(x_ref, oh_ref, t_ref, jnp.minimum(k + 1, ONE - 1), (u + 1) % 2)
                for rc in (2 * (u % 2), 2 * (u % 2) + 1):
                    lane_block(val_ref, cols_ref, src_ref, dst_ref, rc, ONE + (UN // 2) * it + u // 2)
                if first:
                    one_hot(cols_ref, oh_ref, jnp.minimum(k + 2, ONE - 1))
                else:
                    factor_piece(m_ref, col_ref, k * CHOL)
                take(val_ref, dst_ref, t_ref, k, u % 2)
            return carry

        lax.fori_loop(0, ONE // UN, step, 0)

    loop(small_ref, y_ref, True)
    loop(y_ref, z_ref, False)
    solve_to(y2_ref, inverse_of(m_ref), z_ref)
    loop(y2_ref, w_ref, False)
    linv = inverse_of(m_ref)
    linv_ref[...] = linv
    first = wide(index_row(small_ref, SEND0 + entry(SENT, c))).astype(jnp.int32)
    second = wide(index_row(small_ref, SEND0 + entry(SPLIT, c))).astype(jnp.int32)
    half = (c % 2) * (V // 2)
    for n, slot in enumerate((entry(GOT, c), entry(SPLIT, c))):
        row_ref[2 * n : 2 * n + 1, :] = index_row(small_ref, RECV0 + slot)
        row_ref[2 * n + 1 : 2 * n + 2, :] = index_row(small_ref, LIVE0 + slot)
    tiles = [slice(8 * t, 8 * t + 8) for t in range(3 * TILES)]
    for n, index in enumerate((first, second)):
        for at, piece in zip(tiles, rows_of(w_ref, index, tiles, c)):
            g_ref[n, at, :] = piece
    both = jnp.concatenate([g_ref[n, a * V : a * V + V, :] for n in range(2) for a in range(3)], axis=1)
    image = mix(linv, both)
    for a in range(3):
        s1_ref[a * V : a * V + V, :] = image[:, a * LANES : a * LANES + LANES]
        g_ref[1, a * V : a * V + V, :] = image[:, (3 + a) * LANES : (4 + a) * LANES]
        s2_ref[a * (V // 2) : (a + 1) * (V // 2), :] = g_ref[1, pl.ds(pl.multiple_of(a * V + half, 8), V // 2), :]


def middle_kernel(c_ref, row_ref, y2_ref, w_ref, linv_ref, basis_ref, mine1_ref, mine2_ref, center_ref, q_ref):
    c = c_ref[0]
    linv = linv_ref[...]
    solve_to(q_ref, linv, y2_ref)
    basis_ref[...] = q_ref[0]
    tiles = [slice(8 * t, 8 * t + 8) for t in range(3 * TILES)]
    for n, out_ref in enumerate((mine1_ref, mine2_ref)):
        index = wide(row_ref[2 * n : 2 * n + 1, :]).astype(jnp.int32)
        live = wide(row_ref[2 * n + 1 : 2 * n + 2, :])
        for at, piece in zip(tiles, rows_of(q_ref, index, tiles, c)):
            out_ref[at, :] = piece * live
    image = mix(linv, flat(w_ref))
    center_ref[...] = lax.dot_general(
        flat(q_ref), image, NT, precision=HIGH, preferred_element_type=F32
    )


def coarse_kernel(c_ref, mine1_ref, mine2_ref, got1_ref, got2_ref, own_ref, a_ref, far_ref, r_ref):
    c = c_ref[0]

    def side(ref, count):
        return jnp.concatenate([ref[a * count : a * count + count, :] for a in range(3)], axis=1)

    one = lax.dot_general(side(mine1_ref, V), side(got1_ref, V), NT, precision=HIGH, preferred_element_type=F32) * SCALE
    two = lax.dot_general(side(mine2_ref, V), side(got2_ref, V // 2), NT, precision=HIGH, preferred_element_type=F32) * SCALE
    part = V // NC
    for d in range(NC):
        r_ref[d, 0:part, 0:V] = one[d * part : d * part + part, :]
        r_ref[d, 16 : 16 + part, 0 : V // 2] = two[d * part : d * part + part, :]
    own_ref[...] = r_ref[c]
    a_ref[...] = r_ref[c ^ 1]
    far_ref[0] = r_ref[c ^ 2]
    far_ref[1] = r_ref[c ^ 3]


def join_kernel(c_ref, center_ref, own_ref, a_ref, far_ref, on_ref, out_ref, r_ref):
    c = c_ref[0]
    part = V // NC
    for m, value in enumerate((own_ref[...], a_ref[...], far_ref[0], on_ref[1])):
        r_ref[m] = value

    def put(place, value):
        for v in range(part):
            out_ref[place * part + v] = value[v : v + 1, :]

    for d in range(NC):
        slot = GOT[d]
        put(slot if slot < RADIUS else slot + 1, r_ref[c ^ d, 0:part, 0:V])
    for d in (0, 2):
        slot = SPLIT[d]
        sides = [r_ref[c ^ (d + h), 16 : 16 + part, 0 : V // 2] for h in range(2)]
        put(slot if slot < RADIUS else slot + 1, jnp.concatenate(sides, axis=1))
    for d in range(NC):

        @pl.when(c == d)
        def _():
            put(RADIUS, center_ref[d * part : d * part + part, :])


def shards(test_vectors, ell_values, ell_cols, ell_count, pivot, send_rows, recv_rows, ov_count):
    shape = pltpu.VMEM
    c = lax.axis_index("crow").astype(jnp.int32).reshape(1)
    x = jnp.transpose(test_vectors[0], (1, 0, 2)).reshape(3 * V, LANES)
    values = ell_values.reshape(9 * NB, 1, LANES)

    def pass_on(piece, m):
        return lax.ppermute(piece, "crow", [(n, n ^ m) for n in range(NC)])

    far_v = pass_on(values, 2)
    packed = pl.pallas_call(
        pack_kernel,
        out_shape=shape((PACKED, LANES), F32),
        in_specs=[smem(), smem()] + [vmem()] * 6,
        out_specs=vmem(),
    )(
        c,
        ov_count.reshape(SLOTS),
        x,
        ell_cols.reshape(NB, 1, LANES),
        ell_count.reshape(1, LANES),
        pivot.reshape(3, 1, LANES),
        send_rows.reshape(SLOTS, 1, OVD),
        recv_rows.reshape(SLOTS, 1, OVD),
    )
    far_p = pass_on(packed, 2)
    blocks = []
    for own, far in ((packed, far_p), (values, far_v)):
        blocks += [own, pass_on(own, 1), far, pass_on(far, 1)]
    block = (NC, 3 * V, LANES)
    y2, w, linv, s1, s2, row = pl.pallas_call(
        main_kernel,
        out_shape=(
            shape(block, F32),
            shape(block, F32),
            shape((V, V), F32),
            shape((3 * V, LANES), F32),
            shape((3 * V // 2, LANES), F32),
            shape((8, LANES), F32),
        ),
        in_specs=[smem()] + [vmem()] * 8,
        out_specs=(vmem(),) * 6,
        scratch_shapes=[
            pltpu.VMEM(block, F32),
            pltpu.VMEM(block, F32),
            pltpu.VMEM((V + 8, LANES), F32),
            pltpu.VMEM((CHOL, V + 8, LANES), F32),
            pltpu.VMEM((2, 3 * V, LANES), F32),
            pltpu.VMEM((6 * V, NC * LANES), BF16),
            pltpu.VMEM((2, ONE, NC * LANES, 2 * LANES), BF16),
            pltpu.VMEM((2, 2, 3 * V, 2 * LANES), F32),
            pltpu.VMEM((NC, 32, LANES), F32),
        ],
        compiler_params=LIMIT,
    )(c, *map(near, blocks))

    size = lax.axis_size("sub")

    def across(piece, slots, turn):
        pairs = []
        for j in range(size):
            for n in range(NC):
                i = (j - OFFSETS[slots[n]]) % size
                pairs.append((j * NC + n, i * NC + (n ^ turn)))
        return lax.ppermute(piece, ("sub", "crow"), pairs)

    got1 = across(s1, SENT, 2)
    got2 = across(s2, SPLIT, 0)
    basis, mine1, mine2, center = pl.pallas_call(
        middle_kernel,
        out_shape=(
            jax.ShapeDtypeStruct((3 * V, LANES), F32),
            shape((3 * V, LANES), F32),
            shape((3 * V, LANES), F32),
            shape((V, V), F32),
        ),
        in_specs=[smem()] + [vmem()] * 4,
        out_specs=(vmem(),) * 4,
        scratch_shapes=[pltpu.VMEM(block, F32)],
        compiler_params=LIMIT,
    )(c, *map(near, (row, y2, w, linv)))
    own, to1, to2 = pl.pallas_call(
        coarse_kernel,
        out_shape=(shape((32, LANES), F32), shape((32, LANES), F32), shape((2, 32, LANES), F32)),
        in_specs=[smem()] + [vmem()] * 4,
        out_specs=(vmem(),) * 3,
        scratch_shapes=[pltpu.VMEM((NC, 32, LANES), F32)],
        compiler_params=LIMIT,
    )(c, *map(near, (mine1, mine2, got1, got2)))
    far = pass_on(to2, 2)
    got = (pass_on(to1, 1), far, pass_on(far, 1))
    coarse = pl.pallas_call(
        join_kernel,
        out_shape=jax.ShapeDtypeStruct(((2 * RADIUS + 1) * (V // NC), 1, V), F32),
        in_specs=[smem()] + [vmem()] * 5,
        out_specs=vmem(),
        scratch_shapes=[pltpu.VMEM((NC, 32, LANES), F32)],
        compiler_params=LIMIT,
    )(c, *map(near, (center, own, *got)))
    coarse = coarse.reshape(2 * RADIUS + 1, V // NC, V)
    basis = jnp.transpose(basis.reshape(3, V, LANES), (1, 0, 2))
    return basis[None], coarse[None]


def solution(mesh):
    placed = (
        P("sub", None, None, "crow"),
        P("sub", None, None, "crow"),
        P("sub", None, "crow"),
        P("sub", "crow"),
        P("sub", None, "crow"),
        P("sub", None, "crow"),
        P("sub", None, "crow"),
        P("sub", None, "crow"),
    )
    return jax.shard_map(
        shards,
        mesh=mesh,
        in_specs=placed,
        out_specs=(P("sub", None, None, "crow"), P("sub", None, "crow", None)),
        check_vma=False,
    )
```

```python
import jax
import jax.numpy as jnp
from jax import lax
from jax.experimental import pallas as pl
from jax.experimental.pallas import tpu as pltpu
from jax.sharding import PartitionSpec as P

RADIUS = 3
SLOTS = 2 * RADIUS
V = 48
LANES = 128
NB = 27
NC = 4
OVD = 32
SCALE = float(LANES * NC // OVD)
TILES = V // 8

COL0 = 3 * V
PIV0 = COL0 + NB
SEND0 = PIV0 + 3
RECV0 = SEND0 + SLOTS
LIVE0 = RECV0 + SLOTS
PACKED = LIVE0 + SLOTS

OFFSETS = [o - RADIUS if o < RADIUS else o - RADIUS + 1 for o in range(SLOTS)]
SENT = [0, 2, 5, 3]
GOT = [SENT[c ^ 2] for c in range(NC)]
SPLIT = [1, 1, 4, 4]
HIGH = lax.Precision.HIGHEST
F32 = jnp.float32


def vmem():
    return pl.BlockSpec(memory_space=pltpu.VMEM)


def smem():
    return pl.BlockSpec(memory_space=pltpu.SMEM)


LIMIT = pltpu.CompilerParams(vmem_limit_bytes=40 * 2**20)


def near(array):
    return pltpu.with_memory_space_constraint(array, pltpu.VMEM)


class Blocks:
    def __init__(self, refs):
        self.refs = refs

    def __getitem__(self, at):
        return self.refs[at[0]][at[1:]]


def pack_kernel(c_ref, ov_ref, x_ref, col_ref, cnt_ref, piv_ref, send_ref, recv_ref, out_ref):
    out_ref[0 : 3 * V, :] = x_ref[...]
    count = cnt_ref[...]
    for k in range(NB):
        out_ref[COL0 + k : COL0 + k + 1, :] = jnp.where(k < count, col_ref[k].astype(F32), -1.0)
    for a in range(3):
        out_ref[PIV0 + a : PIV0 + a + 1, :] = piv_ref[a]
    lane = lax.broadcasted_iota(jnp.int32, (1, LANES), 1)
    c = c_ref[0]
    here = (lane // OVD) == c
    for o in range(SLOTS):
        for ref, base in ((send_ref, SEND0), (recv_ref, RECV0)):
            piece = ref[o].astype(F32)
            row = jnp.concatenate([piece] * NC, axis=1)
            out_ref[base + o : base + o + 1, :] = jnp.where(here, row, 0.0)
        alive = here & ((lane % OVD) < ov_ref[o])
        out_ref[LIVE0 + o : LIVE0 + o + 1, :] = jnp.where(alive, 1.0, 0.0).astype(F32)


def entry(table, c):
    value = jnp.int32(table[0])
    for n in range(1, NC):
        value = jnp.where(c == n, table[n], value)
    return value


def wide(row):
    return jnp.broadcast_to(row, (8, LANES))


def lanes_of(block, index):
    return jnp.take_along_axis(block, index, axis=1)


def start_op(small_ref, src_ref, dst_ref):
    for q in range(NC):
        for a in range(3):
            piv = wide(small_ref[q, PIV0 + a : PIV0 + a + 1, :])
            for t in range(TILES):
                rows = slice(a * V + 8 * t, a * V + 8 * t + 8)
                dst_ref[q, rows, :] = piv * src_ref[q, rows, :]


ONE = 16
REST = 12
BF16 = jnp.bfloat16


def value_row(val_ref, rc, ab, k):
    return wide(val_ref[rc, ab * NB + k, :, :])


def add_block(val, dst_ref, rc, pick_of):
    for t in range(TILES):
        pick = [pick_of(b, t) for b in range(3)]
        for a in range(3):
            at = slice(a * V + 8 * t, a * V + 8 * t + 8)
            dst_ref[rc, at, :] = dst_ref[rc, at, :] + (
                val[3 * a] * pick[0] + val[3 * a + 1] * pick[1] + val[3 * a + 2] * pick[2]
            )


def pack_pairs(src_ref, scale_ref, pair_ref):
    inverse = []
    for t in range(TILES):
        top = None
        for q in range(NC):
            for b in range(3):
                size = jnp.abs(src_ref[q, b * V + 8 * t : b * V + 8 * t + 8, :])
                top = size if top is None else jnp.maximum(top, size)
        top = jnp.broadcast_to(jnp.maximum(jnp.max(top, axis=1, keepdims=True), 1e-30), (8, LANES))
        scale_ref[8 * t : 8 * t + 8, :] = top * (1.0 / 32767.0)
        inverse.append(32767.0 / top)
    for q in range(NC):
        for b in range(3):
            for p in range(TILES // 2):
                whole = [
                    jnp.round(src_ref[q, b * V + 8 * t : b * V + 8 * t + 8, :] * inverse[t]).astype(jnp.int32)
                    for t in (2 * p, 2 * p + 1)
                ]
                at = 8 * (b * (TILES // 2) + p)
                pair_ref[q, at : at + 8, :] = (whole[0] << 16) | (whole[1] & 65535)


def lane_blocks(val_ref, cols_ref, pair_ref, sum_ref, rc, ks):
    blocks = []
    for k in ks:
        col = wide(cols_ref[rc, pl.ds(k, 1), :]).astype(jnp.int32)
        real = jnp.minimum(k, NB - 1)
        val = [jnp.where(col >= 0, value_row(val_ref, rc, ab, real), 0.0) for ab in range(9)]
        blocks.append((val, col & (LANES - 1), (col & LANES) != 0, col >= 2 * LANES))
    for p in range(TILES // 2):
        rows = [[slice(a * V + 8 * t, a * V + 8 * t + 8) for t in (2 * p, 2 * p + 1)] for a in range(3)]
        total = [[sum_ref[rc, at, :] for at in pair] for pair in rows]
        for val, index, odd, top in blocks:
            for b in range(3):
                at = 8 * (b * (TILES // 2) + p)
                got = [lanes_of(pair_ref[q, at : at + 8, :], index) for q in range(NC)]
                both = jnp.where(top, jnp.where(odd, got[3], got[2]), jnp.where(odd, got[1], got[0]))
                pick = ((both >> 16).astype(F32), ((both << 16) >> 16).astype(F32))
                for a in range(3):
                    for n in range(2):
                        total[a][n] = total[a][n] + val[3 * a + b] * pick[n]
        for a in range(3):
            for n in range(2):
                sum_ref[rc, rows[a][n], :] = total[a][n]


def one_hot(cols_ref, oh_ref, k):
    half = 2 * LANES
    place = lax.broadcasted_iota(jnp.int32, (half, half), 0).astype(F32).astype(BF16)
    for m in range(2):
        col = jnp.concatenate([cols_ref[2 * m + n, pl.ds(k, 1), :] for n in range(2)], axis=1)
        for h in range(2):
            local = col - float(h * half)
            local = jnp.where((local >= 0.0) & (local < float(half)), local, -1.0)
            target = jnp.concatenate([jnp.broadcast_to(local, (16, half)).astype(BF16)] * (half // 16), axis=0)
            oh_ref[m, k, h * half : h * half + half, :] = jnp.where(
                place == target, jnp.ones((), BF16), jnp.zeros((), BF16)
            )


def split_to(x_ref, src_ref):
    for q in range(NC):
        at = slice(q * LANES, q * LANES + LANES)
        value = src_ref[q, 0 : 3 * V, :]
        x_ref[0 : 3 * V, at], x_ref[3 * V :, at] = halves(value)


def issue(x_ref, oh_ref, t_ref, k, parity):
    for m in range(2):
        got = jnp.dot(x_ref[...], oh_ref[m, k], preferred_element_type=F32)
        t_ref[parity, m] = got[: 3 * V, :] + got[3 * V :, :]


def take(val_ref, dst_ref, t_ref, k, parity):
    for m in range(2):
        for n in range(2):
            at = slice(n * LANES, n * LANES + LANES)
            rc = 2 * m + n
            val = [value_row(val_ref, rc, ab, k) for ab in range(9)]
            add_block(val, dst_ref, rc, lambda b, t: t_ref[parity, m, b * V + 8 * t : b * V + 8 * t + 8, at])


def flat(ref):
    return jnp.concatenate([ref[q, a * V : a * V + V, :] for a in range(3) for q in range(NC)], axis=1)


NT = (((1,), (1,)), ((), ()))


def gram_to(m_ref, x_ref):
    total = jnp.zeros((2 * V, V), F32)
    for b in range(3):
        high = x_ref[b * V : b * V + V, :]
        both = jnp.concatenate([high, x_ref[(3 + b) * V : (4 + b) * V, :]], axis=0)
        total = total + lax.dot_general(both, high, NT, preferred_element_type=F32)
    low = total[V:, :]
    gram = total[:V, :] + low + low.T
    row = lax.broadcasted_iota(jnp.int32, (V, 64), 0)
    lane = lax.broadcasted_iota(jnp.int32, (V, 64), 1)
    eye = jnp.where(row == lane, 1.0, 0.0).astype(F32)
    m_ref[:V, :] = jnp.concatenate([eye, gram, jnp.zeros((V, LANES - 64 - V), F32)], axis=1)


def halves(value):
    high = value.astype(BF16)
    return high, (value - high.astype(F32)).astype(BF16)


def mix(linv, value):
    left, left_low = halves(linv)
    right, right_low = halves(value)
    return jnp.dot(
        jnp.concatenate([left, left, left_low], axis=1),
        jnp.concatenate([right, right_low, right], axis=0),
        preferred_element_type=F32,
    )


CHOL = 3
UN = 8


def factor_piece(m_ref, col_ref, j):
    sub = lax.broadcasted_iota(jnp.int32, (8, LANES), 0)
    m = [m_ref[8 * t : 8 * t + 8, :] for t in range(TILES)]
    cols = []
    for s in range(CHOL):
        index = jnp.full((8, LANES), 64 + s, jnp.int32) + j
        cols.append([lanes_of(m[t], index) for t in range(TILES)])
        for t in range(TILES):
            col_ref[s, 8 * t : 8 * t + 8, :] = cols[s][t]
    for s in range(CHOL):
        row = wide(m_ref[pl.ds(j + s, 1), :])
        head = {n: wide(col_ref[n, pl.ds(j + s, 1), :]) for n in range(s, CHOL)}
        inverse = 1.0 / head[s]
        for t in range(TILES):
            factor = jnp.where(sub + 8 * t > j + s, cols[s][t] * inverse, 0.0)
            m[t] = m[t] - factor * row
            m_ref[8 * t : 8 * t + 8, :] = m[t]
            for n in range(s + 1, CHOL):
                cols[n][t] = cols[n][t] - factor * head[n]
                col_ref[n, 8 * t : 8 * t + 8, :] = cols[n][t]


def inverse_of(m_ref):
    m = m_ref[:V, :]
    row = lax.broadcasted_iota(jnp.int32, (V, LANES), 0)
    lane = lax.broadcasted_iota(jnp.int32, (V, LANES), 1)
    diag = jnp.sum(jnp.where(lane == row + 64, m, 0.0), axis=1, keepdims=True)
    return m[:, :V] / jnp.sqrt(diag)


def solve_to(dst_ref, linv, src_ref):
    out = mix(linv, flat(src_ref))
    for a in range(3):
        for q in range(NC):
            at = (a * NC + q) * LANES
            dst_ref[q, a * V : a * V + V, :] = out[:, at : at + LANES]


def rows_of(src_ref, index, tiles, c):
    block = (lax.broadcasted_iota(jnp.int32, (8, LANES), 1) // OVD) ^ c
    out = []
    for at in tiles:
        pick = lanes_of(src_ref[NC - 1, at, :], index)
        for q in range(NC - 1):
            pick = jnp.where(block == q, lanes_of(src_ref[q, at, :], index), pick)
        out.append(pick)
    return out


def index_row(small_ref, row):
    total = small_ref[0, pl.ds(row, 1), :]
    for q in range(1, NC):
        total = total + small_ref[q, pl.ds(row, 1), :]
    return total


def main_kernel(
    c_ref, p0, p1, p2, p3, v0, v1, v2, v3,
    y2_ref, w_ref, linv_ref, s1_ref, s2_ref, row_ref,
    y_ref, z_ref, m_ref, col_ref, g_ref, x_ref, oh_ref, t_ref, cols_ref, pair_ref, scale_ref, sum_ref,
):
    c = c_ref[0]
    small_ref = Blocks((p0, p1, p2, p3))
    val_ref = Blocks((v0, v1, v2, v3))
    for m in range(NC):
        col = small_ref[m, COL0 : COL0 + NB, :]
        local = (col.astype(jnp.int32) ^ (c * LANES)).astype(F32)
        cols_ref[m, NB:32, :] = jnp.full((32 - NB, LANES), -1.0, F32)
        cols_ref[m, 0:NB, :] = jnp.where(col < 0.0, -1.0, local)
    m_ref[V:, :] = jnp.zeros((8, LANES), F32)

    def loop(src_ref, dst_ref, first):
        split_to(x_ref, src_ref)
        if first:
            one_hot(cols_ref, oh_ref, 0)
            one_hot(cols_ref, oh_ref, 1)
        else:
            gram_to(m_ref, x_ref)
        start_op(small_ref, src_ref, dst_ref)
        pack_pairs(src_ref, scale_ref, pair_ref)
        sum_ref[...] = jnp.zeros((NC, 3 * V, LANES), F32)
        issue(x_ref, oh_ref, t_ref, 0, 0)

        def step(it, carry):
            for u in range(UN):
                k = UN * it + u
                issue(x_ref, oh_ref, t_ref, jnp.minimum(k + 1, ONE - 1), (u + 1) % 2)
                ks = [ONE + (REST // 2) * it + 3 * (u % 2) + n for n in range(3)]
                lane_blocks(val_ref, cols_ref, pair_ref, sum_ref, u // 2, ks)
                if first:
                    one_hot(cols_ref, oh_ref, jnp.minimum(k + 2, ONE - 1))
                else:
                    factor_piece(m_ref, col_ref, k * CHOL)
                take(val_ref, dst_ref, t_ref, k, u % 2)
            return carry

        lax.fori_loop(0, ONE // UN, step, 0)
        for q in range(NC):
            for a in range(3):
                at = slice(a * V, a * V + V)
                dst_ref[q, at, :] = dst_ref[q, at, :] + sum_ref[q, at, :] * scale_ref[...]

    loop(small_ref, y_ref, True)
    loop(y_ref, z_ref, False)
    solve_to(y2_ref, inverse_of(m_ref), z_ref)
    loop(y2_ref, w_ref, False)
    linv = inverse_of(m_ref)
    linv_ref[...] = linv
    first = wide(index_row(small_ref, SEND0 + entry(SENT, c))).astype(jnp.int32)
    second = wide(index_row(small_ref, SEND0 + entry(SPLIT, c))).astype(jnp.int32)
    half = (c % 2) * (V // 2)
    for n, slot in enumerate((entry(GOT, c), entry(SPLIT, c))):
        row_ref[2 * n : 2 * n + 1, :] = index_row(small_ref, RECV0 + slot)
        row_ref[2 * n + 1 : 2 * n + 2, :] = index_row(small_ref, LIVE0 + slot)
    tiles = [slice(8 * t, 8 * t + 8) for t in range(3 * TILES)]
    for n, index in enumerate((first, second)):
        for at, piece in zip(tiles, rows_of(w_ref, index, tiles, c)):
            g_ref[n, at, :] = piece
    both = jnp.concatenate([g_ref[n, a * V : a * V + V, :] for n in range(2) for a in range(3)], axis=1)
    image = mix(linv, both)
    for a in range(3):
        s1_ref[a * V : a * V + V, :] = image[:, a * LANES : a * LANES + LANES]
        g_ref[1, a * V : a * V + V, :] = image[:, (3 + a) * LANES : (4 + a) * LANES]
        s2_ref[a * (V // 2) : (a + 1) * (V // 2), :] = g_ref[1, pl.ds(pl.multiple_of(a * V + half, 8), V // 2), :]


def middle_kernel(c_ref, row_ref, y2_ref, w_ref, linv_ref, basis_ref, mine1_ref, mine2_ref, center_ref, q_ref):
    c = c_ref[0]
    linv = linv_ref[...]
    solve_to(q_ref, linv, y2_ref)
    basis_ref[...] = q_ref[0]
    tiles = [slice(8 * t, 8 * t + 8) for t in range(3 * TILES)]
    for n, out_ref in enumerate((mine1_ref, mine2_ref)):
        index = wide(row_ref[2 * n : 2 * n + 1, :]).astype(jnp.int32)
        live = wide(row_ref[2 * n + 1 : 2 * n + 2, :])
        for at, piece in zip(tiles, rows_of(q_ref, index, tiles, c)):
            out_ref[at, :] = piece * live
    image = mix(linv, flat(w_ref))
    center_ref[...] = lax.dot_general(
        flat(q_ref), image, NT, precision=HIGH, preferred_element_type=F32
    )


def coarse_kernel(c_ref, mine1_ref, mine2_ref, got1_ref, got2_ref, near_ref, far_ref, r_ref):
    c = c_ref[0]

    def side(ref, count):
        return jnp.concatenate([ref[a * count : a * count + count, :] for a in range(3)], axis=1)

    one = lax.dot_general(side(mine1_ref, V), side(got1_ref, V), NT, precision=HIGH, preferred_element_type=F32) * SCALE
    two = lax.dot_general(side(mine2_ref, V), side(got2_ref, V // 2), NT, precision=HIGH, preferred_element_type=F32) * SCALE
    part = V // NC
    for d in range(NC):
        r_ref[d, 0:part, 0:V] = one[d * part : d * part + part, :]
        r_ref[d, 16 : 16 + part, 0 : V // 2] = two[d * part : d * part + part, :]
    near_ref[0] = r_ref[c]
    near_ref[1] = r_ref[c ^ 1]
    far_ref[0] = r_ref[c ^ 2]
    far_ref[1] = r_ref[c ^ 3]


def pair_kernel(near_ref, far_ref, out_ref):
    out_ref[0] = near_ref[1]
    out_ref[1] = far_ref[1]


def join_kernel(c_ref, center_ref, near_ref, far_ref, on_ref, out_ref, r_ref):
    c = c_ref[0]
    part = V // NC
    for m, value in enumerate((near_ref[0], on_ref[0], far_ref[0], on_ref[1])):
        r_ref[m] = value

    def put(place, value):
        for v in range(part):
            out_ref[place * part + v] = value[v : v + 1, :]

    for d in range(NC):
        slot = GOT[d]
        put(slot if slot < RADIUS else slot + 1, r_ref[c ^ d, 0:part, 0:V])
    for d in (0, 2):
        slot = SPLIT[d]
        sides = [r_ref[c ^ (d + h), 16 : 16 + part, 0 : V // 2] for h in range(2)]
        put(slot if slot < RADIUS else slot + 1, jnp.concatenate(sides, axis=1))
    for d in range(NC):

        @pl.when(c == d)
        def _():
            put(RADIUS, center_ref[d * part : d * part + part, :])


def shards(test_vectors, ell_values, ell_cols, ell_count, pivot, send_rows, recv_rows, ov_count):
    shape = pltpu.VMEM
    c = lax.axis_index("crow").astype(jnp.int32).reshape(1)
    x = jnp.transpose(test_vectors[0], (1, 0, 2)).reshape(3 * V, LANES)
    values = ell_values.reshape(9 * NB, 1, LANES)

    def pass_on(piece, m):
        return lax.ppermute(piece, "crow", [(n, n ^ m) for n in range(NC)])

    far_v = pass_on(values, 2)
    packed = pl.pallas_call(
        pack_kernel,
        out_shape=shape((PACKED, LANES), F32),
        in_specs=[smem(), smem()] + [vmem()] * 6,
        out_specs=vmem(),
    )(
        c,
        ov_count.reshape(SLOTS),
        x,
        ell_cols.reshape(NB, 1, LANES),
        ell_count.reshape(1, LANES),
        pivot.reshape(3, 1, LANES),
        send_rows.reshape(SLOTS, 1, OVD),
        recv_rows.reshape(SLOTS, 1, OVD),
    )
    far_p = pass_on(packed, 2)
    blocks = []
    for own, far in ((packed, far_p), (values, far_v)):
        blocks += [own, pass_on(own, 1), far, pass_on(far, 1)]
    block = (NC, 3 * V, LANES)
    y2, w, linv, s1, s2, row = pl.pallas_call(
        main_kernel,
        out_shape=(
            shape(block, F32),
            shape(block, F32),
            shape((V, V), F32),
            shape((3 * V, LANES), F32),
            shape((3 * V // 2, LANES), F32),
            shape((8, LANES), F32),
        ),
        in_specs=[smem()] + [vmem()] * 8,
        out_specs=(vmem(),) * 6,
        scratch_shapes=[
            pltpu.VMEM(block, F32),
            pltpu.VMEM(block, F32),
            pltpu.VMEM((V + 8, LANES), F32),
            pltpu.VMEM((CHOL, V + 8, LANES), F32),
            pltpu.VMEM((2, 3 * V, LANES), F32),
            pltpu.VMEM((6 * V, NC * LANES), BF16),
            pltpu.VMEM((2, ONE, NC * LANES, 2 * LANES), BF16),
            pltpu.VMEM((2, 2, 3 * V, 2 * LANES), F32),
            pltpu.VMEM((NC, 32, LANES), F32),
            pltpu.VMEM((NC, 3 * V // 2, LANES), jnp.int32),
            pltpu.VMEM((V, LANES), F32),
            pltpu.VMEM(block, F32),
        ],
        compiler_params=LIMIT,
    )(c, *map(near, blocks))

    size = lax.axis_size("sub")

    def across(piece, slots, turn):
        pairs = []
        for j in range(size):
            for n in range(NC):
                i = (j - OFFSETS[slots[n]]) % size
                pairs.append((j * NC + n, i * NC + (n ^ turn)))
        return lax.ppermute(piece, ("sub", "crow"), pairs)

    got1 = across(s1, SENT, 2)
    got2 = across(s2, SPLIT, 0)
    basis, mine1, mine2, center = pl.pallas_call(
        middle_kernel,
        out_shape=(
            jax.ShapeDtypeStruct((3 * V, LANES), F32),
            shape((3 * V, LANES), F32),
            shape((3 * V, LANES), F32),
            shape((V, V), F32),
        ),
        in_specs=[smem()] + [vmem()] * 4,
        out_specs=(vmem(),) * 4,
        scratch_shapes=[pltpu.VMEM(block, F32)],
        compiler_params=LIMIT,
    )(c, *map(near, (row, y2, w, linv)))
    pair = shape((2, 32, LANES), F32)
    mine, sent = pl.pallas_call(
        coarse_kernel,
        out_shape=(pair, pair),
        in_specs=[smem()] + [vmem()] * 4,
        out_specs=(vmem(),) * 2,
        scratch_shapes=[pltpu.VMEM((NC, 32, LANES), F32)],
        compiler_params=LIMIT,
    )(c, *map(near, (mine1, mine2, got1, got2)))
    far = pass_on(sent, 2)
    both = pl.pallas_call(
        pair_kernel, out_shape=pair, in_specs=[vmem()] * 2, out_specs=vmem(), compiler_params=LIMIT
    )(near(mine), near(far))
    on = pass_on(both, 1)
    coarse = pl.pallas_call(
        join_kernel,
        out_shape=jax.ShapeDtypeStruct(((2 * RADIUS + 1) * (V // NC), 1, V), F32),
        in_specs=[smem()] + [vmem()] * 4,
        out_specs=vmem(),
        scratch_shapes=[pltpu.VMEM((NC, 32, LANES), F32)],
        compiler_params=LIMIT,
    )(c, *map(near, (center, mine, far, on)))
    coarse = coarse.reshape(2 * RADIUS + 1, V // NC, V)
    basis = jnp.transpose(basis.reshape(3, V, LANES), (1, 0, 2))
    return basis[None], coarse[None]


def solution(mesh):
    placed = (
        P("sub", None, None, "crow"),
        P("sub", None, None, "crow"),
        P("sub", None, "crow"),
        P("sub", "crow"),
        P("sub", None, "crow"),
        P("sub", None, "crow"),
        P("sub", None, "crow"),
        P("sub", None, "crow"),
    )
    return jax.shard_map(
        shards,
        mesh=mesh,
        in_specs=placed,
        out_specs=(P("sub", None, None, "crow"), P("sub", None, "crow", None)),
        check_vma=False,
    )
```

```python
import jax
import jax.numpy as jnp
from jax import lax
from jax.experimental import pallas as pl
from jax.experimental.pallas import tpu as pltpu
from jax.sharding import PartitionSpec as P

RADIUS = 3
SLOTS = 2 * RADIUS
V = 48
LANES = 128
NB = 27
NC = 4
OVD = 32
SCALE = float(LANES * NC // OVD)
TILES = V // 8

COL0 = 3 * V
PIV0 = COL0 + NB
SEND0 = PIV0 + 3
RECV0 = SEND0 + SLOTS
LIVE0 = RECV0 + SLOTS
PACKED = LIVE0 + SLOTS

OFFSETS = [o - RADIUS if o < RADIUS else o - RADIUS + 1 for o in range(SLOTS)]
SENT = [0, 2, 5, 3]
GOT = [SENT[c ^ 2] for c in range(NC)]
SPLIT = [1, 1, 4, 4]
HIGH = lax.Precision.HIGHEST
F32 = jnp.float32


def vmem():
    return pl.BlockSpec(memory_space=pltpu.VMEM)


def smem():
    return pl.BlockSpec(memory_space=pltpu.SMEM)


LIMIT = pltpu.CompilerParams(vmem_limit_bytes=40 * 2**20)


def near(array):
    return pltpu.with_memory_space_constraint(array, pltpu.VMEM)


class Blocks:
    def __init__(self, refs):
        self.refs = refs

    def __getitem__(self, at):
        return self.refs[at[0]][at[1:]]


def pack_kernel(c_ref, ov_ref, x_ref, col_ref, cnt_ref, piv_ref, send_ref, recv_ref, out_ref):
    out_ref[0 : 3 * V, :] = x_ref[...]
    count = cnt_ref[...]
    for k in range(NB):
        out_ref[COL0 + k : COL0 + k + 1, :] = jnp.where(k < count, col_ref[k].astype(F32), -1.0)
    for a in range(3):
        out_ref[PIV0 + a : PIV0 + a + 1, :] = piv_ref[a]
    lane = lax.broadcasted_iota(jnp.int32, (1, LANES), 1)
    c = c_ref[0]
    here = (lane // OVD) == c
    for o in range(SLOTS):
        for ref, base in ((send_ref, SEND0), (recv_ref, RECV0)):
            piece = ref[o].astype(F32)
            row = jnp.concatenate([piece] * NC, axis=1)
            out_ref[base + o : base + o + 1, :] = jnp.where(here, row, 0.0)
        alive = here & ((lane % OVD) < ov_ref[o])
        out_ref[LIVE0 + o : LIVE0 + o + 1, :] = jnp.where(alive, 1.0, 0.0).astype(F32)


def entry(table, c):
    value = jnp.int32(table[0])
    for n in range(1, NC):
        value = jnp.where(c == n, table[n], value)
    return value


def wide(row):
    return jnp.broadcast_to(row, (8, LANES))


def lanes_of(block, index):
    return jnp.take_along_axis(block, index, axis=1)


def start_op(small_ref, src_ref, dst_ref):
    for q in range(NC):
        for a in range(3):
            piv = wide(small_ref[q, PIV0 + a : PIV0 + a + 1, :])
            for t in range(TILES):
                rows = slice(a * V + 8 * t, a * V + 8 * t + 8)
                dst_ref[q, rows, :] = piv * src_ref[q, rows, :]


ONE = 16
REST = 12
BF16 = jnp.bfloat16


def value_row(val_ref, rc, ab, k):
    return wide(val_ref[rc, ab * NB + k, :, :])


def add_block(val, dst_ref, rc, pick_of):
    for t in range(TILES):
        pick = [pick_of(b, t) for b in range(3)]
        for a in range(3):
            at = slice(a * V + 8 * t, a * V + 8 * t + 8)
            dst_ref[rc, at, :] = dst_ref[rc, at, :] + (
                val[3 * a] * pick[0] + val[3 * a + 1] * pick[1] + val[3 * a + 2] * pick[2]
            )


def pack_pairs(src_ref, scale_ref, pair_ref):
    inverse = []
    for t in range(TILES):
        top = None
        for q in range(NC):
            for b in range(3):
                size = jnp.abs(src_ref[q, b * V + 8 * t : b * V + 8 * t + 8, :])
                top = size if top is None else jnp.maximum(top, size)
        top = jnp.broadcast_to(jnp.maximum(jnp.max(top, axis=1, keepdims=True), 1e-30), (8, LANES))
        scale_ref[8 * t : 8 * t + 8, :] = top * (1.0 / 32767.0)
        inverse.append(32767.0 / top)
    for q in range(NC):
        for b in range(3):
            for p in range(TILES // 2):
                whole = [
                    jnp.round(src_ref[q, b * V + 8 * t : b * V + 8 * t + 8, :] * inverse[t]).astype(jnp.int32)
                    for t in (2 * p, 2 * p + 1)
                ]
                at = 8 * (b * (TILES // 2) + p)
                pair_ref[q, at : at + 8, :] = (whole[0] << 16) | (whole[1] & 65535)


def lane_blocks(val_ref, cols_ref, pair_ref, sum_ref, rc, ks):
    blocks = []
    for k in ks:
        col = wide(cols_ref[rc, pl.ds(k, 1), :]).astype(jnp.int32)
        real = jnp.minimum(k, NB - 1)
        val = [jnp.where(col >= 0, value_row(val_ref, rc, ab, real), 0.0) for ab in range(9)]
        blocks.append((val, col & (LANES - 1), (col & LANES) != 0, col >= 2 * LANES))
    for p in range(TILES // 2):
        rows = [[slice(a * V + 8 * t, a * V + 8 * t + 8) for t in (2 * p, 2 * p + 1)] for a in range(3)]
        total = [[sum_ref[rc, at, :] for at in pair] for pair in rows]
        for val, index, odd, top in blocks:
            for b in range(3):
                at = 8 * (b * (TILES // 2) + p)
                got = [lanes_of(pair_ref[q, at : at + 8, :], index) for q in range(NC)]
                both = jnp.where(top, jnp.where(odd, got[3], got[2]), jnp.where(odd, got[1], got[0]))
                pick = ((both >> 16).astype(F32), ((both << 16) >> 16).astype(F32))
                for a in range(3):
                    for n in range(2):
                        total[a][n] = total[a][n] + val[3 * a + b] * pick[n]
        for a in range(3):
            for n in range(2):
                sum_ref[rc, rows[a][n], :] = total[a][n]


def one_hot(cols_ref, oh_ref, k):
    half = 2 * LANES
    place = lax.broadcasted_iota(jnp.int32, (half, half), 0).astype(F32).astype(BF16)
    for m in range(2):
        col = jnp.concatenate([cols_ref[2 * m + n, pl.ds(k, 1), :] for n in range(2)], axis=1)
        for h in range(2):
            local = col - float(h * half)
            local = jnp.where((local >= 0.0) & (local < float(half)), local, -1.0)
            target = jnp.concatenate([jnp.broadcast_to(local, (16, half)).astype(BF16)] * (half // 16), axis=0)
            oh_ref[m, k, h * half : h * half + half, :] = jnp.where(
                place == target, jnp.ones((), BF16), jnp.zeros((), BF16)
            )


def split_to(x_ref, src_ref):
    for q in range(NC):
        at = slice(q * LANES, q * LANES + LANES)
        value = src_ref[q, 0 : 3 * V, :]
        x_ref[0 : 3 * V, at], x_ref[3 * V :, at] = halves(value)


def issue(x_ref, oh_ref, t_ref, k, parity):
    for m in range(2):
        got = jnp.dot(x_ref[...], oh_ref[m, k], preferred_element_type=F32)
        t_ref[parity, m] = got[: 3 * V, :] + got[3 * V :, :]


def take(val_ref, dst_ref, t_ref, k, parity):
    for m in range(2):
        for n in range(2):
            at = slice(n * LANES, n * LANES + LANES)
            rc = 2 * m + n
            val = [value_row(val_ref, rc, ab, k) for ab in range(9)]
            add_block(val, dst_ref, rc, lambda b, t: t_ref[parity, m, b * V + 8 * t : b * V + 8 * t + 8, at])


def flat(ref):
    return jnp.concatenate([ref[q, a * V : a * V + V, :] for a in range(3) for q in range(NC)], axis=1)


NT = (((1,), (1,)), ((), ()))


def gram_to(m_ref, x_ref):
    total = jnp.zeros((2 * V, V), F32)
    for b in range(3):
        high = x_ref[b * V : b * V + V, :]
        both = jnp.concatenate([high, x_ref[(3 + b) * V : (4 + b) * V, :]], axis=0)
        total = total + lax.dot_general(both, high, NT, preferred_element_type=F32)
    low = total[V:, :]
    gram = total[:V, :] + low + low.T
    row = lax.broadcasted_iota(jnp.int32, (V, 64), 0)
    lane = lax.broadcasted_iota(jnp.int32, (V, 64), 1)
    eye = jnp.where(row == lane, 1.0, 0.0).astype(F32)
    m_ref[:V, :] = jnp.concatenate([eye, gram, jnp.zeros((V, LANES - 64 - V), F32)], axis=1)


def halves(value):
    high = value.astype(BF16)
    return high, (value - high.astype(F32)).astype(BF16)


def mix(linv, value):
    left, left_low = halves(linv)
    right, right_low = halves(value)
    return jnp.dot(
        jnp.concatenate([left, left, left_low], axis=1),
        jnp.concatenate([right, right_low, right], axis=0),
        preferred_element_type=F32,
    )


CHOL = 3
UN = 8


def factor_piece(m_ref, col_ref, j):
    sub = lax.broadcasted_iota(jnp.int32, (8, LANES), 0)
    m = [m_ref[8 * t : 8 * t + 8, :] for t in range(TILES)]
    cols = []
    for s in range(CHOL):
        index = jnp.full((8, LANES), 64 + s, jnp.int32) + j
        cols.append([lanes_of(m[t], index) for t in range(TILES)])
        for t in range(TILES):
            col_ref[s, 8 * t : 8 * t + 8, :] = cols[s][t]
    for s in range(CHOL):
        row = wide(m_ref[pl.ds(j + s, 1), :])
        head = {n: wide(col_ref[n, pl.ds(j + s, 1), :]) for n in range(s, CHOL)}
        inverse = 1.0 / head[s]
        for t in range(TILES):
            factor = jnp.where(sub + 8 * t > j + s, cols[s][t] * inverse, 0.0)
            m[t] = m[t] - factor * row
            m_ref[8 * t : 8 * t + 8, :] = m[t]
            for n in range(s + 1, CHOL):
                cols[n][t] = cols[n][t] - factor * head[n]
                col_ref[n, 8 * t : 8 * t + 8, :] = cols[n][t]


def inverse_of(m_ref):
    m = m_ref[:V, :]
    row = lax.broadcasted_iota(jnp.int32, (V, LANES), 0)
    lane = lax.broadcasted_iota(jnp.int32, (V, LANES), 1)
    diag = jnp.sum(jnp.where(lane == row + 64, m, 0.0), axis=1, keepdims=True)
    return m[:, :V] / jnp.sqrt(diag)


def solve_to(dst_ref, linv, src_ref):
    out = mix(linv, flat(src_ref))
    for a in range(3):
        for q in range(NC):
            at = (a * NC + q) * LANES
            dst_ref[q, a * V : a * V + V, :] = out[:, at : at + LANES]


def rows_of(src_ref, index, tiles, c):
    block = (lax.broadcasted_iota(jnp.int32, (8, LANES), 1) // OVD) ^ c
    out = []
    for at in tiles:
        pick = lanes_of(src_ref[NC - 1, at, :], index)
        for q in range(NC - 1):
            pick = jnp.where(block == q, lanes_of(src_ref[q, at, :], index), pick)
        out.append(pick)
    return out


def index_row(small_ref, row):
    total = small_ref[0, pl.ds(row, 1), :]
    for q in range(1, NC):
        total = total + small_ref[q, pl.ds(row, 1), :]
    return total


def main_kernel(
    c_ref, p0, p1, p2, p3, v0, v1, v2, v3,
    y2_ref, w_ref, linv_ref, s1_ref, s2_ref, row_ref,
    y_ref, z_ref, m_ref, col_ref, g_ref, x_ref, oh_ref, t_ref, cols_ref, pair_ref, scale_ref, sum_ref,
):
    c = c_ref[0]
    small_ref = Blocks((p0, p1, p2, p3))
    val_ref = Blocks((v0, v1, v2, v3))
    for m in range(NC):
        col = small_ref[m, COL0 : COL0 + NB, :]
        local = (col.astype(jnp.int32) ^ (c * LANES)).astype(F32)
        cols_ref[m, NB:32, :] = jnp.full((32 - NB, LANES), -1.0, F32)
        cols_ref[m, 0:NB, :] = jnp.where(col < 0.0, -1.0, local)
    m_ref[V:, :] = jnp.zeros((8, LANES), F32)

    def loop(src_ref, dst_ref, first):
        split_to(x_ref, src_ref)
        if first:
            one_hot(cols_ref, oh_ref, 0)
            one_hot(cols_ref, oh_ref, 1)
        else:
            gram_to(m_ref, x_ref)
        start_op(small_ref, src_ref, dst_ref)
        pack_pairs(src_ref, scale_ref, pair_ref)
        sum_ref[...] = jnp.zeros((NC, 3 * V, LANES), F32)
        issue(x_ref, oh_ref, t_ref, 0, 0)

        def step(it, carry):
            for u in range(UN):
                k = UN * it + u
                issue(x_ref, oh_ref, t_ref, jnp.minimum(k + 1, ONE - 1), (u + 1) % 2)
                ks = [ONE + (REST // 2) * it + 3 * (u % 2) + n for n in range(3)]
                lane_blocks(val_ref, cols_ref, pair_ref, sum_ref, u // 2, ks)
                if first:
                    one_hot(cols_ref, oh_ref, jnp.minimum(k + 2, ONE - 1))
                else:
                    factor_piece(m_ref, col_ref, k * CHOL)
                take(val_ref, dst_ref, t_ref, k, u % 2)
            return carry

        lax.fori_loop(0, ONE // UN, step, 0)
        for q in range(NC):
            for a in range(3):
                at = slice(a * V, a * V + V)
                dst_ref[q, at, :] = dst_ref[q, at, :] + sum_ref[q, at, :] * scale_ref[...]

    loop(small_ref, y_ref, True)
    loop(y_ref, z_ref, False)
    solve_to(y2_ref, inverse_of(m_ref), z_ref)
    loop(y2_ref, w_ref, False)
    linv = inverse_of(m_ref)
    linv_ref[...] = linv
    first = wide(index_row(small_ref, SEND0 + entry(SENT, c))).astype(jnp.int32)
    second = wide(index_row(small_ref, SEND0 + entry(SPLIT, c))).astype(jnp.int32)
    half = (c % 2) * (V // 2)
    for n, slot in enumerate((entry(GOT, c), entry(SPLIT, c))):
        row_ref[2 * n : 2 * n + 1, :] = index_row(small_ref, RECV0 + slot)
        row_ref[2 * n + 1 : 2 * n + 2, :] = index_row(small_ref, LIVE0 + slot)
    tiles = [slice(8 * t, 8 * t + 8) for t in range(3 * TILES)]
    for n, index in enumerate((first, second)):
        for at, piece in zip(tiles, rows_of(w_ref, index, tiles, c)):
            g_ref[n, at, :] = piece
    both = jnp.concatenate([g_ref[n, a * V : a * V + V, :] for n in range(2) for a in range(3)], axis=1)
    image = mix(linv, both)
    for a in range(3):
        s1_ref[a * V : a * V + V, :] = image[:, a * LANES : a * LANES + LANES]
        g_ref[1, a * V : a * V + V, :] = image[:, (3 + a) * LANES : (4 + a) * LANES]
        s2_ref[a * (V // 2) : (a + 1) * (V // 2), :] = g_ref[1, pl.ds(pl.multiple_of(a * V + half, 8), V // 2), :]


def middle_kernel(c_ref, row_ref, y2_ref, linv_ref, mine1_ref, mine2_ref, g_ref):
    c = c_ref[0]
    tiles = [slice(8 * t, 8 * t + 8) for t in range(3 * TILES)]
    for n in range(2):
        index = wide(row_ref[2 * n : 2 * n + 1, :]).astype(jnp.int32)
        live = wide(row_ref[2 * n + 1 : 2 * n + 2, :])
        for at, piece in zip(tiles, rows_of(y2_ref, index, tiles, c)):
            g_ref[n, at, :] = piece * live
    both = jnp.concatenate([g_ref[n, a * V : a * V + V, :] for n in range(2) for a in range(3)], axis=1)
    mine = mix(linv_ref[...], both)
    for n, out_ref in enumerate((mine1_ref, mine2_ref)):
        for a in range(3):
            at = (3 * n + a) * LANES
            out_ref[a * V : a * V + V, :] = mine[:, at : at + LANES]


def basis_kernel(after_ref, y2_ref, w_ref, linv_ref, basis_ref, center_ref, q_ref):
    linv = linv_ref[...]
    solve_to(q_ref, linv, y2_ref)
    basis_ref[...] = q_ref[0]
    image = mix(linv, flat(w_ref))
    center_ref[...] = lax.dot_general(flat(q_ref), image, NT, precision=HIGH, preferred_element_type=F32)


def coarse_kernel(c_ref, mine1_ref, mine2_ref, got1_ref, got2_ref, near_ref, far_ref, r_ref):
    c = c_ref[0]

    def side(ref, count):
        return jnp.concatenate([ref[a * count : a * count + count, :] for a in range(3)], axis=1)

    one = lax.dot_general(side(mine1_ref, V), side(got1_ref, V), NT, precision=HIGH, preferred_element_type=F32) * SCALE
    two = lax.dot_general(side(mine2_ref, V), side(got2_ref, V // 2), NT, precision=HIGH, preferred_element_type=F32) * SCALE
    part = V // NC
    for d in range(NC):
        r_ref[d, 0:part, 0:V] = one[d * part : d * part + part, :]
        r_ref[d, 16 : 16 + part, 0 : V // 2] = two[d * part : d * part + part, :]
    near_ref[0] = r_ref[c]
    near_ref[1] = r_ref[c ^ 1]
    far_ref[0] = r_ref[c ^ 2]
    far_ref[1] = r_ref[c ^ 3]


def pair_kernel(near_ref, far_ref, after_ref, out_ref):
    out_ref[0] = near_ref[1]
    out_ref[1] = far_ref[1]


def join_kernel(c_ref, center_ref, near_ref, far_ref, on_ref, out_ref, r_ref):
    c = c_ref[0]
    part = V // NC
    for m, value in enumerate((near_ref[0], on_ref[0], far_ref[0], on_ref[1])):
        r_ref[m] = value

    def put(place, value):
        for v in range(part):
            out_ref[place * part + v] = value[v : v + 1, :]

    for d in range(NC):
        slot = GOT[d]
        put(slot if slot < RADIUS else slot + 1, r_ref[c ^ d, 0:part, 0:V])
    for d in (0, 2):
        slot = SPLIT[d]
        sides = [r_ref[c ^ (d + h), 16 : 16 + part, 0 : V // 2] for h in range(2)]
        put(slot if slot < RADIUS else slot + 1, jnp.concatenate(sides, axis=1))
    for d in range(NC):

        @pl.when(c == d)
        def _():
            put(RADIUS, center_ref[d * part : d * part + part, :])


def shards(test_vectors, ell_values, ell_cols, ell_count, pivot, send_rows, recv_rows, ov_count):
    shape = pltpu.VMEM
    c = lax.axis_index("crow").astype(jnp.int32).reshape(1)
    x = jnp.transpose(test_vectors[0], (1, 0, 2)).reshape(3 * V, LANES)
    values = ell_values.reshape(9 * NB, 1, LANES)

    def pass_on(piece, m):
        return lax.ppermute(piece, "crow", [(n, n ^ m) for n in range(NC)])

    far_v = pass_on(values, 2)
    packed = pl.pallas_call(
        pack_kernel,
        out_shape=shape((PACKED, LANES), F32),
        in_specs=[smem(), smem()] + [vmem()] * 6,
        out_specs=vmem(),
    )(
        c,
        ov_count.reshape(SLOTS),
        x,
        ell_cols.reshape(NB, 1, LANES),
        ell_count.reshape(1, LANES),
        pivot.reshape(3, 1, LANES),
        send_rows.reshape(SLOTS, 1, OVD),
        recv_rows.reshape(SLOTS, 1, OVD),
    )
    far_p = pass_on(packed, 2)
    blocks = []
    for own, far in ((packed, far_p), (values, far_v)):
        blocks += [own, pass_on(own, 1), far, pass_on(far, 1)]
    block = (NC, 3 * V, LANES)
    y2, w, linv, s1, s2, row = pl.pallas_call(
        main_kernel,
        out_shape=(
            shape(block, F32),
            shape(block, F32),
            shape((V, V), F32),
            shape((3 * V, LANES), F32),
            shape((3 * V // 2, LANES), F32),
            shape((8, LANES), F32),
        ),
        in_specs=[smem()] + [vmem()] * 8,
        out_specs=(vmem(),) * 6,
        scratch_shapes=[
            pltpu.VMEM(block, F32),
            pltpu.VMEM(block, F32),
            pltpu.VMEM((V + 8, LANES), F32),
            pltpu.VMEM((CHOL, V + 8, LANES), F32),
            pltpu.VMEM((2, 3 * V, LANES), F32),
            pltpu.VMEM((6 * V, NC * LANES), BF16),
            pltpu.VMEM((2, ONE, NC * LANES, 2 * LANES), BF16),
            pltpu.VMEM((2, 2, 3 * V, 2 * LANES), F32),
            pltpu.VMEM((NC, 32, LANES), F32),
            pltpu.VMEM((NC, 3 * V // 2, LANES), jnp.int32),
            pltpu.VMEM((V, LANES), F32),
            pltpu.VMEM(block, F32),
        ],
        compiler_params=LIMIT,
    )(c, *map(near, blocks))

    size = lax.axis_size("sub")

    def across(piece, slots, turn):
        pairs = []
        for j in range(size):
            for n in range(NC):
                i = (j - OFFSETS[slots[n]]) % size
                pairs.append((j * NC + n, i * NC + (n ^ turn)))
        return lax.ppermute(piece, ("sub", "crow"), pairs)

    got1 = across(s1, SENT, 2)
    got2 = across(s2, SPLIT, 0)
    mine1, mine2 = pl.pallas_call(
        middle_kernel,
        out_shape=(shape((3 * V, LANES), F32), shape((3 * V, LANES), F32)),
        in_specs=[smem()] + [vmem()] * 3,
        out_specs=(vmem(),) * 2,
        scratch_shapes=[pltpu.VMEM((2, 3 * V, LANES), F32)],
        compiler_params=LIMIT,
    )(c, *map(near, (row, y2, linv)))
    pair = shape((2, 32, LANES), F32)
    mine, sent = pl.pallas_call(
        coarse_kernel,
        out_shape=(pair, pair),
        in_specs=[smem()] + [vmem()] * 4,
        out_specs=(vmem(),) * 2,
        scratch_shapes=[pltpu.VMEM((NC, 32, LANES), F32)],
        compiler_params=LIMIT,
    )(c, *map(near, (mine1, mine2, got1, got2)))
    far = pass_on(sent, 2)
    basis, center = pl.pallas_call(
        basis_kernel,
        out_shape=(jax.ShapeDtypeStruct((3 * V, LANES), F32), shape((V, V), F32)),
        in_specs=[vmem()] * 4,
        out_specs=(vmem(),) * 2,
        scratch_shapes=[pltpu.VMEM(block, F32)],
        compiler_params=LIMIT,
    )(*map(near, (mine, y2, w, linv)))
    both = pl.pallas_call(
        pair_kernel, out_shape=pair, in_specs=[vmem()] * 3, out_specs=vmem(), compiler_params=LIMIT
    )(near(mine), near(far), near(center))
    on = pass_on(both, 1)
    coarse = pl.pallas_call(
        join_kernel,
        out_shape=jax.ShapeDtypeStruct(((2 * RADIUS + 1) * (V // NC), 1, V), F32),
        in_specs=[smem()] + [vmem()] * 4,
        out_specs=vmem(),
        scratch_shapes=[pltpu.VMEM((NC, 32, LANES), F32)],
        compiler_params=LIMIT,
    )(c, *map(near, (center, mine, far, on)))
    coarse = coarse.reshape(2 * RADIUS + 1, V // NC, V)
    basis = jnp.transpose(basis.reshape(3, V, LANES), (1, 0, 2))
    return basis[None], coarse[None]


def solution(mesh):
    placed = (
        P("sub", None, None, "crow"),
        P("sub", None, None, "crow"),
        P("sub", None, "crow"),
        P("sub", "crow"),
        P("sub", None, "crow"),
        P("sub", None, "crow"),
        P("sub", None, "crow"),
        P("sub", None, "crow"),
    )
    return jax.shard_map(
        shards,
        mesh=mesh,
        in_specs=placed,
        out_specs=(P("sub", None, None, "crow"), P("sub", None, "crow", None)),
        check_vma=False,
    )
```

```python
import jax
import jax.numpy as jnp
from jax import lax
from jax.experimental import pallas as pl
from jax.experimental.pallas import tpu as pltpu
from jax.sharding import PartitionSpec as P

RADIUS = 3
SLOTS = 2 * RADIUS
V = 48
LANES = 128
NB = 27
NC = 4
OVD = 32
SCALE = float(LANES * NC // OVD)
TILES = V // 8

COL0 = 3 * V
PIV0 = COL0 + NB
SEND0 = PIV0 + 3
RECV0 = SEND0 + SLOTS
LIVE0 = RECV0 + SLOTS
PACKED = LIVE0 + SLOTS

OFFSETS = [o - RADIUS if o < RADIUS else o - RADIUS + 1 for o in range(SLOTS)]
SENT = [0, 2, 5, 3]
GOT = [SENT[c ^ 2] for c in range(NC)]
SPLIT = [1, 1, 4, 4]
HIGH = lax.Precision.HIGHEST
F32 = jnp.float32


def vmem():
    return pl.BlockSpec(memory_space=pltpu.VMEM)


def smem():
    return pl.BlockSpec(memory_space=pltpu.SMEM)


LIMIT = pltpu.CompilerParams(vmem_limit_bytes=40 * 2**20)


def near(array):
    return pltpu.with_memory_space_constraint(array, pltpu.VMEM)


class Blocks:
    def __init__(self, refs):
        self.refs = refs

    def __getitem__(self, at):
        return self.refs[at[0]][at[1:]]


def pack_kernel(c_ref, ov_ref, x_ref, col_ref, cnt_ref, piv_ref, send_ref, recv_ref, out_ref):
    out_ref[0 : 3 * V, :] = x_ref[...]
    count = cnt_ref[...]
    for k in range(NB):
        out_ref[COL0 + k : COL0 + k + 1, :] = jnp.where(k < count, col_ref[k].astype(F32), -1.0)
    for a in range(3):
        out_ref[PIV0 + a : PIV0 + a + 1, :] = piv_ref[a]
    lane = lax.broadcasted_iota(jnp.int32, (1, LANES), 1)
    c = c_ref[0]
    here = (lane // OVD) == c
    for o in range(SLOTS):
        for ref, base in ((send_ref, SEND0), (recv_ref, RECV0)):
            piece = ref[o].astype(F32)
            row = jnp.concatenate([piece] * NC, axis=1)
            out_ref[base + o : base + o + 1, :] = jnp.where(here, row, 0.0)
        alive = here & ((lane % OVD) < ov_ref[o])
        out_ref[LIVE0 + o : LIVE0 + o + 1, :] = jnp.where(alive, 1.0, 0.0).astype(F32)


def entry(table, c):
    value = jnp.int32(table[0])
    for n in range(1, NC):
        value = jnp.where(c == n, table[n], value)
    return value


def wide(row):
    return jnp.broadcast_to(row, (8, LANES))


def lanes_of(block, index):
    return jnp.take_along_axis(block, index, axis=1)


def start_op(small_ref, src_ref, dst_ref):
    for q in range(NC):
        for a in range(3):
            piv = wide(small_ref[q, PIV0 + a : PIV0 + a + 1, :])
            for t in range(TILES):
                rows = slice(a * V + 8 * t, a * V + 8 * t + 8)
                dst_ref[q, rows, :] = piv * src_ref[q, rows, :]


ONE = 16
BF16 = jnp.bfloat16


def value_row(val_ref, rc, ab, k):
    return wide(val_ref[rc, ab * NB + k, :, :])


def add_block(val, dst_ref, rc, pick_of):
    for t in range(TILES):
        pick = [pick_of(b, t) for b in range(3)]
        for a in range(3):
            at = slice(a * V + 8 * t, a * V + 8 * t + 8)
            dst_ref[rc, at, :] = dst_ref[rc, at, :] + (
                val[3 * a] * pick[0] + val[3 * a + 1] * pick[1] + val[3 * a + 2] * pick[2]
            )


def pack_pairs(src_ref, scale_ref, pair_ref):
    inverse = []
    for t in range(TILES):
        top = None
        for q in range(NC):
            for b in range(3):
                size = jnp.abs(src_ref[q, b * V + 8 * t : b * V + 8 * t + 8, :])
                top = size if top is None else jnp.maximum(top, size)
        top = jnp.broadcast_to(jnp.maximum(jnp.max(top, axis=1, keepdims=True), 1e-30), (8, LANES))
        scale_ref[8 * t : 8 * t + 8, :] = top * (1.0 / 32767.0)
        inverse.append(32767.0 / top)
    for q in range(NC):
        for b in range(3):
            for p in range(TILES // 2):
                whole = [
                    jnp.round(src_ref[q, b * V + 8 * t : b * V + 8 * t + 8, :] * inverse[t]).astype(jnp.int32)
                    for t in (2 * p, 2 * p + 1)
                ]
                at = 8 * (b * (TILES // 2) + p)
                pair_ref[q, at : at + 8, :] = (whole[0] << 16) | (whole[1] & 65535)


def lane_blocks(val_ref, cols_ref, pair_ref, sum_ref, rc, ks):
    blocks = []
    for k in ks:
        col = wide(cols_ref[rc, k : k + 1, :]).astype(jnp.int32)
        val = [jnp.where(col >= 0, value_row(val_ref, rc, ab, k), 0.0) for ab in range(9)]
        blocks.append((val, col & (LANES - 1), (col & LANES) != 0, col >= 2 * LANES))
    for p in range(TILES // 2):
        rows = [[slice(a * V + 8 * t, a * V + 8 * t + 8) for t in (2 * p, 2 * p + 1)] for a in range(3)]
        total = [[sum_ref[rc, at, :] for at in pair] for pair in rows]
        for val, index, odd, top in blocks:
            for b in range(3):
                at = 8 * (b * (TILES // 2) + p)
                got = [lanes_of(pair_ref[q, at : at + 8, :], index) for q in range(NC)]
                both = jnp.where(top, jnp.where(odd, got[3], got[2]), jnp.where(odd, got[1], got[0]))
                pick = ((both >> 16).astype(F32), ((both << 16) >> 16).astype(F32))
                for a in range(3):
                    for n in range(2):
                        total[a][n] = total[a][n] + val[3 * a + b] * pick[n]
        for a in range(3):
            for n in range(2):
                sum_ref[rc, rows[a][n], :] = total[a][n]


def one_hot(cols_ref, oh_ref, k):
    half = 2 * LANES
    place = lax.broadcasted_iota(jnp.int32, (half, half), 0).astype(F32).astype(BF16)
    for m in range(2):
        col = jnp.concatenate([cols_ref[2 * m + n, k : k + 1, :] for n in range(2)], axis=1)
        for h in range(2):
            local = col - float(h * half)
            local = jnp.where((local >= 0.0) & (local < float(half)), local, -1.0)
            target = jnp.concatenate([jnp.broadcast_to(local, (16, half)).astype(BF16)] * (half // 16), axis=0)
            oh_ref[m, k, h * half : h * half + half, :] = jnp.where(
                place == target, jnp.ones((), BF16), jnp.zeros((), BF16)
            )


def split_to(x_ref, src_ref):
    for q in range(NC):
        at = slice(q * LANES, q * LANES + LANES)
        value = src_ref[q, 0 : 3 * V, :]
        x_ref[0 : 3 * V, at], x_ref[3 * V :, at] = halves(value)


def issue(x_ref, oh_ref, t_ref, k, parity):
    for m in range(2):
        got = jnp.dot(x_ref[...], oh_ref[m, k], preferred_element_type=F32)
        t_ref[parity, m] = got[: 3 * V, :] + got[3 * V :, :]


def take(val_ref, dst_ref, t_ref, k, parity):
    for m in range(2):
        for n in range(2):
            at = slice(n * LANES, n * LANES + LANES)
            rc = 2 * m + n
            val = [value_row(val_ref, rc, ab, k) for ab in range(9)]
            add_block(val, dst_ref, rc, lambda b, t: t_ref[parity, m, b * V + 8 * t : b * V + 8 * t + 8, at])


def flat(ref):
    return jnp.concatenate([ref[q, a * V : a * V + V, :] for a in range(3) for q in range(NC)], axis=1)


NT = (((1,), (1,)), ((), ()))


def gram_to(m_ref, x_ref):
    total = jnp.zeros((2 * V, V), F32)
    for b in range(3):
        high = x_ref[b * V : b * V + V, :]
        both = jnp.concatenate([high, x_ref[(3 + b) * V : (4 + b) * V, :]], axis=0)
        total = total + lax.dot_general(both, high, NT, preferred_element_type=F32)
    low = total[V:, :]
    gram = total[:V, :] + low + low.T
    row = lax.broadcasted_iota(jnp.int32, (V, 64), 0)
    lane = lax.broadcasted_iota(jnp.int32, (V, 64), 1)
    eye = jnp.where(row == lane, 1.0, 0.0).astype(F32)
    m_ref[:V, :] = jnp.concatenate([eye, gram, jnp.zeros((V, LANES - 64 - V), F32)], axis=1)


def halves(value):
    high = value.astype(BF16)
    return high, (value - high.astype(F32)).astype(BF16)


def mix(linv, value):
    left, left_low = halves(linv)
    right, right_low = halves(value)
    return jnp.dot(
        jnp.concatenate([left, left, left_low], axis=1),
        jnp.concatenate([right, right_low, right], axis=0),
        preferred_element_type=F32,
    )


CHOL = 3


def factor_piece(m_ref, col_ref, j):
    sub = lax.broadcasted_iota(jnp.int32, (8, LANES), 0)
    tiles = range(j // 8, TILES)
    m = {t: m_ref[8 * t : 8 * t + 8, :] for t in tiles}
    cols = []
    for s in range(CHOL):
        index = jnp.full((8, LANES), 64 + s + j, jnp.int32)
        cols.append({t: lanes_of(m[t], index) for t in tiles})
        for t in tiles:
            col_ref[s, 8 * t : 8 * t + 8, :] = cols[s][t]
    for s in range(CHOL):
        row = wide(m_ref[j + s : j + s + 1, :])
        head = {n: wide(col_ref[n, j + s : j + s + 1, :]) for n in range(s, CHOL)}
        inverse = 1.0 / head[s]
        for t in tiles:
            if 8 * t + 7 <= j + s:
                continue
            factor = cols[s][t] * inverse
            if 8 * t <= j + s:
                factor = jnp.where(sub + 8 * t > j + s, factor, 0.0)
            m[t] = m[t] - factor * row
            m_ref[8 * t : 8 * t + 8, :] = m[t]
            for n in range(s + 1, CHOL):
                cols[n][t] = cols[n][t] - factor * head[n]
                col_ref[n, 8 * t : 8 * t + 8, :] = cols[n][t]


def inverse_of(m_ref):
    m = m_ref[:V, :]
    row = lax.broadcasted_iota(jnp.int32, (V, LANES), 0)
    lane = lax.broadcasted_iota(jnp.int32, (V, LANES), 1)
    diag = jnp.sum(jnp.where(lane == row + 64, m, 0.0), axis=1, keepdims=True)
    return m[:, :V] / jnp.sqrt(diag)


def solve_to(dst_ref, linv, src_ref):
    out = mix(linv, flat(src_ref))
    for a in range(3):
        for q in range(NC):
            at = (a * NC + q) * LANES
            dst_ref[q, a * V : a * V + V, :] = out[:, at : at + LANES]


def rows_of(src_ref, index, tiles, c):
    block = (lax.broadcasted_iota(jnp.int32, (8, LANES), 1) // OVD) ^ c
    out = []
    for at in tiles:
        pick = lanes_of(src_ref[NC - 1, at, :], index)
        for q in range(NC - 1):
            pick = jnp.where(block == q, lanes_of(src_ref[q, at, :], index), pick)
        out.append(pick)
    return out


def index_row(small_ref, row):
    total = small_ref[0, pl.ds(row, 1), :]
    for q in range(1, NC):
        total = total + small_ref[q, pl.ds(row, 1), :]
    return total


def main_kernel(
    c_ref, p0, p1, p2, p3, v0, v1, v2, v3,
    y2_ref, w_ref, linv_ref, s1_ref, s2_ref, row_ref,
    y_ref, z_ref, m_ref, col_ref, g_ref, x_ref, oh_ref, t_ref, cols_ref, pair_ref, scale_ref, sum_ref,
):
    c = c_ref[0]
    small_ref = Blocks((p0, p1, p2, p3))
    val_ref = Blocks((v0, v1, v2, v3))
    for m in range(NC):
        col = small_ref[m, COL0 : COL0 + NB, :]
        local = (col.astype(jnp.int32) ^ (c * LANES)).astype(F32)
        cols_ref[m, NB:32, :] = jnp.full((32 - NB, LANES), -1.0, F32)
        cols_ref[m, 0:NB, :] = jnp.where(col < 0.0, -1.0, local)
    m_ref[V:, :] = jnp.zeros((8, LANES), F32)

    def apply(src_ref, dst_ref, first):
        split_to(x_ref, src_ref)
        if first:
            one_hot(cols_ref, oh_ref, 0)
            one_hot(cols_ref, oh_ref, 1)
        else:
            gram_to(m_ref, x_ref)
        start_op(small_ref, src_ref, dst_ref)
        pack_pairs(src_ref, scale_ref, pair_ref)
        sum_ref[...] = jnp.zeros((NC, 3 * V, LANES), F32)
        issue(x_ref, oh_ref, t_ref, 0, 0)

        for k in range(ONE):
            if k + 1 < ONE:
                issue(x_ref, oh_ref, t_ref, k + 1, (k + 1) % 2)
            ks = [n for n in range(ONE + 3 * (k % 4), ONE + 3 * (k % 4) + 3) if n < NB]
            lane_blocks(val_ref, cols_ref, pair_ref, sum_ref, k // 4, ks)
            if first:
                if k + 2 < ONE:
                    one_hot(cols_ref, oh_ref, k + 2)
            else:
                factor_piece(m_ref, col_ref, k * CHOL)
            take(val_ref, dst_ref, t_ref, k, k % 2)
        for q in range(NC):
            for a in range(3):
                at = slice(a * V, a * V + V)
                dst_ref[q, at, :] = dst_ref[q, at, :] + sum_ref[q, at, :] * scale_ref[...]

    apply(small_ref, y_ref, True)
    apply(y_ref, z_ref, False)
    solve_to(y2_ref, inverse_of(m_ref), z_ref)
    apply(y2_ref, w_ref, False)
    linv = inverse_of(m_ref)
    linv_ref[...] = linv
    first = wide(index_row(small_ref, SEND0 + entry(SENT, c))).astype(jnp.int32)
    second = wide(index_row(small_ref, SEND0 + entry(SPLIT, c))).astype(jnp.int32)
    half = (c % 2) * (V // 2)
    for n, slot in enumerate((entry(GOT, c), entry(SPLIT, c))):
        row_ref[2 * n : 2 * n + 1, :] = index_row(small_ref, RECV0 + slot)
        row_ref[2 * n + 1 : 2 * n + 2, :] = index_row(small_ref, LIVE0 + slot)
    tiles = [slice(8 * t, 8 * t + 8) for t in range(3 * TILES)]
    for n, index in enumerate((first, second)):
        for at, piece in zip(tiles, rows_of(w_ref, index, tiles, c)):
            g_ref[n, at, :] = piece
    both = jnp.concatenate([g_ref[n, a * V : a * V + V, :] for n in range(2) for a in range(3)], axis=1)
    image = mix(linv, both)
    for a in range(3):
        s1_ref[a * V : a * V + V, :] = image[:, a * LANES : a * LANES + LANES]
        g_ref[1, a * V : a * V + V, :] = image[:, (3 + a) * LANES : (4 + a) * LANES]
        s2_ref[a * (V // 2) : (a + 1) * (V // 2), :] = g_ref[1, pl.ds(pl.multiple_of(a * V + half, 8), V // 2), :]


def middle_kernel(c_ref, row_ref, y2_ref, linv_ref, mine1_ref, mine2_ref, g_ref):
    c = c_ref[0]
    tiles = [slice(8 * t, 8 * t + 8) for t in range(3 * TILES)]
    for n in range(2):
        index = wide(row_ref[2 * n : 2 * n + 1, :]).astype(jnp.int32)
        live = wide(row_ref[2 * n + 1 : 2 * n + 2, :])
        for at, piece in zip(tiles, rows_of(y2_ref, index, tiles, c)):
            g_ref[n, at, :] = piece * live
    both = jnp.concatenate([g_ref[n, a * V : a * V + V, :] for n in range(2) for a in range(3)], axis=1)
    mine = mix(linv_ref[...], both)
    for n, out_ref in enumerate((mine1_ref, mine2_ref)):
        for a in range(3):
            at = (3 * n + a) * LANES
            out_ref[a * V : a * V + V, :] = mine[:, at : at + LANES]


def basis_kernel(after_ref, y2_ref, w_ref, linv_ref, basis_ref, center_ref, q_ref):
    linv = linv_ref[...]
    solve_to(q_ref, linv, y2_ref)
    basis_ref[...] = q_ref[0]
    image = mix(linv, flat(w_ref))
    center_ref[...] = lax.dot_general(flat(q_ref), image, NT, precision=HIGH, preferred_element_type=F32)


def coarse_kernel(c_ref, mine1_ref, mine2_ref, got1_ref, got2_ref, near_ref, far_ref, r_ref):
    c = c_ref[0]

    def side(ref, count):
        return jnp.concatenate([ref[a * count : a * count + count, :] for a in range(3)], axis=1)

    one = lax.dot_general(side(mine1_ref, V), side(got1_ref, V), NT, precision=HIGH, preferred_element_type=F32) * SCALE
    two = lax.dot_general(side(mine2_ref, V), side(got2_ref, V // 2), NT, precision=HIGH, preferred_element_type=F32) * SCALE
    part = V // NC
    for d in range(NC):
        r_ref[d, 0:part, 0:V] = one[d * part : d * part + part, :]
        r_ref[d, 16 : 16 + part, 0 : V // 2] = two[d * part : d * part + part, :]
    near_ref[0] = r_ref[c]
    near_ref[1] = r_ref[c ^ 1]
    far_ref[0] = r_ref[c ^ 2]
    far_ref[1] = r_ref[c ^ 3]


def pair_kernel(near_ref, far_ref, after_ref, out_ref):
    out_ref[0] = near_ref[1]
    out_ref[1] = far_ref[1]


def join_kernel(c_ref, center_ref, near_ref, far_ref, on_ref, out_ref, r_ref):
    c = c_ref[0]
    part = V // NC
    for m, value in enumerate((near_ref[0], on_ref[0], far_ref[0], on_ref[1])):
        r_ref[m] = value

    def put(place, value):
        for v in range(part):
            out_ref[place * part + v] = value[v : v + 1, :]

    for d in range(NC):
        slot = GOT[d]
        put(slot if slot < RADIUS else slot + 1, r_ref[c ^ d, 0:part, 0:V])
    for d in (0, 2):
        slot = SPLIT[d]
        sides = [r_ref[c ^ (d + h), 16 : 16 + part, 0 : V // 2] for h in range(2)]
        put(slot if slot < RADIUS else slot + 1, jnp.concatenate(sides, axis=1))
    for d in range(NC):

        @pl.when(c == d)
        def _():
            put(RADIUS, center_ref[d * part : d * part + part, :])


def shards(test_vectors, ell_values, ell_cols, ell_count, pivot, send_rows, recv_rows, ov_count):
    shape = pltpu.VMEM
    c = lax.axis_index("crow").astype(jnp.int32).reshape(1)
    x = jnp.transpose(test_vectors[0], (1, 0, 2)).reshape(3 * V, LANES)
    values = ell_values.reshape(9 * NB, 1, LANES)

    def pass_on(piece, m):
        return lax.ppermute(piece, "crow", [(n, n ^ m) for n in range(NC)])

    far_v = pass_on(values, 2)
    packed = pl.pallas_call(
        pack_kernel,
        out_shape=shape((PACKED, LANES), F32),
        in_specs=[smem(), smem()] + [vmem()] * 6,
        out_specs=vmem(),
    )(
        c,
        ov_count.reshape(SLOTS),
        x,
        ell_cols.reshape(NB, 1, LANES),
        ell_count.reshape(1, LANES),
        pivot.reshape(3, 1, LANES),
        send_rows.reshape(SLOTS, 1, OVD),
        recv_rows.reshape(SLOTS, 1, OVD),
    )
    far_p = pass_on(packed, 2)
    blocks = []
    for own, far in ((packed, far_p), (values, far_v)):
        blocks += [own, pass_on(own, 1), far, pass_on(far, 1)]
    block = (NC, 3 * V, LANES)
    y2, w, linv, s1, s2, row = pl.pallas_call(
        main_kernel,
        out_shape=(
            shape(block, F32),
            shape(block, F32),
            shape((V, V), F32),
            shape((3 * V, LANES), F32),
            shape((3 * V // 2, LANES), F32),
            shape((8, LANES), F32),
        ),
        in_specs=[smem()] + [vmem()] * 8,
        out_specs=(vmem(),) * 6,
        scratch_shapes=[
            pltpu.VMEM(block, F32),
            pltpu.VMEM(block, F32),
            pltpu.VMEM((V + 8, LANES), F32),
            pltpu.VMEM((CHOL, V + 8, LANES), F32),
            pltpu.VMEM((2, 3 * V, LANES), F32),
            pltpu.VMEM((6 * V, NC * LANES), BF16),
            pltpu.VMEM((2, ONE, NC * LANES, 2 * LANES), BF16),
            pltpu.VMEM((2, 2, 3 * V, 2 * LANES), F32),
            pltpu.VMEM((NC, 32, LANES), F32),
            pltpu.VMEM((NC, 3 * V // 2, LANES), jnp.int32),
            pltpu.VMEM((V, LANES), F32),
            pltpu.VMEM(block, F32),
        ],
        compiler_params=LIMIT,
    )(c, *map(near, blocks))

    size = lax.axis_size("sub")

    def across(piece, slots, turn):
        pairs = []
        for j in range(size):
            for n in range(NC):
                i = (j - OFFSETS[slots[n]]) % size
                pairs.append((j * NC + n, i * NC + (n ^ turn)))
        return lax.ppermute(piece, ("sub", "crow"), pairs)

    got1 = across(s1, SENT, 2)
    got2 = across(s2, SPLIT, 0)
    mine1, mine2 = pl.pallas_call(
        middle_kernel,
        out_shape=(shape((3 * V, LANES), F32), shape((3 * V, LANES), F32)),
        in_specs=[smem()] + [vmem()] * 3,
        out_specs=(vmem(),) * 2,
        scratch_shapes=[pltpu.VMEM((2, 3 * V, LANES), F32)],
        compiler_params=LIMIT,
    )(c, *map(near, (row, y2, linv)))
    pair = shape((2, 32, LANES), F32)
    mine, sent = pl.pallas_call(
        coarse_kernel,
        out_shape=(pair, pair),
        in_specs=[smem()] + [vmem()] * 4,
        out_specs=(vmem(),) * 2,
        scratch_shapes=[pltpu.VMEM((NC, 32, LANES), F32)],
        compiler_params=LIMIT,
    )(c, *map(near, (mine1, mine2, got1, got2)))
    far = pass_on(sent, 2)
    basis, center = pl.pallas_call(
        basis_kernel,
        out_shape=(jax.ShapeDtypeStruct((3 * V, LANES), F32), shape((V, V), F32)),
        in_specs=[vmem()] * 4,
        out_specs=(vmem(),) * 2,
        scratch_shapes=[pltpu.VMEM(block, F32)],
        compiler_params=LIMIT,
    )(*map(near, (mine, y2, w, linv)))
    both = pl.pallas_call(
        pair_kernel, out_shape=pair, in_specs=[vmem()] * 3, out_specs=vmem(), compiler_params=LIMIT
    )(near(mine), near(far), near(center))
    on = pass_on(both, 1)
    coarse = pl.pallas_call(
        join_kernel,
        out_shape=jax.ShapeDtypeStruct(((2 * RADIUS + 1) * (V // NC), 1, V), F32),
        in_specs=[smem()] + [vmem()] * 4,
        out_specs=vmem(),
        scratch_shapes=[pltpu.VMEM((NC, 32, LANES), F32)],
        compiler_params=LIMIT,
    )(c, *map(near, (center, mine, far, on)))
    coarse = coarse.reshape(2 * RADIUS + 1, V // NC, V)
    basis = jnp.transpose(basis.reshape(3, V, LANES), (1, 0, 2))
    return basis[None], coarse[None]


def solution(mesh):
    placed = (
        P("sub", None, None, "crow"),
        P("sub", None, None, "crow"),
        P("sub", None, "crow"),
        P("sub", "crow"),
        P("sub", None, "crow"),
        P("sub", None, "crow"),
        P("sub", None, "crow"),
        P("sub", None, "crow"),
    )
    return jax.shard_map(
        shards,
        mesh=mesh,
        in_specs=placed,
        out_specs=(P("sub", None, None, "crow"), P("sub", None, "crow", None)),
        check_vma=False,
    )
```

```python
import jax
import jax.numpy as jnp
from jax import lax
from jax.experimental import pallas as pl
from jax.experimental.pallas import tpu as pltpu
from jax.sharding import PartitionSpec as P

RADIUS = 3
SLOTS = 2 * RADIUS
V = 48
LANES = 128
NB = 27
NC = 4
OVD = 32
SCALE = float(LANES * NC // OVD)
TILES = V // 8

COL0 = 3 * V
PIV0 = COL0 + NB
SEND0 = PIV0 + 3
RECV0 = SEND0 + SLOTS
LIVE0 = RECV0 + SLOTS
PACKED = LIVE0 + SLOTS

OFFSETS = [o - RADIUS if o < RADIUS else o - RADIUS + 1 for o in range(SLOTS)]
SENT = [0, 2, 5, 3]
GOT = [SENT[c ^ 2] for c in range(NC)]
SPLIT = [1, 1, 4, 4]
HIGH = lax.Precision.HIGHEST
F32 = jnp.float32


def vmem():
    return pl.BlockSpec(memory_space=pltpu.VMEM)


def smem():
    return pl.BlockSpec(memory_space=pltpu.SMEM)


LIMIT = pltpu.CompilerParams(vmem_limit_bytes=40 * 2**20)


def near(array):
    return pltpu.with_memory_space_constraint(array, pltpu.VMEM)


class Blocks:
    def __init__(self, refs):
        self.refs = refs

    def __getitem__(self, at):
        return self.refs[at[0]][at[1:]]


def pack_kernel(c_ref, ov_ref, x_ref, col_ref, cnt_ref, piv_ref, send_ref, recv_ref, out_ref):
    out_ref[0 : 3 * V, :] = x_ref[...]
    count = cnt_ref[...]
    for k in range(NB):
        out_ref[COL0 + k : COL0 + k + 1, :] = jnp.where(k < count, col_ref[k].astype(F32), -1.0)
    for a in range(3):
        out_ref[PIV0 + a : PIV0 + a + 1, :] = piv_ref[a]
    lane = lax.broadcasted_iota(jnp.int32, (1, LANES), 1)
    c = c_ref[0]
    here = (lane // OVD) == c
    for o in range(SLOTS):
        for ref, base in ((send_ref, SEND0), (recv_ref, RECV0)):
            piece = ref[o].astype(F32)
            row = jnp.concatenate([piece] * NC, axis=1)
            out_ref[base + o : base + o + 1, :] = jnp.where(here, row, 0.0)
        alive = here & ((lane % OVD) < ov_ref[o])
        out_ref[LIVE0 + o : LIVE0 + o + 1, :] = jnp.where(alive, 1.0, 0.0).astype(F32)


def entry(table, c):
    value = jnp.int32(table[0])
    for n in range(1, NC):
        value = jnp.where(c == n, table[n], value)
    return value


def wide(row):
    return jnp.broadcast_to(row, (8, LANES))


def lanes_of(block, index):
    return jnp.take_along_axis(block, index, axis=1)


def start_op(small_ref, src_ref, dst_ref):
    for q in range(NC):
        for a in range(3):
            piv = wide(small_ref[q, PIV0 + a : PIV0 + a + 1, :])
            for t in range(TILES):
                rows = slice(a * V + 8 * t, a * V + 8 * t + 8)
                dst_ref[q, rows, :] = piv * src_ref[q, rows, :]


ONE = 14
BF16 = jnp.bfloat16


def value_row(val_ref, rc, ab, k):
    return wide(val_ref[rc, ab * NB + k, :, :])


def add_block(val, dst_ref, rc, pick_of):
    for t in range(TILES):
        pick = [pick_of(b, t) for b in range(3)]
        for a in range(3):
            at = slice(a * V + 8 * t, a * V + 8 * t + 8)
            dst_ref[rc, at, :] = dst_ref[rc, at, :] + (
                val[3 * a] * pick[0] + val[3 * a + 1] * pick[1] + val[3 * a + 2] * pick[2]
            )


def pack_pairs(src_ref, scale_ref, pair_ref):
    inverse = []
    for t in range(TILES):
        top = None
        for q in range(NC):
            for b in range(3):
                size = jnp.abs(src_ref[q, b * V + 8 * t : b * V + 8 * t + 8, :])
                top = size if top is None else jnp.maximum(top, size)
        top = jnp.broadcast_to(jnp.maximum(jnp.max(top, axis=1, keepdims=True), 1e-30), (8, LANES))
        scale_ref[8 * t : 8 * t + 8, :] = top * (1.0 / 32767.0)
        inverse.append(32767.0 / top)
    for q in range(NC):
        for b in range(3):
            for p in range(TILES // 2):
                whole = [
                    jnp.round(src_ref[q, b * V + 8 * t : b * V + 8 * t + 8, :] * inverse[t]).astype(jnp.int32)
                    for t in (2 * p, 2 * p + 1)
                ]
                at = 8 * (b * (TILES // 2) + p)
                pair_ref[q, at : at + 8, :] = (whole[0] << 16) | (whole[1] & 65535)


def lane_blocks(val_ref, cols_ref, pair_ref, sum_ref, rc, ks):
    blocks = []
    for k in ks:
        col = wide(cols_ref[rc, k : k + 1, :]).astype(jnp.int32)
        val = [jnp.where(col >= 0, value_row(val_ref, rc, ab, k), 0.0) for ab in range(9)]
        blocks.append((val, col & (LANES - 1), (col & LANES) != 0, col >= 2 * LANES))
    for p in range(TILES // 2):
        rows = [[slice(a * V + 8 * t, a * V + 8 * t + 8) for t in (2 * p, 2 * p + 1)] for a in range(3)]
        total = [[sum_ref[rc, at, :] for at in pair] for pair in rows]
        for val, index, odd, top in blocks:
            for b in range(3):
                at = 8 * (b * (TILES // 2) + p)
                got = [lanes_of(pair_ref[q, at : at + 8, :], index) for q in range(NC)]
                both = jnp.where(top, jnp.where(odd, got[3], got[2]), jnp.where(odd, got[1], got[0]))
                pick = ((both >> 16).astype(F32), ((both << 16) >> 16).astype(F32))
                for a in range(3):
                    for n in range(2):
                        total[a][n] = total[a][n] + val[3 * a + b] * pick[n]
        for a in range(3):
            for n in range(2):
                sum_ref[rc, rows[a][n], :] = total[a][n]


def one_hot(cols_ref, oh_ref, k):
    half = 2 * LANES
    place = lax.broadcasted_iota(jnp.int32, (half, half), 0).astype(F32).astype(BF16)
    for m in range(2):
        col = jnp.concatenate([cols_ref[2 * m + n, k : k + 1, :] for n in range(2)], axis=1)
        for h in range(2):
            local = col - float(h * half)
            local = jnp.where((local >= 0.0) & (local < float(half)), local, -1.0)
            target = jnp.concatenate([jnp.broadcast_to(local, (16, half)).astype(BF16)] * (half // 16), axis=0)
            oh_ref[m, k, h * half : h * half + half, :] = jnp.where(
                place == target, jnp.ones((), BF16), jnp.zeros((), BF16)
            )


def split_to(x_ref, src_ref):
    for q in range(NC):
        at = slice(q * LANES, q * LANES + LANES)
        value = src_ref[q, 0 : 3 * V, :]
        x_ref[0 : 3 * V, at], x_ref[3 * V :, at] = halves(value)


def issue(x_ref, oh_ref, t_ref, k, parity):
    for m in range(2):
        got = jnp.dot(x_ref[...], oh_ref[m, k], preferred_element_type=F32)
        t_ref[parity, m] = got[: 3 * V, :] + got[3 * V :, :]


def take(val_ref, dst_ref, t_ref, k, parity):
    for m in range(2):
        for n in range(2):
            at = slice(n * LANES, n * LANES + LANES)
            rc = 2 * m + n
            val = [value_row(val_ref, rc, ab, k) for ab in range(9)]
            add_block(val, dst_ref, rc, lambda b, t: t_ref[parity, m, b * V + 8 * t : b * V + 8 * t + 8, at])


def flat(ref):
    return jnp.concatenate([ref[q, a * V : a * V + V, :] for a in range(3) for q in range(NC)], axis=1)


NT = (((1,), (1,)), ((), ()))


def gram_to(m_ref, x_ref):
    total = jnp.zeros((2 * V, V), F32)
    for b in range(3):
        high = x_ref[b * V : b * V + V, :]
        both = jnp.concatenate([high, x_ref[(3 + b) * V : (4 + b) * V, :]], axis=0)
        total = total + lax.dot_general(both, high, NT, preferred_element_type=F32)
    low = total[V:, :]
    gram = total[:V, :] + low + low.T
    row = lax.broadcasted_iota(jnp.int32, (V, 64), 0)
    lane = lax.broadcasted_iota(jnp.int32, (V, 64), 1)
    eye = jnp.where(row == lane, 1.0, 0.0).astype(F32)
    m_ref[:V, :] = jnp.concatenate([eye, gram, jnp.zeros((V, LANES - 64 - V), F32)], axis=1)


def halves(value):
    high = value.astype(BF16)
    return high, (value - high.astype(F32)).astype(BF16)


def mix(linv, value):
    left, left_low = halves(linv)
    right, right_low = halves(value)
    return jnp.dot(
        jnp.concatenate([left, left, left_low], axis=1),
        jnp.concatenate([right, right_low, right], axis=0),
        preferred_element_type=F32,
    )


CHOL = 4


def factor_piece(m_ref, col_ref, j):
    sub = lax.broadcasted_iota(jnp.int32, (8, LANES), 0)
    tiles = range(j // 8, TILES)
    m = {t: m_ref[8 * t : 8 * t + 8, :] for t in tiles}
    cols = []
    for s in range(CHOL):
        index = jnp.full((8, LANES), 64 + s + j, jnp.int32)
        cols.append({t: lanes_of(m[t], index) for t in tiles})
        for t in tiles:
            col_ref[s, 8 * t : 8 * t + 8, :] = cols[s][t]
    for s in range(CHOL):
        row = wide(m_ref[j + s : j + s + 1, :])
        head = {n: wide(col_ref[n, j + s : j + s + 1, :]) for n in range(s, CHOL)}
        inverse = 1.0 / head[s]
        for t in tiles:
            if 8 * t + 7 <= j + s:
                continue
            factor = cols[s][t] * inverse
            if 8 * t <= j + s:
                factor = jnp.where(sub + 8 * t > j + s, factor, 0.0)
            m[t] = m[t] - factor * row
            m_ref[8 * t : 8 * t + 8, :] = m[t]
            for n in range(s + 1, CHOL):
                cols[n][t] = cols[n][t] - factor * head[n]
                col_ref[n, 8 * t : 8 * t + 8, :] = cols[n][t]


def inverse_of(m_ref):
    m = m_ref[:V, :]
    row = lax.broadcasted_iota(jnp.int32, (V, LANES), 0)
    lane = lax.broadcasted_iota(jnp.int32, (V, LANES), 1)
    diag = jnp.sum(jnp.where(lane == row + 64, m, 0.0), axis=1, keepdims=True)
    return m[:, :V] / jnp.sqrt(diag)


def solve_to(dst_ref, linv, src_ref):
    out = mix(linv, flat(src_ref))
    for a in range(3):
        for q in range(NC):
            at = (a * NC + q) * LANES
            dst_ref[q, a * V : a * V + V, :] = out[:, at : at + LANES]


def rows_of(src_ref, index, tiles, c):
    block = (lax.broadcasted_iota(jnp.int32, (8, LANES), 1) // OVD) ^ c
    out = []
    for at in tiles:
        pick = lanes_of(src_ref[NC - 1, at, :], index)
        for q in range(NC - 1):
            pick = jnp.where(block == q, lanes_of(src_ref[q, at, :], index), pick)
        out.append(pick)
    return out


def index_row(small_ref, row):
    total = small_ref[0, pl.ds(row, 1), :]
    for q in range(1, NC):
        total = total + small_ref[q, pl.ds(row, 1), :]
    return total


def main_kernel(
    c_ref, p0, p1, p2, p3, v0, v1, v2, v3,
    y2_ref, w_ref, linv_ref, s1_ref, s2_ref, row_ref,
    y_ref, z_ref, m_ref, col_ref, g_ref, x_ref, oh_ref, t_ref, cols_ref, pair_ref, scale_ref, sum_ref,
):
    c = c_ref[0]
    small_ref = Blocks((p0, p1, p2, p3))
    val_ref = Blocks((v0, v1, v2, v3))
    for m in range(NC):
        col = small_ref[m, COL0 : COL0 + NB, :]
        local = (col.astype(jnp.int32) ^ (c * LANES)).astype(F32)
        cols_ref[m, NB:32, :] = jnp.full((32 - NB, LANES), -1.0, F32)
        cols_ref[m, 0:NB, :] = jnp.where(col < 0.0, -1.0, local)
    m_ref[V:, :] = jnp.zeros((8, LANES), F32)

    def apply(src_ref, dst_ref, first):
        split_to(x_ref, src_ref)
        if first:
            one_hot(cols_ref, oh_ref, 0)
            one_hot(cols_ref, oh_ref, 1)
        else:
            gram_to(m_ref, x_ref)
        start_op(small_ref, src_ref, dst_ref)
        pack_pairs(src_ref, scale_ref, pair_ref)
        sum_ref[...] = jnp.zeros((NC, 3 * V, LANES), F32)
        issue(x_ref, oh_ref, t_ref, 0, 0)

        groups = [(rc, range(n, min(n + 4, NB))) for rc in range(NC) for n in range(ONE, NB, 4)]
        for k in range(ONE):
            if k + 1 < ONE:
                issue(x_ref, oh_ref, t_ref, k + 1, (k + 1) % 2)
            for rc, ks in groups[k * len(groups) // ONE : (k + 1) * len(groups) // ONE]:
                lane_blocks(val_ref, cols_ref, pair_ref, sum_ref, rc, ks)
            if first:
                if k + 2 < ONE:
                    one_hot(cols_ref, oh_ref, k + 2)
            elif k * CHOL < V:
                factor_piece(m_ref, col_ref, k * CHOL)
            take(val_ref, dst_ref, t_ref, k, k % 2)
        for q in range(NC):
            for a in range(3):
                at = slice(a * V, a * V + V)
                dst_ref[q, at, :] = dst_ref[q, at, :] + sum_ref[q, at, :] * scale_ref[...]

    apply(small_ref, y_ref, True)
    apply(y_ref, z_ref, False)
    solve_to(y2_ref, inverse_of(m_ref), z_ref)
    apply(y2_ref, w_ref, False)
    linv = inverse_of(m_ref)
    linv_ref[...] = linv
    first = wide(index_row(small_ref, SEND0 + entry(SENT, c))).astype(jnp.int32)
    second = wide(index_row(small_ref, SEND0 + entry(SPLIT, c))).astype(jnp.int32)
    half = (c % 2) * (V // 2)
    for n, slot in enumerate((entry(GOT, c), entry(SPLIT, c))):
        row_ref[2 * n : 2 * n + 1, :] = index_row(small_ref, RECV0 + slot)
        row_ref[2 * n + 1 : 2 * n + 2, :] = index_row(small_ref, LIVE0 + slot)
    tiles = [slice(8 * t, 8 * t + 8) for t in range(3 * TILES)]
    for n, index in enumerate((first, second)):
        for at, piece in zip(tiles, rows_of(w_ref, index, tiles, c)):
            g_ref[n, at, :] = piece
    both = jnp.concatenate([g_ref[n, a * V : a * V + V, :] for n in range(2) for a in range(3)], axis=1)
    image = mix(linv, both)
    for a in range(3):
        s1_ref[a * V : a * V + V, :] = image[:, a * LANES : a * LANES + LANES]
        g_ref[1, a * V : a * V + V, :] = image[:, (3 + a) * LANES : (4 + a) * LANES]
        s2_ref[a * (V // 2) : (a + 1) * (V // 2), :] = g_ref[1, pl.ds(pl.multiple_of(a * V + half, 8), V // 2), :]


def middle_kernel(c_ref, row_ref, y2_ref, linv_ref, mine1_ref, mine2_ref, g_ref):
    c = c_ref[0]
    tiles = [slice(8 * t, 8 * t + 8) for t in range(3 * TILES)]
    for n in range(2):
        index = wide(row_ref[2 * n : 2 * n + 1, :]).astype(jnp.int32)
        live = wide(row_ref[2 * n + 1 : 2 * n + 2, :])
        for at, piece in zip(tiles, rows_of(y2_ref, index, tiles, c)):
            g_ref[n, at, :] = piece * live
    both = jnp.concatenate([g_ref[n, a * V : a * V + V, :] for n in range(2) for a in range(3)], axis=1)
    mine = mix(linv_ref[...], both)
    for n, out_ref in enumerate((mine1_ref, mine2_ref)):
        for a in range(3):
            at = (3 * n + a) * LANES
            out_ref[a * V : a * V + V, :] = mine[:, at : at + LANES]


def basis_kernel(after_ref, y2_ref, w_ref, linv_ref, basis_ref, center_ref, q_ref):
    linv = linv_ref[...]
    solve_to(q_ref, linv, y2_ref)
    basis_ref[...] = q_ref[0]
    image = mix(linv, flat(w_ref))
    center_ref[...] = lax.dot_general(flat(q_ref), image, NT, precision=HIGH, preferred_element_type=F32)


def coarse_kernel(c_ref, mine1_ref, mine2_ref, got1_ref, got2_ref, near_ref, far_ref, r_ref):
    c = c_ref[0]

    def side(ref, count):
        return jnp.concatenate([ref[a * count : a * count + count, :] for a in range(3)], axis=1)

    one = lax.dot_general(side(mine1_ref, V), side(got1_ref, V), NT, precision=HIGH, preferred_element_type=F32) * SCALE
    two = lax.dot_general(side(mine2_ref, V), side(got2_ref, V // 2), NT, precision=HIGH, preferred_element_type=F32) * SCALE
    part = V // NC
    for d in range(NC):
        r_ref[d, 0:part, 0:V] = one[d * part : d * part + part, :]
        r_ref[d, 16 : 16 + part, 0 : V // 2] = two[d * part : d * part + part, :]
    near_ref[0] = r_ref[c]
    near_ref[1] = r_ref[c ^ 1]
    far_ref[0] = r_ref[c ^ 2]
    far_ref[1] = r_ref[c ^ 3]


def pair_kernel(near_ref, far_ref, after_ref, out_ref):
    out_ref[0] = near_ref[1]
    out_ref[1] = far_ref[1]


def join_kernel(c_ref, center_ref, near_ref, far_ref, on_ref, out_ref, r_ref):
    c = c_ref[0]
    part = V // NC
    for m, value in enumerate((near_ref[0], on_ref[0], far_ref[0], on_ref[1])):
        r_ref[m] = value

    def put(place, value):
        for v in range(part):
            out_ref[place * part + v] = value[v : v + 1, :]

    for d in range(NC):
        slot = GOT[d]
        put(slot if slot < RADIUS else slot + 1, r_ref[c ^ d, 0:part, 0:V])
    for d in (0, 2):
        slot = SPLIT[d]
        sides = [r_ref[c ^ (d + h), 16 : 16 + part, 0 : V // 2] for h in range(2)]
        put(slot if slot < RADIUS else slot + 1, jnp.concatenate(sides, axis=1))
    for d in range(NC):

        @pl.when(c == d)
        def _():
            put(RADIUS, center_ref[d * part : d * part + part, :])


def shards(test_vectors, ell_values, ell_cols, ell_count, pivot, send_rows, recv_rows, ov_count):
    shape = pltpu.VMEM
    c = lax.axis_index("crow").astype(jnp.int32).reshape(1)
    x = jnp.transpose(test_vectors[0], (1, 0, 2)).reshape(3 * V, LANES)
    values = ell_values.reshape(9 * NB, 1, LANES)

    def pass_on(piece, m):
        return lax.ppermute(piece, "crow", [(n, n ^ m) for n in range(NC)])

    far_v = pass_on(values, 2)
    packed = pl.pallas_call(
        pack_kernel,
        out_shape=shape((PACKED, LANES), F32),
        in_specs=[smem(), smem()] + [vmem()] * 6,
        out_specs=vmem(),
    )(
        c,
        ov_count.reshape(SLOTS),
        x,
        ell_cols.reshape(NB, 1, LANES),
        ell_count.reshape(1, LANES),
        pivot.reshape(3, 1, LANES),
        send_rows.reshape(SLOTS, 1, OVD),
        recv_rows.reshape(SLOTS, 1, OVD),
    )
    far_p = pass_on(packed, 2)
    near_v = pass_on(values, 1)
    near_p = pass_on(packed, 1)
    far_v, near_p = lax.optimization_barrier((far_v, near_p))
    blocks = [packed, near_p, far_p, pass_on(far_p, 1), values, near_v, far_v, pass_on(far_v, 1)]
    block = (NC, 3 * V, LANES)
    y2, w, linv, s1, s2, row = pl.pallas_call(
        main_kernel,
        out_shape=(
            shape(block, F32),
            shape(block, F32),
            shape((V, V), F32),
            shape((3 * V, LANES), F32),
            shape((3 * V // 2, LANES), F32),
            shape((8, LANES), F32),
        ),
        in_specs=[smem()] + [vmem()] * 8,
        out_specs=(vmem(),) * 6,
        scratch_shapes=[
            pltpu.VMEM(block, F32),
            pltpu.VMEM(block, F32),
            pltpu.VMEM((V + 8, LANES), F32),
            pltpu.VMEM((CHOL, V + 8, LANES), F32),
            pltpu.VMEM((2, 3 * V, LANES), F32),
            pltpu.VMEM((6 * V, NC * LANES), BF16),
            pltpu.VMEM((2, ONE, NC * LANES, 2 * LANES), BF16),
            pltpu.VMEM((2, 2, 3 * V, 2 * LANES), F32),
            pltpu.VMEM((NC, 32, LANES), F32),
            pltpu.VMEM((NC, 3 * V // 2, LANES), jnp.int32),
            pltpu.VMEM((V, LANES), F32),
            pltpu.VMEM(block, F32),
        ],
        compiler_params=LIMIT,
    )(c, *map(near, blocks))

    size = lax.axis_size("sub")

    def across(piece, slots, turn):
        pairs = []
        for j in range(size):
            for n in range(NC):
                i = (j - OFFSETS[slots[n]]) % size
                pairs.append((j * NC + n, i * NC + (n ^ turn)))
        return lax.ppermute(piece, ("sub", "crow"), pairs)

    got1 = across(s1, SENT, 2)
    got2 = across(s2, SPLIT, 0)
    mine1, mine2 = pl.pallas_call(
        middle_kernel,
        out_shape=(shape((3 * V, LANES), F32), shape((3 * V, LANES), F32)),
        in_specs=[smem()] + [vmem()] * 3,
        out_specs=(vmem(),) * 2,
        scratch_shapes=[pltpu.VMEM((2, 3 * V, LANES), F32)],
        compiler_params=LIMIT,
    )(c, *map(near, (row, y2, linv)))
    pair = shape((2, 32, LANES), F32)
    mine, sent = pl.pallas_call(
        coarse_kernel,
        out_shape=(pair, pair),
        in_specs=[smem()] + [vmem()] * 4,
        out_specs=(vmem(),) * 2,
        scratch_shapes=[pltpu.VMEM((NC, 32, LANES), F32)],
        compiler_params=LIMIT,
    )(c, *map(near, (mine1, mine2, got1, got2)))
    far = pass_on(sent, 2)
    basis, center = pl.pallas_call(
        basis_kernel,
        out_shape=(jax.ShapeDtypeStruct((3 * V, LANES), F32), shape((V, V), F32)),
        in_specs=[vmem()] * 4,
        out_specs=(vmem(),) * 2,
        scratch_shapes=[pltpu.VMEM(block, F32)],
        compiler_params=LIMIT,
    )(*map(near, (mine, y2, w, linv)))
    both = pl.pallas_call(
        pair_kernel, out_shape=pair, in_specs=[vmem()] * 3, out_specs=vmem(), compiler_params=LIMIT
    )(near(mine), near(far), near(center))
    on = pass_on(both, 1)
    coarse = pl.pallas_call(
        join_kernel,
        out_shape=jax.ShapeDtypeStruct(((2 * RADIUS + 1) * (V // NC), 1, V), F32),
        in_specs=[smem()] + [vmem()] * 4,
        out_specs=vmem(),
        scratch_shapes=[pltpu.VMEM((NC, 32, LANES), F32)],
        compiler_params=LIMIT,
    )(c, *map(near, (center, mine, far, on)))
    coarse = coarse.reshape(2 * RADIUS + 1, V // NC, V)
    basis = jnp.transpose(basis.reshape(3, V, LANES), (1, 0, 2))
    return basis[None], coarse[None]


def solution(mesh):
    placed = (
        P("sub", None, None, "crow"),
        P("sub", None, None, "crow"),
        P("sub", None, "crow"),
        P("sub", "crow"),
        P("sub", None, "crow"),
        P("sub", None, "crow"),
        P("sub", None, "crow"),
        P("sub", None, "crow"),
    )
    return jax.shard_map(
        shards,
        mesh=mesh,
        in_specs=placed,
        out_specs=(P("sub", None, None, "crow"), P("sub", None, "crow", None)),
        check_vma=False,
    )
```
